32 devices in a mesh: fsdp: 8 (over z, core), rows: 4 (over y, x).
Axes of the slice: x: 2, y: 2, z: 4, core: 2. Of those that a mesh axis runs over, the one named last changes fastest.
Arguments:
- query_rows: bfloat16 [8, 1024, 1536], P('fsdp', 'rows'), may hold values from -6 to 6
- key_rows: bfloat16 [8, 1024, 1536], P('fsdp', 'rows'), may hold values from -6 to 6
- value_rows: bfloat16 [8, 1024, 1536], P('fsdp', 'rows'), may hold values from -6 to 6
- grad_out: bfloat16 [8, 1024, 3072], P('fsdp', 'rows'), may hold values from -6 to 6
- w_out: bfloat16 [1536, 3072], P('fsdp'), may hold values from -0.15625 to 0.15625
Outputs:
- grad_query: bfloat16 [8, 1024, 1536], P('fsdp', 'rows')
- grad_key: bfloat16 [8, 1024, 1536], P('fsdp', 'rows')
- grad_value: bfloat16 [8, 1024, 1536], P('fsdp', 'rows')
- grad_w_out: float32 [1536, 3072], P('fsdp')
The draws below stay inside these ranges and needn't reach their ends.
All inputs are finite; a program needn't handle non-finite values.
Results may differ from the reference program's by a relative error of at most 0.02.
Values may be sent and summed in bfloat16 or wider, within the bound.
No kernel may reach another device: no remote copies, remote signals or barrier semaphores. Data moves between devices by JAX's collectives and lax.ppermute only.
A program may use at most 192 MiB of HBM per device.

```python
import math
import jax
import jax.numpy as jnp
from jax import lax

D = 3072
HDIM = 128
HEADS = 12
TOK_DEV = 256
HW = 1536
SEQ = 1024
IMAGES = 8
N_ROWS = 4


def drawn(key):
    base = jax.random.fold_in(key, 11)
    key_query, key_keys = jax.random.split(base, 2)
    shape = (IMAGES, SEQ, HW)
    query = jnp.clip(jax.random.normal(key_query, shape, jnp.float32), -6.0, 6.0)
    keys_out = jnp.clip(jax.random.normal(key_keys, shape, jnp.float32), -6.0, 6.0)
    return (query.astype(jnp.bfloat16), keys_out.astype(jnp.bfloat16))


def draw_query_rows(key, part):
    return drawn(key)[0]


def draw_key_rows(key, part):
    return drawn(key)[1]


def strengthened(result, key, source, target, parts, factor):
    owner, partner = [(jnp.arange(result.shape[dim]) // (result.shape[dim] // parts)).reshape([-1 if axis == dim else 1 for axis in range(result.ndim)]) for dim in (source, target)]
    chosen = jax.random.permutation(key, parts)[partner]
    strong = (owner == chosen) | (owner == (partner + parts // 2) % parts)
    return jnp.where(strong, factor * result, result)


def levels(stream_key, dims, pieces, least, largest):
    level, own = 1.0, jax.random.fold_in(stream_key, 6)
    for axis_at, blocks in pieces:
        steps = jnp.exp(jax.random.uniform(jax.random.fold_in(own, axis_at), (blocks,), jnp.float32, least / len(pieces), largest / len(pieces)))
        level = level * jnp.repeat(steps, dims[axis_at] // blocks).reshape([-1 if axis == axis_at else 1 for axis in range(len(dims))])
    return level


def bell_draw(stream_key, extent, width, most, shards=(), held_as=jnp.bfloat16):
    entries = jax.random.normal(stream_key, extent, jnp.float32) * width
    if len(shards) > 0:
        entries = levels(stream_key, extent, shards, -0.22, 0.18) * entries
    return jnp.clip(entries, min=-most, max=most).astype(held_as)


def noise_with(own_key, extent, deviation, most, cuts, heavy, held_as=jnp.bfloat16):
    array = deviation * jax.random.normal(own_key, extent, jnp.float32)
    if cuts:
        array = array * levels(own_key, extent, cuts, -0.22, 0.18)
    return jnp.clip(strengthened(array, jax.random.fold_in(own_key, 3), *heavy), -most, most).astype(held_as)


def setup_inputs(seed: int = 0) -> dict:
    key_of = jax.random.split(jax.random.key(seed), 6)
    return {
        "query_rows": draw_query_rows(jax.random.fold_in(key_of[5], 71), 0),
        "key_rows": draw_key_rows(jax.random.fold_in(key_of[5], 71), 0),
        "value_rows": noise_with(key_of[2], (IMAGES, SEQ, HW), 1.0, 6.0, ((0, 8), (1, 4)), (0, 2, 8, 2.0)),
        "grad_out": bell_draw(key_of[3], (IMAGES, SEQ, D), 1.0, 6.0, ((0, 8), (1, 4))),
        "w_out": bell_draw(key_of[4], (HW, D), HW ** -0.5, 0.15625, ((0, 8),)),
    }


def one_image(inputs, w_out):
    query, key_in, value, grad_img = inputs
    factor = 1.0 / math.sqrt(HDIM)
    query_f = query.astype(jnp.float32).reshape(N_ROWS, TOK_DEV, HEADS, HDIM)
    key_f = key_in.astype(jnp.float32).reshape(SEQ, HEADS, HDIM)
    value_f = value.astype(jnp.float32).reshape(SEQ, HEADS, HDIM)
    scores = jnp.einsum('rqhd,khd->rhqk', query_f, key_f) * factor
    probs = jax.nn.softmax(scores, axis=-1)
    probs_low = lax.optimization_barrier(probs.astype(jnp.bfloat16)).astype(jnp.float32)
    attended = jnp.einsum('rhqk,khd->rqhd', probs_low, value_f).astype(jnp.bfloat16).reshape(SEQ, HW)
    grad_attn = jnp.dot(grad_img, w_out.T, preferred_element_type=jnp.float32).astype(jnp.bfloat16)
    grad_heads = lax.optimization_barrier(grad_attn).astype(jnp.float32).reshape(N_ROWS, TOK_DEV, HEADS, HDIM)
    value_part = jnp.einsum('rhqk,rqhd->rkhd', probs_low, grad_heads)
    value_part = lax.optimization_barrier(value_part.astype(jnp.bfloat16)).astype(jnp.float32)
    grad_value = lax.optimization_barrier(jnp.sum(value_part, axis=0)).astype(jnp.bfloat16).reshape(SEQ, HW)
    grad_probs = jnp.einsum('rqhd,khd->rhqk', grad_heads, value_f)
    centre = lax.optimization_barrier(jnp.sum(probs * grad_probs, axis=-1, keepdims=True))
    grad_scores = lax.optimization_barrier((probs * (grad_probs - centre)).astype(jnp.bfloat16)).astype(jnp.float32)
    grad_query = (jnp.einsum('rhqk,khd->rqhd', grad_scores, key_f) * factor).astype(jnp.bfloat16).reshape(SEQ, HW)
    key_part = jnp.einsum('rhqk,rqhd->rkhd', grad_scores, query_f) * factor
    key_part = lax.optimization_barrier(key_part.astype(jnp.bfloat16)).astype(jnp.float32)
    grad_key = lax.optimization_barrier(jnp.sum(key_part, axis=0)).astype(jnp.bfloat16).reshape(SEQ, HW)
    attended_blocks = lax.optimization_barrier(attended).astype(jnp.float32).reshape(N_ROWS, TOK_DEV, HW)
    grad_blocks = grad_img.astype(jnp.float32).reshape(N_ROWS, TOK_DEV, D)
    block_terms = jnp.einsum('rti,rtd->rid', attended_blocks, grad_blocks)
    block_terms = lax.optimization_barrier(block_terms.astype(jnp.bfloat16)).astype(jnp.float32)
    grad_weight = lax.optimization_barrier(jnp.sum(block_terms, axis=0))
    return (grad_query, grad_key, grad_value, grad_weight)

def reference(query_rows, key_rows, value_rows, grad_out, w_out):
    grad_query, grad_key, grad_value, grad_weight = lax.map(lambda inputs: one_image(inputs, w_out), (query_rows, key_rows, value_rows, grad_out))
    return (grad_query, grad_key, grad_value, lax.optimization_barrier(jnp.sum(grad_weight, axis=0)))
```

```python
import functools
import math

import jax
import jax.numpy as jnp
from jax import lax
from jax.experimental import pallas as pl
from jax.experimental.pallas import tpu as pltpu
from jax.sharding import PartitionSpec as P

HDIM = 128


NT = (((1,), (1,)), ((), ()))
NN = (((1,), (0,)), ((), ()))


def dot(a, b, dims=NN):
    return lax.dot_general(a, b, dims, preferred_element_type=jnp.float32)


def whole(shape):
    return pl.BlockSpec(shape, lambda *_: (0,) * len(shape))


def cost(flops, moved, exps=0):
    return pl.CostEstimate(flops=flops, bytes_accessed=moved, transcendentals=exps)


def pack(place, query, key, value, rows):
    tokens, width = query.shape[1], query.shape[2] // rows

    def body(place_ref, q_ref, k_ref, v_ref, *out):
        for slot in range(rows):

            @pl.when(pl.program_id(0) == slot)
            def _():
                out[slot][0] = q_ref[0]
                out[slot][1] = k_ref[0]
                out[slot][2] = v_ref[0]

    part = pl.BlockSpec((1, tokens, width), lambda j, place_ref: (0, 0, place_ref[0] ^ j))
    shape = (3, tokens, width)
    return pl.pallas_call(
        body,
        grid_spec=pltpu.PrefetchScalarGridSpec(
            num_scalar_prefetch=1,
            grid=(rows,),
            in_specs=[part] * 3,
            out_specs=[whole(shape)] * rows,
        ),
        out_shape=[jax.ShapeDtypeStruct(shape, query.dtype)] * rows,
        cost_estimate=cost(0, 12 * query.size),
        name="pack",
    )(place, query, key, value)


def unpack(place, parts, rows):
    _, tokens, width = parts[0].shape

    def body(place_ref, *refs):
        ins, outs = refs[:rows], refs[rows:]
        for slot in range(rows):

            @pl.when(pl.program_id(0) == slot)
            def _():
                for at in range(3):
                    outs[at][0] = ins[slot][at]

    part = pl.BlockSpec((1, tokens, width), lambda j, place_ref: (0, 0, place_ref[0] ^ j))
    full = jax.ShapeDtypeStruct((1, tokens, width * rows), parts[0].dtype)
    return pl.pallas_call(
        body,
        grid_spec=pltpu.PrefetchScalarGridSpec(
            num_scalar_prefetch=1,
            grid=(rows,),
            in_specs=[whole(parts[0].shape)] * rows,
            out_specs=[part] * 3,
        ),
        out_shape=[full] * 3,
        cost_estimate=cost(0, 4 * rows * parts[0].size),
        name="unpack",
    )(place, *parts)


def forward(parts):
    rows = len(parts)
    _, tokens, width = parts[0].shape
    length, heads = rows * tokens, width // HDIM
    scale = math.log2(math.e) / math.sqrt(HDIM)

    def body(*refs):
        ins, (probs_ref, attended_ref) = refs[:rows], refs[rows:]
        keys = jnp.concatenate([ref[1] for ref in ins], axis=0)
        values = jnp.concatenate([ref[2] for ref in ins], axis=0).T
        for slot in range(rows):
            across = slice(slot * tokens, (slot + 1) * tokens)
            scores = dot(keys, ins[slot][0], NT)
            top = jnp.max(scores, axis=0, keepdims=True)
            powers = jnp.exp2((scores - top) * scale)
            total = jnp.sum(powers, axis=0, keepdims=True)
            probs = (powers * (1.0 / total)).astype(jnp.bfloat16)
            probs_ref[0, :, across] = probs
            attended_ref[:, across] = dot(values, probs).astype(jnp.bfloat16)

    part = pl.BlockSpec((3, tokens, HDIM), lambda h: (0, 0, h))
    return pl.pallas_call(
        body,
        grid=(heads,),
        in_specs=[part] * rows,
        out_specs=[
            pl.BlockSpec((1, length, length), lambda h: (h, 0, 0)),
            pl.BlockSpec((HDIM, length), lambda h: (h, 0)),
        ],
        out_shape=[
            jax.ShapeDtypeStruct((heads, length, length), jnp.bfloat16),
            jax.ShapeDtypeStruct((width, length), jnp.bfloat16),
        ],
        cost_estimate=cost(
            8 * heads * length * length * HDIM, 2 * heads * length * length, heads * length * length
        ),
        name="forward",
    )(*parts)


def backward(parts, probs, grad_attn):
    rows = len(parts)
    _, tokens, width = parts[0].shape
    length, heads = rows * tokens, width // HDIM
    factor = 1.0 / math.sqrt(HDIM)

    def body(*refs):
        ins, (probs_ref, grad_ref), outs = refs[:rows], refs[rows : rows + 2], refs[rows + 2 :]
        keys = jnp.concatenate([ref[1] for ref in ins], axis=0).T
        values = jnp.concatenate([ref[2] for ref in ins], axis=0)
        grad_key = jnp.zeros((length, HDIM), jnp.float32)
        grad_value = jnp.zeros((length, HDIM), jnp.float32)
        for slot in range(rows):
            across = slice(slot * tokens, (slot + 1) * tokens)
            grad = grad_ref[:, across]
            low = probs_ref[0, :, across]
            high = low.astype(jnp.float32)
            grad_probs = dot(values, grad)
            centre = jnp.sum(high * grad_probs, axis=0, keepdims=True)
            grad_scores = (high * (grad_probs - centre)).astype(jnp.bfloat16)
            outs[slot][0] = (dot(keys, grad_scores) * factor).T.astype(jnp.bfloat16)
            grad_key += dot(grad_scores, ins[slot][0])
            grad_value += dot(low, grad, NT)
        grad_key *= factor
        for slot in range(rows):
            down = slice(slot * tokens, (slot + 1) * tokens)
            outs[slot][1] = grad_key[down].astype(jnp.bfloat16)
            outs[slot][2] = grad_value[down].astype(jnp.bfloat16)

    part = pl.BlockSpec((3, tokens, HDIM), lambda h: (0, 0, h))
    return pl.pallas_call(
        body,
        grid=(heads,),
        in_specs=[part] * rows
        + [
            pl.BlockSpec((1, length, length), lambda h: (h, 0, 0)),
            pl.BlockSpec((HDIM, length), lambda h: (h, 0)),
        ],
        out_specs=[part] * rows,
        out_shape=[jax.ShapeDtypeStruct((3, tokens, width), jnp.bfloat16)] * rows,
        cost_estimate=cost(8 * heads * length * length * HDIM, 2 * heads * length * length),
        name="backward",
    )(*parts, probs, grad_attn)


def project(weights, grads):
    chunks, rows = len(grads), len(grads[0])
    half, depth = weights[0].shape
    tokens, wide = grads[0][0].shape
    steps = 2
    step = wide // steps

    def body(*refs):
        first, second = refs[:2]
        ins, out, total = refs[2:-2], refs[-2], refs[-1]
        at = pl.program_id(0)

        @pl.when(at == 0)
        def _():
            total[...] = jnp.zeros_like(total)

        for chunk in range(chunks):

            @pl.when(at // steps == chunk)
            def _():
                for slot in range(rows):
                    across = slice(slot * tokens, (slot + 1) * tokens)
                    block = ins[chunk * rows + slot][...]
                    total[:half, across] += dot(first[...], block, NT)
                    total[half:, across] += dot(second[...], block, NT)

        @pl.when(at == chunks * steps - 1)
        def _():
            out[...] = total[...].astype(out.dtype)

    def block_of(chunk):
        return pl.BlockSpec(
            (tokens, step), lambda i: (0, jnp.clip(i - chunk * steps, 0, steps - 1))
        )

    shape = (2 * half, rows * tokens)
    return pl.pallas_call(
        body,
        grid=(chunks * steps,),
        in_specs=[pl.BlockSpec((half, step), lambda i: (0, i))] * 2
        + [block_of(chunk) for chunk in range(chunks) for _ in range(rows)],
        out_specs=whole(shape),
        out_shape=jax.ShapeDtypeStruct(shape, jnp.bfloat16),
        scratch_shapes=[pltpu.VMEM(shape, jnp.float32)],
        cost_estimate=cost(2 * shape[0] * shape[1] * depth, 2 * depth * (shape[0] + shape[1])),
        name="project",
    )(*weights, *(block for chunk in grads for block in chunk))


def weight_terms(place, attended, grads, planes):
    rows = len(grads)
    width, length = attended.shape
    tokens, wide = grads[0].shape
    piece = width // 2 // planes
    step = wide // 2

    def body(place_ref, attended_ref, *refs):
        ins, (keep, give) = refs[:rows], refs[rows:]
        columns = jnp.concatenate([ref[...] for ref in ins], axis=0)
        plane, core = place_ref[1], place_ref[2]
        for out, side in ((keep, core), (give, 1 - core)):
            for ahead in range(planes):
                start = side * (width // 2) + ((plane + ahead) & (planes - 1)) * piece
                lines = attended_ref[pl.ds(pl.multiple_of(start, 16), piece), :]
                out[ahead] = dot(lines, columns).astype(out.dtype)

    shape = jax.ShapeDtypeStruct((planes, piece, wide), jnp.bfloat16)
    spec = pl.BlockSpec((planes, piece, step), lambda i, place_ref: (0, 0, i))
    return pl.pallas_call(
        body,
        grid_spec=pltpu.PrefetchScalarGridSpec(
            num_scalar_prefetch=1,
            grid=(wide // step,),
            in_specs=[whole((width, length))]
            + [pl.BlockSpec((tokens, step), lambda i, place_ref: (0, i))] * rows,
            out_specs=[spec] * 2,
        ),
        out_shape=[shape] * 2,
        cost_estimate=cost(2 * width * length * wide, 2 * (width * length + length * wide)),
        name="weight_terms",
    )(place, attended, *grads)


def assemble(place, pieces, planes):
    chunks = len(pieces)
    piece, wide = pieces[0][0].shape

    def body(place_ref, *refs):
        ins, out = refs[:-1], refs[-1]
        for chunk in range(chunks):
            for back in range(planes):
                start = ((place_ref[1] + planes - back) & (planes - 1)) * piece
                out[pl.ds(pl.multiple_of(start, 16), piece), chunk * wide : (chunk + 1) * wide] = (
                    ins[chunk * planes + back][...].astype(out.dtype)
                )

    shape = (planes * piece, chunks * wide)
    return pl.pallas_call(
        body,
        grid_spec=pltpu.PrefetchScalarGridSpec(
            num_scalar_prefetch=1,
            grid=(1,),
            in_specs=[whole((piece, wide))] * (chunks * planes),
            out_specs=whole(shape),
        ),
        out_shape=jax.ShapeDtypeStruct(shape, jnp.float32),
        cost_estimate=cost(0, 6 * shape[0] * shape[1]),
        name="assemble",
    )(place, *(block for chunk in pieces for block in chunk))


def by_heads(fsdp, rows, query_rows, key_rows, value_rows, grad_out, w_out):
    planes = fsdp // 2
    row = lax.axis_index("rows")
    member = lax.axis_index("fsdp")
    plane, core = member // 2, member % 2
    place = jnp.stack([row, plane, core]).astype(jnp.int32)

    def send(array, target):
        pairs = []
        for z in range(planes):
            for c in range(2):
                for r in range(rows):
                    to = target(z, c, r)
                    if to is not None:
                        pairs.append(((z * 2 + c) * rows + r, (to[0] * 2 + to[1]) * rows + to[2]))
        return lax.ppermute(array, ("fsdp", "rows"), pairs)

    def to_row(array, slot):
        return send(array, lambda z, c, r: (z, c, r ^ slot))

    def to_core(array):
        return send(array, lambda z, c, r: (z, 1 - c, r))

    def to_plane(array, ahead):
        return send(array, lambda z, c, r: ((z + ahead) % planes, c, r))

    packed = pack(place, query_rows, key_rows, value_rows, rows)
    parts = [packed[0]] + [to_row(packed[slot], slot) for slot in range(1, rows)]

    grad_flat = grad_out[0]
    wide = grad_flat.shape[1] // 2
    own = [grad_flat[:, :wide], grad_flat[:, wide:]]
    by_x = [to_row(block, 1) for block in own]
    by_y = [to_row(block, 2) for block in own]
    across = [to_row(by_x[0], 2), to_row(by_y[1], 1)]
    grads = [[own[at], by_x[at], by_y[at], across[at]] for at in range(2)]

    here = w_out
    for ahead in range(1, planes):
        got = send(w_out, lambda z, c, r: ((z + ahead) % planes, c, r) if z == r else None)
        here = jnp.where((plane - row) % planes == ahead, got, here)
    other = to_core(here)
    weights = [jnp.where(core == 0, here, other), jnp.where(core == 0, other, here)]

    probs, attended = forward(parts)
    grad_attn = project(weights, grads)
    sent = backward(parts, probs, grad_attn)
    back = [sent[0]] + [to_row(sent[slot], slot) for slot in range(1, rows)]
    grad_query, grad_key, grad_value = unpack(place, back, rows)

    pieces = []
    for chunk in grads:
        keep, give = weight_terms(place, attended, chunk, planes)
        both = keep.astype(jnp.float32) + to_core(give).astype(jnp.float32)
        total = both[0]
        for ahead in range(1, planes):
            total = total + to_plane(both[ahead].astype(jnp.bfloat16), ahead).astype(jnp.float32)
        total = total.astype(jnp.bfloat16)
        blocks = jnp.stack([total] + [to_row(total, slot) for slot in range(1, rows)])
        pieces.append(
            [
                to_plane(
                    lax.dynamic_index_in_dim(blocks, ((plane + ahead) % planes) ^ row, 0, False),
                    ahead,
                )
                if ahead
                else lax.dynamic_index_in_dim(blocks, plane ^ row, 0, False)
                for ahead in range(planes)
            ]
        )
    grad_w_out = assemble(place, pieces, planes)
    return grad_query, grad_key, grad_value, grad_w_out


def by_tokens(query_rows, key_rows, value_rows, grad_out, w_out):
    tokens, width = query_rows.shape[1:]
    heads = width // HDIM
    factor = 1.0 / math.sqrt(HDIM)
    grad_flat = grad_out[0]
    groups = math.gcd(heads, 3)

    def split(array, count):
        return jnp.moveaxis(array.reshape(count, groups, heads // groups, HDIM), 1, 0)

    def join(array, count):
        return jnp.moveaxis(array, 0, 1).reshape(count, width)

    grad_attn = lax.dot_general(
        grad_flat,
        lax.all_gather(w_out, "fsdp", axis=0, tiled=True),
        NT,
        preferred_element_type=jnp.float32,
    ).astype(jnp.bfloat16)
    all_keys = lax.all_gather(key_rows, "rows", axis=1, tiled=True)
    all_values = lax.all_gather(value_rows, "rows", axis=1, tiled=True)
    length = all_keys.shape[1]

    def product(spec, a, b):
        return jnp.einsum(spec, a, b, preferred_element_type=jnp.float32)

    def attend(inputs):
        queries, keys, values, grads = inputs
        probs = jax.nn.softmax(product("qhd,khd->hqk", queries, keys) * factor, axis=-1)
        low = probs.astype(jnp.bfloat16)
        attended = product("hqk,khd->qhd", low, values)
        value_part = product("hqk,qhd->khd", low, grads)
        grad_probs = product("qhd,khd->hqk", grads, values)
        centre = jnp.sum(probs * grad_probs, axis=-1, keepdims=True)
        grad_scores = (probs * (grad_probs - centre)).astype(jnp.bfloat16)
        grad_query = product("hqk,khd->qhd", grad_scores, keys) * factor
        key_part = product("hqk,qhd->khd", grad_scores, queries) * factor
        return (
            attended.astype(jnp.bfloat16),
            grad_query.astype(jnp.bfloat16),
            key_part.astype(jnp.bfloat16),
            value_part.astype(jnp.bfloat16),
        )

    attended, grad_query, key_part, value_part = lax.map(
        attend,
        (
            split(query_rows[0], tokens),
            split(all_keys[0], length),
            split(all_values[0], length),
            split(grad_attn, tokens),
        ),
    )

    def scatter(part):
        part = join(part, length).reshape(1, length, width)
        return lax.psum_scatter(part, "rows", scatter_dimension=1, tiled=True)

    term = lax.dot_general(
        join(attended, tokens),
        grad_flat,
        (((0,), (0,)), ((), ())),
        preferred_element_type=jnp.float32,
    ).astype(jnp.bfloat16)
    share = lax.psum_scatter(term, "fsdp", scatter_dimension=0, tiled=True)
    grad_w_out = lax.psum(share, "rows").astype(jnp.float32)
    return (
        join(grad_query, tokens).reshape(1, tokens, width),
        scatter(key_part),
        scatter(value_part),
        grad_w_out,
    )


def solution(mesh):
    fsdp, rows = mesh.shape["fsdp"], mesh.shape["rows"]

    def local(query_rows, key_rows, value_rows, grad_out, w_out):
        heads = query_rows.shape[2] // HDIM
        if rows == 4 and fsdp == 2 * rows and heads % rows == 0:
            plan = functools.partial(by_heads, fsdp, rows)
        else:
            plan = by_tokens
        return plan(query_rows, key_rows, value_rows, grad_out, w_out)

    tokens = P("fsdp", "rows", None)
    return jax.shard_map(
        local,
        mesh=mesh,
        in_specs=(tokens, tokens, tokens, tokens, P("fsdp", None)),
        out_specs=(tokens, tokens, tokens, P("fsdp", None)),
        check_vma=False,
    )
```

```python
import functools
import math

import jax
import jax.numpy as jnp
from jax import lax
from jax.experimental import pallas as pl
from jax.experimental.pallas import tpu as pltpu
from jax.sharding import PartitionSpec as P


HDIM = 128


NT = (((1,), (1,)), ((), ()))
NN = (((1,), (0,)), ((), ()))


def dot(a, b, dims=NN):
    return lax.dot_general(a, b, dims, preferred_element_type=jnp.float32)


def whole(shape):
    return pl.BlockSpec(shape, lambda *_: (0,) * len(shape))


def cost(flops, moved, exps=0):
    return pl.CostEstimate(flops=flops, bytes_accessed=moved, transcendentals=exps)


def pack(place, query, key, value, rows):
    tokens, width = query.shape[1], query.shape[2] // rows

    def body(place_ref, q_ref, k_ref, v_ref, *out):
        for slot in range(rows):

            @pl.when(pl.program_id(0) == slot)
            def _():
                out[slot][0] = q_ref[0]
                out[slot][1] = k_ref[0]
                out[slot][2] = v_ref[0]

    part = pl.BlockSpec((1, tokens, width), lambda j, place_ref: (0, 0, place_ref[0] ^ j))
    shape = (3, tokens, width)
    return pl.pallas_call(
        body,
        grid_spec=pltpu.PrefetchScalarGridSpec(
            num_scalar_prefetch=1,
            grid=(rows,),
            in_specs=[part] * 3,
            out_specs=[whole(shape)] * rows,
        ),
        out_shape=[jax.ShapeDtypeStruct(shape, query.dtype)] * rows,
        cost_estimate=cost(0, 12 * query.size),
        name="pack",
    )(place, query, key, value)


def unpack(place, parts):
    heads, rows = len(parts), len(parts[0])
    _, tokens, width = parts[0][0].shape

    def body(place_ref, *refs):
        ins, outs = refs[:-3], refs[-3:]
        for slot in range(rows):

            @pl.when(pl.program_id(0) == slot)
            def _():
                for head in range(heads):
                    for at in range(3):
                        outs[at][0, :, head * width : (head + 1) * width] = ins[
                            head * rows + slot
                        ][at]

    part = pl.BlockSpec(
        (1, tokens, width * heads), lambda j, place_ref: (0, 0, place_ref[0] ^ j)
    )
    full = jax.ShapeDtypeStruct((1, tokens, width * heads * rows), parts[0][0].dtype)
    return pl.pallas_call(
        body,
        grid_spec=pltpu.PrefetchScalarGridSpec(
            num_scalar_prefetch=1,
            grid=(rows,),
            in_specs=[whole(parts[0][0].shape)] * (rows * heads),
            out_specs=[part] * 3,
        ),
        out_shape=[full] * 3,
        cost_estimate=cost(0, 12 * tokens * width * heads * rows),
        name="unpack",
    )(place, *(block for head in parts for block in head))


def forward(parts):
    rows = len(parts)
    _, tokens, width = parts[0].shape
    length, heads = rows * tokens, width // HDIM
    scale = math.log2(math.e) / math.sqrt(HDIM)

    def body(*refs):
        ins, (probs_ref, attended_ref) = refs[:rows], refs[rows:]
        keys = jnp.concatenate([ref[1] for ref in ins], axis=0)
        values = jnp.concatenate([ref[2] for ref in ins], axis=0).T
        for slot in range(rows):
            across = slice(slot * tokens, (slot + 1) * tokens)
            scores = dot(keys, ins[slot][0], NT)
            top = jnp.max(scores, axis=0, keepdims=True)
            powers = jnp.exp2((scores - top) * scale)
            total = jnp.sum(powers, axis=0, keepdims=True)
            probs = (powers * (1.0 / total)).astype(jnp.bfloat16)
            probs_ref[0, :, across] = probs
            attended_ref[:, across] = dot(values, probs).astype(jnp.bfloat16)

    part = pl.BlockSpec((3, tokens, HDIM), lambda h: (0, 0, h))
    return pl.pallas_call(
        body,
        grid=(heads,),
        in_specs=[part] * rows,
        out_specs=[
            pl.BlockSpec((1, length, length), lambda h: (h, 0, 0)),
            pl.BlockSpec((HDIM, length), lambda h: (h, 0)),
        ],
        out_shape=[
            jax.ShapeDtypeStruct((heads, length, length), jnp.bfloat16),
            jax.ShapeDtypeStruct((width, length), jnp.bfloat16),
        ],
        cost_estimate=cost(
            8 * heads * length * length * HDIM, 2 * heads * length * length, heads * length * length
        ),
        name="forward",
    )(*parts)


def backward(parts, probs, grad_attn, head):
    rows = len(parts)
    tokens = parts[0].shape[1]
    length = rows * tokens
    factor = 1.0 / math.sqrt(HDIM)

    def body(*refs):
        ins, (probs_ref, grad_ref), outs = refs[:rows], refs[rows : rows + 2], refs[rows + 2 :]
        keys = jnp.concatenate([ref[1] for ref in ins], axis=0).T
        values = jnp.concatenate([ref[2] for ref in ins], axis=0)
        grad_key = jnp.zeros((length, HDIM), jnp.float32)
        grad_value = jnp.zeros((length, HDIM), jnp.float32)
        for slot in range(rows):
            across = slice(slot * tokens, (slot + 1) * tokens)
            grad = grad_ref[:, across]
            low = probs_ref[0, :, across]
            high = low.astype(jnp.float32)
            grad_probs = dot(values, grad)
            centre = jnp.sum(high * grad_probs, axis=0, keepdims=True)
            grad_scores = (high * (grad_probs - centre)).astype(jnp.bfloat16)
            outs[slot][0] = (dot(keys, grad_scores) * factor).T.astype(jnp.bfloat16)
            grad_key += dot(grad_scores, ins[slot][0])
            grad_value += dot(low, grad, NT)
        grad_key *= factor
        for slot in range(rows):
            down = slice(slot * tokens, (slot + 1) * tokens)
            outs[slot][1] = grad_key[down].astype(jnp.bfloat16)
            outs[slot][2] = grad_value[down].astype(jnp.bfloat16)

    part = pl.BlockSpec((3, tokens, HDIM), lambda i: (0, 0, head))
    shape = (3, tokens, HDIM)
    return pl.pallas_call(
        body,
        grid=(1,),
        in_specs=[part] * rows
        + [
            pl.BlockSpec((1, length, length), lambda i: (head, 0, 0)),
            pl.BlockSpec((HDIM, length), lambda i: (head, 0)),
        ],
        out_specs=[whole(shape)] * rows,
        out_shape=[jax.ShapeDtypeStruct(shape, jnp.bfloat16)] * rows,
        cost_estimate=cost(8 * length * length * HDIM, 2 * length * length),
        name="backward",
    )(*parts, probs, grad_attn)


def project(weights, grads):
    chunks, rows = len(grads), len(grads[0])
    half, depth = weights[0].shape
    tokens, wide = grads[0][0].shape
    steps = 2
    step = wide // steps

    def body(*refs):
        first, second = refs[:2]
        ins, out, total = refs[2:-2], refs[-2], refs[-1]
        at = pl.program_id(0)
        lines = jnp.concatenate([first[...], second[...]], axis=0)
        for chunk in range(chunks):

            @pl.when(at // steps == chunk)
            def _():
                columns = jnp.concatenate(
                    [ins[chunk * rows + slot][...] for slot in range(rows)], axis=0
                )
                term = dot(lines, columns, NT)
                if chunk:
                    total[...] += term
                else:
                    total[...] = jnp.where(at == 0, 0.0, total[...]) + term

        @pl.when(at == chunks * steps - 1)
        def _():
            out[...] = total[...].astype(out.dtype)

    def block_of(chunk):
        return pl.BlockSpec(
            (tokens, step), lambda i: (0, jnp.clip(i - chunk * steps, 0, steps - 1))
        )

    shape = (2 * half, rows * tokens)
    return pl.pallas_call(
        body,
        grid=(chunks * steps,),
        in_specs=[pl.BlockSpec((half, step), lambda i: (0, i))] * 2
        + [block_of(chunk) for chunk in range(chunks) for _ in range(rows)],
        out_specs=whole(shape),
        out_shape=jax.ShapeDtypeStruct(shape, jnp.bfloat16),
        scratch_shapes=[pltpu.VMEM(shape, jnp.float32)],
        cost_estimate=cost(2 * shape[0] * shape[1] * depth, 2 * depth * (shape[0] + shape[1])),
        name="project",
    )(*weights, *(block for chunk in grads for block in chunk))


def weight_terms(place, attended, grads, planes):
    rows = len(grads)
    width, length = attended.shape
    tokens, wide = grads[0].shape
    piece = width // 2 // planes
    step = wide // 2

    def body(place_ref, attended_ref, *refs):
        ins, (keep, give) = refs[:rows], refs[rows:]
        columns = jnp.concatenate([ref[...] for ref in ins], axis=0)
        term = dot(attended_ref[...], columns).astype(jnp.bfloat16)
        plane, core = place_ref[1], place_ref[2]
        for side in range(2):
            for out, mine in ((keep, core == side), (give, core != side)):

                @pl.when(mine)
                def _():
                    for at in range(planes):
                        start = (side * planes + at) * piece
                        out[(at - plane) & (planes - 1)] = term[start : start + piece]

    shape = jax.ShapeDtypeStruct((planes, piece, wide), jnp.bfloat16)
    spec = pl.BlockSpec((planes, piece, step), lambda i, place_ref: (0, 0, i))
    return pl.pallas_call(
        body,
        grid_spec=pltpu.PrefetchScalarGridSpec(
            num_scalar_prefetch=1,
            grid=(wide // step,),
            in_specs=[whole((width, length))]
            + [pl.BlockSpec((tokens, step), lambda i, place_ref: (0, i))] * rows,
            out_specs=[spec] * 2,
        ),
        out_shape=[shape] * 2,
        cost_estimate=cost(2 * width * length * wide, 2 * (width * length + length * wide)),
        name="weight_terms",
    )(place, attended, *grads)


def assemble(place, pieces, planes):
    chunks = len(pieces)
    piece, wide = pieces[0][0].shape

    def body(place_ref, *refs):
        ins, out = refs[:-1], refs[-1]
        for chunk in range(chunks):
            for back in range(planes):
                start = ((place_ref[1] + planes - back) & (planes - 1)) * piece
                out[pl.ds(pl.multiple_of(start, 16), piece), chunk * wide : (chunk + 1) * wide] = (
                    ins[chunk * planes + back][...].astype(out.dtype)
                )

    shape = (planes * piece, chunks * wide)
    return pl.pallas_call(
        body,
        grid_spec=pltpu.PrefetchScalarGridSpec(
            num_scalar_prefetch=1,
            grid=(1,),
            in_specs=[whole((piece, wide))] * (chunks * planes),
            out_specs=whole(shape),
        ),
        out_shape=jax.ShapeDtypeStruct(shape, jnp.float32),
        cost_estimate=cost(0, 6 * shape[0] * shape[1]),
        name="assemble",
    )(place, *(block for chunk in pieces for block in chunk))


def after(value, *done):
    return lax.optimization_barrier((value, done))[0]


def onward(planes, hop, z, c, r):
    to = z + 1 if z > r else z - 1
    return (to, c, r) if abs(z - r) == hop and 0 <= to < planes else None


def by_heads(fsdp, rows, query_rows, key_rows, value_rows, grad_out, w_out):
    planes = fsdp // 2
    row = lax.axis_index("rows")
    member = lax.axis_index("fsdp")
    plane, core = member // 2, member % 2
    place = jnp.stack([row, plane, core]).astype(jnp.int32)

    def send(array, target):
        pairs = []
        for z in range(planes):
            for c in range(2):
                for r in range(rows):
                    to = target(z, c, r)
                    if to is not None:
                        pairs.append(((z * 2 + c) * rows + r, (to[0] * 2 + to[1]) * rows + to[2]))
        return lax.ppermute(array, ("fsdp", "rows"), pairs)

    def to_row(array, slot):
        return send(array, lambda z, c, r: (z, c, r ^ slot))

    def to_core(array):
        return send(array, lambda z, c, r: (z, 1 - c, r))

    def to_plane(array, ahead):
        return send(array, lambda z, c, r: ((z + ahead) % planes, c, r))

    grad_flat = grad_out[0]
    wide = grad_flat.shape[1] // 2
    own = [grad_flat[:, :wide], grad_flat[:, wide:]]
    by_x, by_y = [to_row(own[0], 1)], [to_row(own[0], 2)]

    packed = pack(place, query_rows, key_rows, value_rows, rows)
    parts = [packed[0]] + [to_row(packed[slot], slot) for slot in range(1, rows)]

    here = []
    away = jnp.abs(plane - row)
    cut = w_out.shape[0] // 2
    for half in (w_out[:cut], w_out[cut:]):
        half = after(half, packed[0])
        above = send(half, lambda z, c, r: (z + 1, c, r) if z == r and z + 1 < planes else None)
        below = send(half, lambda z, c, r: (z - 1, c, r) if z == r and z > 0 else None)
        got = half
        stage = jnp.where(plane > row, above, below)
        for hop in range(1, planes):
            got = jnp.where(away == hop, stage, got)
            if hop + 1 < planes:
                stage = send(stage, functools.partial(onward, planes, hop))
        here.append(got)
    here = jnp.concatenate(here, axis=0)
    other = to_core(here)
    weights = [jnp.where(core == 0, here, other), jnp.where(core == 0, other, here)]

    probs, attended = forward(parts)

    across = [to_row(by_x[0], 2)]
    second = after(own[1], by_x[0], by_y[0])
    by_x.append(to_row(second, 1))
    by_y.append(to_row(second, 2))
    across.append(to_row(by_y[1], 1))
    grads = [[own[at], by_x[at], by_y[at], across[at]] for at in range(2)]

    def reduce_cores(attended, chunk):
        keep, give = weight_terms(place, attended, chunk, planes)
        got = to_core(give)
        return [
            (keep[at].astype(jnp.float32) + got[at].astype(jnp.float32)).astype(jnp.bfloat16)
            for at in range(planes)
        ]

    def reduce_planes(both, *done):
        got = [to_plane(both[ahead], ahead) for ahead in range(1, planes)]
        got = after(got, *done)
        total = both[0].astype(jnp.float32)
        for part in got:
            total = total + part.astype(jnp.float32)
        return total.astype(jnp.bfloat16)

    def gather_rows(total):
        return [total] + [to_row(total, slot) for slot in range(1, rows)]

    def to_owners(blocks):
        stack = jnp.stack(blocks)
        pieces = []
        for ahead in range(planes):
            block = lax.dynamic_index_in_dim(stack, ((plane + ahead) % planes) ^ row, 0, False)
            pieces.append(to_plane(block, ahead) if ahead else block)
        return pieces

    first = reduce_planes(reduce_cores(attended, grads[0]))
    blocks = gather_rows(first)
    both = reduce_cores(after(attended, first), grads[1])
    grad_attn = project(after(weights, both[0]), grads)
    back = []
    for head in range(probs.shape[0]):
        sent = backward(parts, probs, grad_attn, head)
        back.append([sent[0]] + [to_row(sent[slot], slot) for slot in range(1, rows)])
    grad_query, grad_key, grad_value = unpack(place, back)
    last = gather_rows(reduce_planes(both, back[0][0]))
    pieces = [to_owners(blocks), to_owners(after(last, back[-1][0]))]
    grad_w_out = assemble(place, pieces, planes)
    return grad_query, grad_key, grad_value, grad_w_out


def by_tokens(query_rows, key_rows, value_rows, grad_out, w_out):
    tokens, width = query_rows.shape[1:]
    heads = width // HDIM
    factor = 1.0 / math.sqrt(HDIM)
    grad_flat = grad_out[0]
    groups = math.gcd(heads, 3)

    def split(array, count):
        return jnp.moveaxis(array.reshape(count, groups, heads // groups, HDIM), 1, 0)

    def join(array, count):
        return jnp.moveaxis(array, 0, 1).reshape(count, width)

    grad_attn = lax.dot_general(
        grad_flat,
        lax.all_gather(w_out, "fsdp", axis=0, tiled=True),
        NT,
        preferred_element_type=jnp.float32,
    ).astype(jnp.bfloat16)
    all_keys = lax.all_gather(key_rows, "rows", axis=1, tiled=True)
    all_values = lax.all_gather(value_rows, "rows", axis=1, tiled=True)
    length = all_keys.shape[1]

    def product(spec, a, b):
        return jnp.einsum(spec, a, b, preferred_element_type=jnp.float32)

    def attend(inputs):
        queries, keys, values, grads = inputs
        probs = jax.nn.softmax(product("qhd,khd->hqk", queries, keys) * factor, axis=-1)
        low = probs.astype(jnp.bfloat16)
        attended = product("hqk,khd->qhd", low, values)
        value_part = product("hqk,qhd->khd", low, grads)
        grad_probs = product("qhd,khd->hqk", grads, values)
        centre = jnp.sum(probs * grad_probs, axis=-1, keepdims=True)
        grad_scores = (probs * (grad_probs - centre)).astype(jnp.bfloat16)
        grad_query = product("hqk,khd->qhd", grad_scores, keys) * factor
        key_part = product("hqk,qhd->khd", grad_scores, queries) * factor
        return (
            attended.astype(jnp.bfloat16),
            grad_query.astype(jnp.bfloat16),
            key_part.astype(jnp.bfloat16),
            value_part.astype(jnp.bfloat16),
        )

    attended, grad_query, key_part, value_part = lax.map(
        attend,
        (
            split(query_rows[0], tokens),
            split(all_keys[0], length),
            split(all_values[0], length),
            split(grad_attn, tokens),
        ),
    )

    def scatter(part):
        part = join(part, length).reshape(1, length, width)
        return lax.psum_scatter(part, "rows", scatter_dimension=1, tiled=True)

    term = lax.dot_general(
        join(attended, tokens),
        grad_flat,
        (((0,), (0,)), ((), ())),
        preferred_element_type=jnp.float32,
    ).astype(jnp.bfloat16)
    share = lax.psum_scatter(term, "fsdp", scatter_dimension=0, tiled=True)
    grad_w_out = lax.psum(share, "rows").astype(jnp.float32)
    return (
        join(grad_query, tokens).reshape(1, tokens, width),
        scatter(key_part),
        scatter(value_part),
        grad_w_out,
    )


def solution(mesh):
    fsdp, rows = mesh.shape["fsdp"], mesh.shape["rows"]

    def local(query_rows, key_rows, value_rows, grad_out, w_out):
        heads = query_rows.shape[2] // HDIM
        if rows == 4 and fsdp == 2 * rows and heads % rows == 0:
            plan = functools.partial(by_heads, fsdp, rows)
        else:
            plan = by_tokens
        return plan(query_rows, key_rows, value_rows, grad_out, w_out)

    tokens = P("fsdp", "rows", None)
    return jax.shard_map(
        local,
        mesh=mesh,
        in_specs=(tokens, tokens, tokens, tokens, P("fsdp", None)),
        out_specs=(tokens, tokens, tokens, P("fsdp", None)),
        check_vma=False,
    )
```

```python
import functools
import math

import jax
import jax.numpy as jnp
from jax import lax
from jax.experimental import pallas as pl
from jax.experimental.pallas import tpu as pltpu
from jax.sharding import PartitionSpec as P


HDIM = 128


NT = (((1,), (1,)), ((), ()))
NN = (((1,), (0,)), ((), ()))


def dot(a, b, dims=NN):
    return lax.dot_general(a, b, dims, preferred_element_type=jnp.float32)


def whole(shape):
    return pl.BlockSpec(shape, lambda *_: (0,) * len(shape))


def cost(flops, moved, exps=0):
    return pl.CostEstimate(flops=flops, bytes_accessed=moved, transcendentals=exps)


def pack(place, query, key, value, rows):
    tokens, width = query.shape[1], query.shape[2] // rows

    def body(place_ref, q_ref, k_ref, v_ref, *out):
        for slot in range(rows):

            @pl.when(pl.program_id(0) == slot)
            def _():
                out[slot][0] = q_ref[0]
                out[slot][1] = k_ref[0]
                out[slot][2] = v_ref[0]

    part = pl.BlockSpec((1, tokens, width), lambda j, place_ref: (0, 0, place_ref[0] ^ j))
    shape = (3, tokens, width)
    return pl.pallas_call(
        body,
        grid_spec=pltpu.PrefetchScalarGridSpec(
            num_scalar_prefetch=1,
            grid=(rows,),
            in_specs=[part] * 3,
            out_specs=[whole(shape)] * rows,
        ),
        out_shape=[jax.ShapeDtypeStruct(shape, query.dtype)] * rows,
        cost_estimate=cost(0, 12 * query.size),
        name="pack",
    )(place, query, key, value)


def unpack(place, parts):
    calls, rows = len(parts), len(parts[0])
    tokens = parts[0][0].shape[1]
    widths = [part[0].shape[2] for part in parts]
    starts = [sum(widths[:at]) for at in range(calls + 1)]

    def body(place_ref, *refs):
        ins, outs = refs[:-3], refs[-3:]
        for slot in range(rows):

            @pl.when(pl.program_id(0) == slot)
            def _():
                for call in range(calls):
                    for at in range(3):
                        outs[at][0, :, starts[call] : starts[call + 1]] = ins[
                            call * rows + slot
                        ][at]

    part = pl.BlockSpec((1, tokens, starts[-1]), lambda j, place_ref: (0, 0, place_ref[0] ^ j))
    full = jax.ShapeDtypeStruct((1, tokens, starts[-1] * rows), parts[0][0].dtype)
    return pl.pallas_call(
        body,
        grid_spec=pltpu.PrefetchScalarGridSpec(
            num_scalar_prefetch=1,
            grid=(rows,),
            in_specs=[whole(block.shape) for part in parts for block in part],
            out_specs=[part] * 3,
        ),
        out_shape=[full] * 3,
        cost_estimate=cost(0, 12 * tokens * starts[-1] * rows),
        name="unpack",
    )(place, *(block for part in parts for block in part))


def forward(parts):
    rows = len(parts)
    _, tokens, width = parts[0].shape
    length, heads = rows * tokens, width // HDIM
    scale = math.log2(math.e) / math.sqrt(HDIM)

    def body(*refs):
        ins, (probs_ref, attended_ref) = refs[:rows], refs[rows:]
        keys = jnp.concatenate([ref[1] for ref in ins], axis=0)
        values = jnp.concatenate([ref[2] for ref in ins], axis=0).T
        for slot in range(rows):
            across = slice(slot * tokens, (slot + 1) * tokens)
            scores = dot(keys, ins[slot][0], NT)
            top = jnp.max(scores, axis=0, keepdims=True)
            powers = jnp.exp2((scores - top) * scale)
            total = jnp.sum(powers, axis=0, keepdims=True)
            probs = (powers * (1.0 / total)).astype(jnp.bfloat16)
            probs_ref[0, :, across] = probs
            attended_ref[:, across] = dot(values, probs).astype(jnp.bfloat16)

    part = pl.BlockSpec((3, tokens, HDIM), lambda h: (0, 0, h))
    return pl.pallas_call(
        body,
        grid=(heads,),
        in_specs=[part] * rows,
        out_specs=[
            pl.BlockSpec((1, length, length), lambda h: (h, 0, 0)),
            pl.BlockSpec((HDIM, length), lambda h: (h, 0)),
        ],
        out_shape=[
            jax.ShapeDtypeStruct((heads, length, length), jnp.bfloat16),
            jax.ShapeDtypeStruct((width, length), jnp.bfloat16),
        ],
        cost_estimate=cost(
            8 * heads * length * length * HDIM, 2 * heads * length * length, heads * length * length
        ),
        name="forward",
    )(*parts)


def backward(parts, probs, grad_attn, first, count):
    rows = len(parts)
    tokens = parts[0].shape[1]
    length = rows * tokens
    factor = 1.0 / math.sqrt(HDIM)

    def body(*refs):
        ins, (probs_ref, grad_ref), outs = refs[:rows], refs[rows : rows + 2], refs[rows + 2 :]
        keys = jnp.concatenate([ref[1] for ref in ins], axis=0).T
        values = jnp.concatenate([ref[2] for ref in ins], axis=0)
        grad_key = jnp.zeros((length, HDIM), jnp.float32)
        grad_value = jnp.zeros((length, HDIM), jnp.float32)
        for slot in range(rows):
            across = slice(slot * tokens, (slot + 1) * tokens)
            grad = grad_ref[:, across]
            low = probs_ref[0, :, across]
            high = low.astype(jnp.float32)
            grad_probs = dot(values, grad)
            centre = jnp.sum(high * grad_probs, axis=0, keepdims=True)
            grad_scores = (high * (grad_probs - centre)).astype(jnp.bfloat16)
            outs[slot][0] = (dot(keys, grad_scores) * factor).T.astype(jnp.bfloat16)
            grad_key += dot(grad_scores, ins[slot][0])
            grad_value += dot(low, grad, NT)
        grad_key *= factor
        for slot in range(rows):
            down = slice(slot * tokens, (slot + 1) * tokens)
            outs[slot][1] = grad_key[down].astype(jnp.bfloat16)
            outs[slot][2] = grad_value[down].astype(jnp.bfloat16)

    part = pl.BlockSpec((3, tokens, HDIM), lambda i: (0, 0, first + i))
    shape = (3, tokens, count * HDIM)
    return pl.pallas_call(
        body,
        grid=(count,),
        in_specs=[part] * rows
        + [
            pl.BlockSpec((1, length, length), lambda i: (first + i, 0, 0)),
            pl.BlockSpec((HDIM, length), lambda i: (first + i, 0)),
        ],
        out_specs=[pl.BlockSpec((3, tokens, HDIM), lambda i: (0, 0, i))] * rows,
        out_shape=[jax.ShapeDtypeStruct(shape, jnp.bfloat16)] * rows,
        cost_estimate=cost(8 * count * length * length * HDIM, 2 * count * length * length),
        name="backward",
    )(*parts, probs, grad_attn)


def project(place, weights, grads):
    chunks, rows = len(grads), len(grads[0])
    half, depth = weights[0].shape
    tokens, wide = grads[0][0].shape
    steps = 2
    step = wide // steps

    def body(place_ref, *refs):
        first, second = refs[:2]
        ins, out, total = refs[2:-2], refs[-2], refs[-1]
        at = pl.program_id(0)
        lines = jnp.concatenate([first[...], second[...]], axis=0)
        for chunk in range(chunks):

            @pl.when(at // steps == chunk)
            def _():
                columns = jnp.concatenate(
                    [ins[chunk * rows + slot][...] for slot in range(rows)], axis=0
                )
                term = dot(lines, columns, NT)
                if chunk:
                    total[...] += term
                else:
                    total[...] = jnp.where(at == 0, 0.0, total[...]) + term

        @pl.when(at == chunks * steps - 1)
        def _():
            for core in range(2):

                @pl.when(place_ref[2] == core)
                def _():
                    out[core * half : (core + 1) * half] = total[:half].astype(out.dtype)
                    out[(1 - core) * half : (2 - core) * half] = total[half:].astype(out.dtype)

    def block_of(chunk):
        return pl.BlockSpec(
            (tokens, step), lambda i, place_ref: (0, jnp.clip(i - chunk * steps, 0, steps - 1))
        )

    shape = (2 * half, rows * tokens)
    return pl.pallas_call(
        body,
        grid_spec=pltpu.PrefetchScalarGridSpec(
            num_scalar_prefetch=1,
            grid=(chunks * steps,),
            in_specs=[pl.BlockSpec((half, step), lambda i, place_ref: (0, i))] * 2
            + [block_of(chunk) for chunk in range(chunks) for _ in range(rows)],
            out_specs=whole(shape),
            scratch_shapes=[pltpu.VMEM(shape, jnp.float32)],
        ),
        out_shape=jax.ShapeDtypeStruct(shape, jnp.bfloat16),
        cost_estimate=cost(2 * shape[0] * shape[1] * depth, 2 * depth * (shape[0] + shape[1])),
        name="project",
    )(place, *weights, *(block for chunk in grads for block in chunk))


def weight_terms(place, attended, grads, planes):
    rows = len(grads)
    width, length = attended.shape
    tokens, wide = grads[0].shape
    piece = width // 2 // planes
    step = wide // 2

    def body(place_ref, attended_ref, *refs):
        ins, (keep, give) = refs[:rows], refs[rows:]
        columns = jnp.concatenate([ref[...] for ref in ins], axis=0)
        term = dot(attended_ref[...], columns).astype(jnp.bfloat16)
        plane, core = place_ref[1], place_ref[2]
        for side in range(2):
            for out, mine in ((keep, core == side), (give, core != side)):

                @pl.when(mine)
                def _():
                    for at in range(planes):
                        start = (side * planes + at) * piece
                        out[(at - plane) & (planes - 1)] = term[start : start + piece]

    shape = jax.ShapeDtypeStruct((planes, piece, wide), jnp.bfloat16)
    spec = pl.BlockSpec((planes, piece, step), lambda i, place_ref: (0, 0, i))
    return pl.pallas_call(
        body,
        grid_spec=pltpu.PrefetchScalarGridSpec(
            num_scalar_prefetch=1,
            grid=(wide // step,),
            in_specs=[whole((width, length))]
            + [pl.BlockSpec((tokens, step), lambda i, place_ref: (0, i))] * rows,
            out_specs=[spec] * 2,
        ),
        out_shape=[shape] * 2,
        cost_estimate=cost(2 * width * length * wide, 2 * (width * length + length * wide)),
        name="weight_terms",
    )(place, attended, *grads)


def assemble(place, pieces, planes):
    chunks = len(pieces)
    piece, wide = pieces[0][0].shape

    def body(place_ref, *refs):
        ins, out = refs[:-1], refs[-1]
        for chunk in range(chunks):
            for turn in range(planes):
                start = (((place_ref[1] ^ place_ref[0]) - turn) & (planes - 1)) * piece
                out[pl.ds(pl.multiple_of(start, 16), piece), chunk * wide : (chunk + 1) * wide] = (
                    ins[chunk * planes + turn][...].astype(out.dtype)
                )

    shape = (planes * piece, chunks * wide)
    return pl.pallas_call(
        body,
        grid_spec=pltpu.PrefetchScalarGridSpec(
            num_scalar_prefetch=1,
            grid=(1,),
            in_specs=[whole((piece, wide))] * (chunks * planes),
            out_specs=whole(shape),
        ),
        out_shape=jax.ShapeDtypeStruct(shape, jnp.float32),
        cost_estimate=cost(0, 6 * shape[0] * shape[1]),
        name="assemble",
    )(place, *(block for chunk in pieces for block in chunk))


def after(value, *done):
    return lax.optimization_barrier((value, done))[0]


def by_heads(fsdp, rows, query_rows, key_rows, value_rows, grad_out, w_out):
    planes = fsdp // 2
    row = lax.axis_index("rows")
    member = lax.axis_index("fsdp")
    plane, core = member // 2, member % 2
    place = jnp.stack([row, plane, core]).astype(jnp.int32)

    def send(array, target):
        pairs = []
        for z in range(planes):
            for c in range(2):
                for r in range(rows):
                    to = target(z, c, r)
                    if to is not None:
                        pairs.append(((z * 2 + c) * rows + r, (to[0] * 2 + to[1]) * rows + to[2]))
        return lax.ppermute(array, ("fsdp", "rows"), pairs)

    def to_row(array, slot):
        return send(array, lambda z, c, r: (z, c, r ^ slot))

    def to_core(array):
        return send(array, lambda z, c, r: (z, 1 - c, r))

    def to_plane(array, ahead):
        return send(array, lambda z, c, r: ((z + ahead) % planes, c, r))

    grad_flat = grad_out[0]
    wide = grad_flat.shape[1] // 2
    left, right = grad_flat[:, :wide], grad_flat[:, wide:]
    left_x, right_y = to_row(left, 1), to_row(right, 2)

    packed = pack(place, query_rows, key_rows, value_rows, rows)
    parts = [packed[0]] + [to_row(packed[slot], slot) for slot in range(1, rows)]

    here = w_out
    for ahead in range(1, planes):
        got = send(w_out, lambda z, c, r: ((z + ahead) % planes, c, r) if z == r else None)
        here = jnp.where((plane - row) % planes == ahead, got, here)
    weights = [here, to_core(here)]

    hand_y, hand_x = to_row(left_x, 2), to_row(right_y, 1)
    left, right = after((left, right), left_x, right_y)
    left_y, right_x = to_row(left, 2), to_row(right, 1)
    grads = [[left, left_x, left_y, hand_y], [right, right_x, right_y, hand_x]]

    probs, attended = forward(parts)

    def reduce_cores(attended, chunk):
        keep, give = weight_terms(place, attended, chunk, planes)
        got = to_core(give)
        return [
            (keep[at].astype(jnp.float32) + got[at].astype(jnp.float32)).astype(jnp.bfloat16)
            for at in range(planes)
        ]

    def reduce_planes(both, *done):
        got = [to_plane(both[ahead], ahead) for ahead in range(1, planes)]
        got = after(got, *done)
        total = both[0].astype(jnp.float32)
        for part in got:
            total = total + part.astype(jnp.float32)
        return total.astype(jnp.bfloat16)

    def deliver(total):
        return [
            send(total, lambda z, c, r: (r, c, r ^ ((z + turn) % planes)))
            for turn in range(planes)
        ]

    both = [reduce_cores(attended, grads[0])]
    both.append(reduce_cores(after(attended, both[0]), grads[1]))
    grad_attn = project(place, after(weights, both[1]), grads)
    heads = probs.shape[0]
    back, sent = [], []
    for first, count in ((0, 1), (1, heads - 1)):
        sent.append(backward(parts, probs, grad_attn, first, count))
        back.append([sent[-1][0]] + [to_row(sent[-1][slot], slot) for slot in range(1, rows)])
        if not first:
            early = reduce_planes(both[0], sent[0][0])
            probs = after(probs, early)
    late = reduce_planes(both[1], sent[1][0])
    pieces = [deliver(early), deliver(late)]
    grad_query, grad_key, grad_value = unpack(place, back)
    grad_w_out = assemble(place, pieces, planes)
    return grad_query, grad_key, grad_value, grad_w_out


def by_tokens(query_rows, key_rows, value_rows, grad_out, w_out):
    tokens, width = query_rows.shape[1:]
    heads = width // HDIM
    factor = 1.0 / math.sqrt(HDIM)
    grad_flat = grad_out[0]
    groups = math.gcd(heads, 3)

    def split(array, count):
        return jnp.moveaxis(array.reshape(count, groups, heads // groups, HDIM), 1, 0)

    def join(array, count):
        return jnp.moveaxis(array, 0, 1).reshape(count, width)

    grad_attn = lax.dot_general(
        grad_flat,
        lax.all_gather(w_out, "fsdp", axis=0, tiled=True),
        NT,
        preferred_element_type=jnp.float32,
    ).astype(jnp.bfloat16)
    all_keys = lax.all_gather(key_rows, "rows", axis=1, tiled=True)
    all_values = lax.all_gather(value_rows, "rows", axis=1, tiled=True)
    length = all_keys.shape[1]

    def product(spec, a, b):
        return jnp.einsum(spec, a, b, preferred_element_type=jnp.float32)

    def attend(inputs):
        queries, keys, values, grads = inputs
        probs = jax.nn.softmax(product("qhd,khd->hqk", queries, keys) * factor, axis=-1)
        low = probs.astype(jnp.bfloat16)
        attended = product("hqk,khd->qhd", low, values)
        value_part = product("hqk,qhd->khd", low, grads)
        grad_probs = product("qhd,khd->hqk", grads, values)
        centre = jnp.sum(probs * grad_probs, axis=-1, keepdims=True)
        grad_scores = (probs * (grad_probs - centre)).astype(jnp.bfloat16)
        grad_query = product("hqk,khd->qhd", grad_scores, keys) * factor
        key_part = product("hqk,qhd->khd", grad_scores, queries) * factor
        return (
            attended.astype(jnp.bfloat16),
            grad_query.astype(jnp.bfloat16),
            key_part.astype(jnp.bfloat16),
            value_part.astype(jnp.bfloat16),
        )

    attended, grad_query, key_part, value_part = lax.map(
        attend,
        (
            split(query_rows[0], tokens),
            split(all_keys[0], length),
            split(all_values[0], length),
            split(grad_attn, tokens),
        ),
    )

    def scatter(part):
        part = join(part, length).reshape(1, length, width)
        return lax.psum_scatter(part, "rows", scatter_dimension=1, tiled=True)

    term = lax.dot_general(
        join(attended, tokens),
        grad_flat,
        (((0,), (0,)), ((), ())),
        preferred_element_type=jnp.float32,
    ).astype(jnp.bfloat16)
    share = lax.psum_scatter(term, "fsdp", scatter_dimension=0, tiled=True)
    grad_w_out = lax.psum(share, "rows").astype(jnp.float32)
    return (
        join(grad_query, tokens).reshape(1, tokens, width),
        scatter(key_part),
        scatter(value_part),
        grad_w_out,
    )


def solution(mesh):
    fsdp, rows = mesh.shape["fsdp"], mesh.shape["rows"]

    def local(query_rows, key_rows, value_rows, grad_out, w_out):
        heads = query_rows.shape[2] // HDIM
        if rows == 4 and fsdp == 2 * rows and heads % rows == 0:
            plan = functools.partial(by_heads, fsdp, rows)
        else:
            plan = by_tokens
        return plan(query_rows, key_rows, value_rows, grad_out, w_out)

    tokens = P("fsdp", "rows", None)
    return jax.shard_map(
        local,
        mesh=mesh,
        in_specs=(tokens, tokens, tokens, tokens, P("fsdp", None)),
        out_specs=(tokens, tokens, tokens, P("fsdp", None)),
        check_vma=False,
    )
```

```python
import functools
import math

import jax
import jax.numpy as jnp
from jax import lax
from jax.experimental import pallas as pl
from jax.experimental.pallas import tpu as pltpu
from jax.sharding import PartitionSpec as P


HDIM = 128


NT = (((1,), (1,)), ((), ()))
NN = (((1,), (0,)), ((), ()))


def dot(a, b, dims=NN):
    return lax.dot_general(a, b, dims, preferred_element_type=jnp.float32)


def whole(shape):
    return pl.BlockSpec(shape, lambda *_: (0,) * len(shape))


def cost(flops, moved, exps=0):
    return pl.CostEstimate(flops=flops, bytes_accessed=moved, transcendentals=exps)


def pack(place, query, key, value, rows):
    tokens, width = query.shape[1], query.shape[2] // rows

    def body(place_ref, *refs):
        ins, outs, (held, sems) = refs[:3], refs[3:-2], refs[-2:]
        moves = []
        for slot in (*range(1, rows), 0):
            start = pl.multiple_of((place_ref[0] ^ slot) * width, HDIM)
            for at in range(3):
                box = held.at[slot, at]
                moves.append(
                    (
                        pltpu.make_async_copy(
                            ins[at].at[0, :, pl.ds(start, width)], box, sems.at[0, slot, at]
                        ),
                        pltpu.make_async_copy(box, outs[slot].at[at], sems.at[1, slot, at]),
                    )
                )
        run(moves)

    shape = (3, tokens, width)
    return pl.pallas_call(
        body,
        grid_spec=pltpu.PrefetchScalarGridSpec(
            num_scalar_prefetch=1,
            grid=(1,),
            in_specs=[pl.BlockSpec(memory_space=pl.ANY)] * 3,
            out_specs=[pl.BlockSpec(memory_space=pl.ANY)] * rows,
            scratch_shapes=[
                pltpu.VMEM((rows, *shape), query.dtype),
                pltpu.SemaphoreType.DMA((2, rows, 3)),
            ],
        ),
        out_shape=[jax.ShapeDtypeStruct(shape, query.dtype)] * rows,
        cost_estimate=cost(0, 12 * query.size),
        name="pack",
    )(place, query, key, value)


def run(moves):
    for fetch, _ in moves:
        fetch.start()
    for fetch, store in moves:
        fetch.wait()
        store.start()
    for _, store in moves:
        store.wait()


def unpack(place, parts):
    calls, rows = len(parts), len(parts[0])
    tokens = parts[0][0].shape[1]
    widths = [part[0].shape[2] for part in parts]
    starts = [sum(widths[:at]) for at in range(calls + 1)]
    width = starts[-1]

    def body(place_ref, *refs):
        ins, outs, held, sems = refs[: calls * rows], refs[calls * rows : -2], refs[-2], refs[-1]
        moves = []
        for call in range(calls):
            for slot in range(rows):
                start = (place_ref[0] ^ slot) * width + starts[call]
                start = pl.multiple_of(start, HDIM)
                for at in range(3):
                    box = held.at[slot, at, :, starts[call] : starts[call + 1]]
                    moves.append(
                        (
                            pltpu.make_async_copy(
                                ins[call * rows + slot].at[at], box, sems.at[0, call, slot, at]
                            ),
                            pltpu.make_async_copy(
                                box,
                                outs[at].at[0, :, pl.ds(start, widths[call])],
                                sems.at[1, call, slot, at],
                            ),
                        )
                    )
        run(moves)

    full = jax.ShapeDtypeStruct((1, tokens, width * rows), parts[0][0].dtype)
    return pl.pallas_call(
        body,
        grid_spec=pltpu.PrefetchScalarGridSpec(
            num_scalar_prefetch=1,
            grid=(1,),
            in_specs=[pl.BlockSpec(memory_space=pl.ANY)] * (calls * rows),
            out_specs=[pl.BlockSpec(memory_space=pl.ANY)] * 3,
            scratch_shapes=[
                pltpu.VMEM((rows, 3, tokens, width), parts[0][0].dtype),
                pltpu.SemaphoreType.DMA((2, calls, rows, 3)),
            ],
        ),
        out_shape=[full] * 3,
        cost_estimate=cost(0, 12 * tokens * width * rows),
        name="unpack",
    )(place, *(block for part in parts for block in part))


def forward(parts):
    rows = len(parts)
    _, tokens, width = parts[0].shape
    length, heads = rows * tokens, width // HDIM
    scale = math.log2(math.e) / math.sqrt(HDIM)

    def body(*refs):
        ins, (probs_ref, attended_ref) = refs[:rows], refs[rows:]
        keys = jnp.concatenate([ref[1] for ref in ins], axis=0)
        values = jnp.concatenate([ref[2] for ref in ins], axis=0).T
        for slot in range(rows):
            across = slice(slot * tokens, (slot + 1) * tokens)
            scores = dot(keys, ins[slot][0], NT)
            top = jnp.max(scores, axis=0, keepdims=True)
            powers = jnp.exp2((scores - top) * scale)
            total = jnp.sum(powers, axis=0, keepdims=True)
            probs = (powers * (1.0 / total)).astype(jnp.bfloat16)
            probs_ref[0, :, across] = probs
            attended_ref[:, across] = dot(values, probs).astype(jnp.bfloat16)

    part = pl.BlockSpec((3, tokens, HDIM), lambda h: (0, 0, h))
    return pl.pallas_call(
        body,
        grid=(heads,),
        in_specs=[part] * rows,
        out_specs=[
            pl.BlockSpec((1, length, length), lambda h: (h, 0, 0)),
            pl.BlockSpec((HDIM, length), lambda h: (h, 0)),
        ],
        out_shape=[
            jax.ShapeDtypeStruct((heads, length, length), jnp.bfloat16),
            jax.ShapeDtypeStruct((width, length), jnp.bfloat16),
        ],
        cost_estimate=cost(
            8 * heads * length * length * HDIM, 2 * heads * length * length, heads * length * length
        ),
        name="forward",
    )(*parts)


def backward(parts, probs, grad_attn, first, count):
    rows = len(parts)
    tokens = parts[0].shape[1]
    length = rows * tokens
    factor = 1.0 / math.sqrt(HDIM)

    def body(*refs):
        ins, (probs_ref, grad_ref) = refs[:rows], refs[rows : rows + 2]
        outs, scores_ref = refs[rows + 2 : -1], refs[-1]
        queries = jnp.concatenate([ref[0] for ref in ins], axis=0)
        keys = jnp.concatenate([ref[1] for ref in ins], axis=0).T
        values = jnp.concatenate([ref[2] for ref in ins], axis=0)
        for slot in range(rows):
            across = slice(slot * tokens, (slot + 1) * tokens)
            probs = probs_ref[0, :, across].astype(jnp.float32)
            terms = probs * dot(values, grad_ref[:, across])
            centre = jnp.sum(terms, axis=0, keepdims=True)
            scores_ref[:, across] = (terms - probs * centre).astype(jnp.bfloat16)
        scores = scores_ref[...]
        grad_query = (dot(keys, scores) * factor).T
        grad_key = dot(scores, queries) * factor
        grad_value = dot(probs_ref[0], grad_ref[...], NT)
        for slot in range(rows):
            down = slice(slot * tokens, (slot + 1) * tokens)
            outs[slot][0] = grad_query[down].astype(jnp.bfloat16)
            outs[slot][1] = grad_key[down].astype(jnp.bfloat16)
            outs[slot][2] = grad_value[down].astype(jnp.bfloat16)

    part = pl.BlockSpec((3, tokens, HDIM), lambda i: (0, 0, first + i))
    shape = (3, tokens, count * HDIM)
    return pl.pallas_call(
        body,
        grid=(count,),
        in_specs=[part] * rows
        + [
            pl.BlockSpec((1, length, length), lambda i: (first + i, 0, 0)),
            pl.BlockSpec((HDIM, length), lambda i: (first + i, 0)),
        ],
        out_specs=[pl.BlockSpec((3, tokens, HDIM), lambda i: (0, 0, i))] * rows,
        out_shape=[jax.ShapeDtypeStruct(shape, jnp.bfloat16)] * rows,
        scratch_shapes=[pltpu.VMEM((length, length), jnp.bfloat16)],
        cost_estimate=cost(8 * count * length * length * HDIM, 2 * count * length * length),
        name="backward",
    )(*parts, probs, grad_attn)


def columns_of(blocks, odd):
    return jnp.concatenate(
        [ref[...] for ref in blocks[:-2]] + [jnp.where(odd, blocks[-1][...], blocks[-2][...])], axis=0
    )


def project(place, weights, grads):
    chunks, count = len(grads), len(grads[0])
    half, depth = weights[0].shape
    tokens, step = grads[0][-1].shape

    def body(place_ref, *refs):
        first, second = refs[:2]
        ins, out, total = refs[2:-2], refs[-2], refs[-1]
        at = pl.program_id(0)
        lines = jnp.concatenate([first[...], second[...]], axis=0)
        for chunk in range(chunks):

            @pl.when(at // 2 == chunk)
            def _():
                columns = columns_of(ins[chunk * count : (chunk + 1) * count], at % 2 == 1)
                term = dot(lines, columns, NT)
                if chunk:
                    total[...] += term
                else:
                    total[...] = jnp.where(at == 0, 0.0, total[...]) + term

        @pl.when(at == chunks * 2 - 1)
        def _():
            for core in range(2):

                @pl.when(place_ref[2] == core)
                def _():
                    out[core * half : (core + 1) * half] = total[:half].astype(out.dtype)
                    out[(1 - core) * half : (2 - core) * half] = total[half:].astype(out.dtype)

    def block_of(chunk):
        return pl.BlockSpec(
            (tokens, step), lambda i, place_ref: (0, jnp.clip(i - chunk * 2, 0, 1))
        )

    shape = (2 * half, (count - 1) * tokens)
    return pl.pallas_call(
        body,
        grid_spec=pltpu.PrefetchScalarGridSpec(
            num_scalar_prefetch=1,
            grid=(chunks * 2,),
            in_specs=[pl.BlockSpec((half, step), lambda i, place_ref: (0, i))] * 2
            + [
                spec
                for chunk in range(chunks)
                for spec in [block_of(chunk)] * (count - 2) + [whole((tokens, step))] * 2
            ],
            out_specs=whole(shape),
            scratch_shapes=[pltpu.VMEM(shape, jnp.float32)],
        ),
        out_shape=jax.ShapeDtypeStruct(shape, jnp.bfloat16),
        cost_estimate=cost(2 * shape[0] * shape[1] * depth, 2 * depth * (shape[0] + shape[1])),
        name="project",
    )(place, *weights, *(block for chunk in grads for block in chunk))


def weight_terms(place, attended, grads):
    rows = len(grads) - 1
    width, length = attended.shape
    tokens, step = grads[-1].shape
    piece = width // 2 // rows

    def body(place_ref, attended_ref, *refs):
        ins, (keep, give) = refs[:-2], refs[-2:]
        columns = columns_of(ins, pl.program_id(0) == 1)
        term = dot(attended_ref[...], columns).astype(jnp.bfloat16)
        row, core = place_ref[0], place_ref[2]
        for side in range(2):
            for out, mine in ((keep, core == side), (give, core != side)):

                @pl.when(mine)
                def _():
                    for at in range(rows):
                        start = (side * rows + at) * piece
                        out[at ^ row] = term[start : start + piece]

    shape = jax.ShapeDtypeStruct((rows, piece, 2 * step), jnp.bfloat16)
    spec = pl.BlockSpec((rows, piece, step), lambda i, place_ref: (0, 0, i))
    return pl.pallas_call(
        body,
        grid_spec=pltpu.PrefetchScalarGridSpec(
            num_scalar_prefetch=1,
            grid=(2,),
            in_specs=[whole((width, length))]
            + [pl.BlockSpec((tokens, step), lambda i, place_ref: (0, i))] * (rows - 1)
            + [whole((tokens, step))] * 2,
            out_specs=[spec] * 2,
        ),
        out_shape=[shape] * 2,
        cost_estimate=cost(4 * width * length * step, 2 * (width * length + 2 * length * step)),
        name="weight_terms",
    )(place, attended, *grads)


def assemble(place, pieces):
    chunks, rows = len(pieces), len(pieces[0])
    piece, wide = pieces[0][0].shape
    step = wide // 2

    def body(place_ref, *refs):
        ins, out = refs[:-1], refs[-1]
        for chunk in range(chunks):

            @pl.when(pl.program_id(0) // 2 == chunk)
            def _():
                for slot in range(rows):
                    start = (place_ref[0] ^ slot) * piece
                    out[pl.ds(pl.multiple_of(start, 16), piece), :] = ins[chunk * rows + slot][
                        ...
                    ].astype(out.dtype)

    def block_of(chunk):
        return pl.BlockSpec((piece, step), lambda i, place_ref: (0, jnp.clip(i - 2 * chunk, 0, 1)))

    shape = (rows * piece, chunks * wide)
    return pl.pallas_call(
        body,
        grid_spec=pltpu.PrefetchScalarGridSpec(
            num_scalar_prefetch=1,
            grid=(2 * chunks,),
            in_specs=[block_of(chunk) for chunk in range(chunks) for _ in range(rows)],
            out_specs=pl.BlockSpec((rows * piece, step), lambda i, place_ref: (0, i)),
        ),
        out_shape=jax.ShapeDtypeStruct(shape, jnp.float32),
        cost_estimate=cost(0, 6 * shape[0] * shape[1]),
        name="assemble",
    )(place, *(block for chunk in pieces for block in chunk))


def after(value, *done):
    return lax.optimization_barrier((value, done))[0]


def by_heads(fsdp, rows, query_rows, key_rows, value_rows, grad_out, w_out):
    planes = fsdp // 2
    row = lax.axis_index("rows")
    member = lax.axis_index("fsdp")
    plane, core = member // 2, member % 2
    place = jnp.stack([row, plane, core]).astype(jnp.int32)

    def send(array, target):
        pairs = []
        for z in range(planes):
            for c in range(2):
                for r in range(rows):
                    to = target(z, c, r)
                    if to is not None:
                        pairs.append(((z * 2 + c) * rows + r, (to[0] * 2 + to[1]) * rows + to[2]))
        return lax.ppermute(array, ("fsdp", "rows"), pairs)

    def to_row(array, slot):
        return send(array, lambda z, c, r: (z, c, r ^ slot))

    def to_core(array):
        return send(array, lambda z, c, r: (z, 1 - c, r))

    def to_plane(array, ahead):
        return send(array, lambda z, c, r: ((z + ahead) % planes, c, r))

    grad_flat = grad_out[0]
    wide = grad_flat.shape[1] // 2

    def gather(chunk):
        by_x, by_y = to_row(chunk, 1), to_row(chunk, 2)
        even = to_row(by_x[:, : wide // 2], 2)
        odd = to_row(by_y[:, wide // 2 :], 1)
        return [chunk, by_x, by_y, even, odd]

    grads = [gather(grad_flat[:, :wide])]

    lines = [w_out] + [
        send(w_out, lambda z, c, r: ((z + ahead) % planes, c, r) if z == r else None)
        for ahead in range(1, planes)
    ]

    packed = pack(place, query_rows, key_rows, value_rows, rows)
    parts = [packed[0]] + [to_row(packed[slot], slot) for slot in range(1, rows)]
    probs, attended = forward(parts)
    grads.append(gather(after(grad_flat[:, wide:], parts)))

    def reduce_cores(attended, chunk):
        keep, give = weight_terms(place, attended, chunk)
        return keep, to_core(give)

    def spread(keep, got):
        both = [
            (keep[slot].astype(jnp.float32) + got[slot].astype(jnp.float32)).astype(jnp.bfloat16)
            for slot in range(rows)
        ]
        return [both[0]] + [to_row(both[slot], slot) for slot in range(1, rows)]

    def reduce_planes(blocks):
        stack = jnp.stack(blocks)

        def block_of(ahead):
            return lax.dynamic_index_in_dim(stack, ((plane + ahead) % planes) ^ row, 0, False)

        return block_of(0), [to_plane(block_of(ahead), ahead) for ahead in range(1, planes)]

    def collect(total, got):
        for part in got:
            total = total.astype(jnp.float32) + part.astype(jnp.float32)
        total = total.astype(jnp.bfloat16)
        return [total] + [to_row(total, slot) for slot in range(1, rows)]

    early = reduce_planes(spread(*reduce_cores(attended, grads[0])))
    late = reduce_cores(after(attended, early[0]), grads[1])
    lines = after(lines, late[0])
    here = lines[0]
    for ahead in range(1, planes):
        here = jnp.where((plane - row) % planes == ahead, lines[ahead], here)
    other = to_core(here)
    grad_attn = project(place, [here, other], grads)
    heads = probs.shape[0]
    sent = [backward(parts, probs, grad_attn, 0, 1)]
    blocks = after(spread(*late), sent[0][0])
    late = reduce_planes(blocks)
    sent.append(backward(parts, after(probs, late[0]), grad_attn, 1, heads - 1))
    back = [
        [message[0]]
        + [to_row(message[slot], slot) for slot in range(1, rows)]
        for message in sent
    ]
    pieces = [collect(*early), collect(*after(late, sent[1][0]))]
    grad_query, grad_key, grad_value = unpack(place, back)
    grad_w_out = assemble(place, pieces)
    return grad_query, grad_key, grad_value, grad_w_out


def by_tokens(query_rows, key_rows, value_rows, grad_out, w_out):
    tokens, width = query_rows.shape[1:]
    heads = width // HDIM
    factor = 1.0 / math.sqrt(HDIM)
    grad_flat = grad_out[0]
    groups = math.gcd(heads, 3)

    def split(array, count):
        return jnp.moveaxis(array.reshape(count, groups, heads // groups, HDIM), 1, 0)

    def join(array, count):
        return jnp.moveaxis(array, 0, 1).reshape(count, width)

    grad_attn = lax.dot_general(
        grad_flat,
        lax.all_gather(w_out, "fsdp", axis=0, tiled=True),
        NT,
        preferred_element_type=jnp.float32,
    ).astype(jnp.bfloat16)
    all_keys = lax.all_gather(key_rows, "rows", axis=1, tiled=True)
    all_values = lax.all_gather(value_rows, "rows", axis=1, tiled=True)
    length = all_keys.shape[1]

    def product(spec, a, b):
        return jnp.einsum(spec, a, b, preferred_element_type=jnp.float32)

    def attend(inputs):
        queries, keys, values, grads = inputs
        probs = jax.nn.softmax(product("qhd,khd->hqk", queries, keys) * factor, axis=-1)
        low = probs.astype(jnp.bfloat16)
        attended = product("hqk,khd->qhd", low, values)
        value_part = product("hqk,qhd->khd", low, grads)
        grad_probs = product("qhd,khd->hqk", grads, values)
        centre = jnp.sum(probs * grad_probs, axis=-1, keepdims=True)
        grad_scores = (probs * (grad_probs - centre)).astype(jnp.bfloat16)
        grad_query = product("hqk,khd->qhd", grad_scores, keys) * factor
        key_part = product("hqk,qhd->khd", grad_scores, queries) * factor
        return (
            attended.astype(jnp.bfloat16),
            grad_query.astype(jnp.bfloat16),
            key_part.astype(jnp.bfloat16),
            value_part.astype(jnp.bfloat16),
        )

    attended, grad_query, key_part, value_part = lax.map(
        attend,
        (
            split(query_rows[0], tokens),
            split(all_keys[0], length),
            split(all_values[0], length),
            split(grad_attn, tokens),
        ),
    )

    def scatter(part):
        part = join(part, length).reshape(1, length, width)
        return lax.psum_scatter(part, "rows", scatter_dimension=1, tiled=True)

    term = lax.dot_general(
        join(attended, tokens),
        grad_flat,
        (((0,), (0,)), ((), ())),
        preferred_element_type=jnp.float32,
    ).astype(jnp.bfloat16)
    share = lax.psum_scatter(term, "fsdp", scatter_dimension=0, tiled=True)
    grad_w_out = lax.psum(share, "rows").astype(jnp.float32)
    return (
        join(grad_query, tokens).reshape(1, tokens, width),
        scatter(key_part),
        scatter(value_part),
        grad_w_out,
    )


def solution(mesh):
    fsdp, rows = mesh.shape["fsdp"], mesh.shape["rows"]

    def local(query_rows, key_rows, value_rows, grad_out, w_out):
        heads = query_rows.shape[2] // HDIM
        if rows == 4 and fsdp == 2 * rows and heads % rows == 0:
            plan = functools.partial(by_heads, fsdp, rows)
        else:
            plan = by_tokens
        return plan(query_rows, key_rows, value_rows, grad_out, w_out)

    tokens = P("fsdp", "rows", None)
    return jax.shard_map(
        local,
        mesh=mesh,
        in_specs=(tokens, tokens, tokens, tokens, P("fsdp", None)),
        out_specs=(tokens, tokens, tokens, P("fsdp", None)),
        check_vma=False,
    )
```

```python
import functools
import math

import jax
import jax.numpy as jnp
from jax import lax
from jax.experimental import pallas as pl
from jax.experimental.pallas import tpu as pltpu
from jax.sharding import PartitionSpec as P


HDIM = 128


NT = (((1,), (1,)), ((), ()))
NN = (((1,), (0,)), ((), ()))


def dot(a, b, dims=NN):
    return lax.dot_general(a, b, dims, preferred_element_type=jnp.float32)


def whole(shape):
    return pl.BlockSpec(shape, lambda *_: (0,) * len(shape))


def cost(flops, moved, exps=0):
    return pl.CostEstimate(flops=flops, bytes_accessed=moved, transcendentals=exps)


def pack(place, query, key, value, rows):
    tokens, width = query.shape[1], query.shape[2] // rows

    def body(place_ref, *refs):
        ins, outs, (held, sems) = refs[:3], refs[3:-2], refs[-2:]
        moves = []
        for slot in (*range(1, rows), 0):
            start = pl.multiple_of((place_ref[0] ^ slot) * width, HDIM)
            for at in range(3):
                box = held.at[slot, at]
                moves.append(
                    (
                        pltpu.make_async_copy(
                            ins[at].at[0, :, pl.ds(start, width)], box, sems.at[0, slot, at]
                        ),
                        pltpu.make_async_copy(box, outs[slot].at[at], sems.at[1, slot, at]),
                    )
                )
        run(moves)

    shape = (3, tokens, width)
    return pl.pallas_call(
        body,
        grid_spec=pltpu.PrefetchScalarGridSpec(
            num_scalar_prefetch=1,
            grid=(1,),
            in_specs=[pl.BlockSpec(memory_space=pltpu.HBM)] * 3,
            out_specs=[pl.BlockSpec(memory_space=pltpu.HBM)] * rows,
            scratch_shapes=[
                pltpu.VMEM((rows, *shape), query.dtype),
                pltpu.SemaphoreType.DMA((2, rows, 3)),
            ],
        ),
        out_shape=[jax.ShapeDtypeStruct(shape, query.dtype)] * rows,
        cost_estimate=cost(0, 12 * query.size),
        name="pack",
    )(place, query, key, value)


def run(moves):
    for fetch, _ in moves:
        fetch.start()
    for fetch, store in moves:
        fetch.wait()
        store.start()
    for _, store in moves:
        store.wait()


def unpack(place, parts):
    calls, rows = len(parts), len(parts[0])
    tokens = parts[0][0].shape[1]
    widths = [part[0].shape[2] for part in parts]
    starts = [sum(widths[:at]) for at in range(calls + 1)]
    width = starts[-1]

    def body(place_ref, *refs):
        ins, outs, held, sems = refs[: calls * rows], refs[calls * rows : -2], refs[-2], refs[-1]
        moves = []
        for call in range(calls):
            for slot in range(rows):
                start = (place_ref[0] ^ slot) * width + starts[call]
                start = pl.multiple_of(start, HDIM)
                for at in range(3):
                    box = held.at[slot, at, :, starts[call] : starts[call + 1]]
                    moves.append(
                        (
                            pltpu.make_async_copy(
                                ins[call * rows + slot].at[at], box, sems.at[0, call, slot, at]
                            ),
                            pltpu.make_async_copy(
                                box,
                                outs[at].at[0, :, pl.ds(start, widths[call])],
                                sems.at[1, call, slot, at],
                            ),
                        )
                    )
        run(moves)

    full = jax.ShapeDtypeStruct((1, tokens, width * rows), parts[0][0].dtype)
    return pl.pallas_call(
        body,
        grid_spec=pltpu.PrefetchScalarGridSpec(
            num_scalar_prefetch=1,
            grid=(1,),
            in_specs=[pl.BlockSpec(memory_space=pltpu.HBM)] * (calls * rows),
            out_specs=[pl.BlockSpec(memory_space=pltpu.HBM)] * 3,
            scratch_shapes=[
                pltpu.VMEM((rows, 3, tokens, width), parts[0][0].dtype),
                pltpu.SemaphoreType.DMA((2, calls, rows, 3)),
            ],
        ),
        out_shape=[full] * 3,
        cost_estimate=cost(0, 12 * tokens * width * rows),
        name="unpack",
    )(place, *(block for part in parts for block in part))


def forward(parts):
    rows = len(parts)
    _, tokens, width = parts[0].shape
    length, heads = rows * tokens, width // HDIM
    scale = math.log2(math.e) / math.sqrt(HDIM)

    def body(*refs):
        ins, (probs_ref, attended_ref) = refs[:rows], refs[rows:]
        keys = jnp.concatenate([ref[1] for ref in ins], axis=0)
        values = jnp.concatenate([ref[2] for ref in ins], axis=0).T
        for slot in range(rows):
            across = slice(slot * tokens, (slot + 1) * tokens)
            scores = dot(keys, ins[slot][0], NT)
            top = jnp.max(scores, axis=0, keepdims=True)
            powers = jnp.exp2((scores - top) * scale)
            total = jnp.sum(powers, axis=0, keepdims=True)
            probs = (powers * (1.0 / total)).astype(jnp.bfloat16)
            probs_ref[0, :, across] = probs
            attended_ref[:, across] = dot(values, probs).astype(jnp.bfloat16)

    part = pl.BlockSpec((3, tokens, HDIM), lambda h: (0, 0, h))
    return pl.pallas_call(
        body,
        grid=(heads,),
        in_specs=[part] * rows,
        out_specs=[
            pl.BlockSpec((1, length, length), lambda h: (h, 0, 0)),
            pl.BlockSpec((HDIM, length), lambda h: (h, 0)),
        ],
        out_shape=[
            jax.ShapeDtypeStruct((heads, length, length), jnp.bfloat16),
            jax.ShapeDtypeStruct((width, length), jnp.bfloat16),
        ],
        cost_estimate=cost(
            8 * heads * length * length * HDIM, 2 * heads * length * length, heads * length * length
        ),
        name="forward",
    )(*parts)


def backward(parts, probs, grad_attn, first, count):
    rows = len(parts)
    tokens = parts[0].shape[1]
    length = rows * tokens
    factor = 1.0 / math.sqrt(HDIM)

    def body(*refs):
        ins, (probs_ref, grad_ref) = refs[:rows], refs[rows : rows + 2]
        outs, scores_ref = refs[rows + 2 : -1], refs[-1]
        queries = jnp.concatenate([ref[0] for ref in ins], axis=0)
        keys = jnp.concatenate([ref[1] for ref in ins], axis=0).T
        values = jnp.concatenate([ref[2] for ref in ins], axis=0)
        for slot in range(rows):
            across = slice(slot * tokens, (slot + 1) * tokens)
            probs = probs_ref[0, :, across].astype(jnp.float32)
            terms = probs * dot(values, grad_ref[:, across])
            centre = jnp.sum(terms, axis=0, keepdims=True)
            scores_ref[:, across] = (terms - probs * centre).astype(jnp.bfloat16)
        scores = scores_ref[...]
        grad_query = (dot(keys, scores) * factor).T
        grad_key = dot(scores, queries) * factor
        grad_value = dot(probs_ref[0], grad_ref[...], NT)
        for slot in range(rows):
            down = slice(slot * tokens, (slot + 1) * tokens)
            outs[slot][0] = grad_query[down].astype(jnp.bfloat16)
            outs[slot][1] = grad_key[down].astype(jnp.bfloat16)
            outs[slot][2] = grad_value[down].astype(jnp.bfloat16)

    part = pl.BlockSpec((3, tokens, HDIM), lambda i: (0, 0, first + i))
    shape = (3, tokens, count * HDIM)
    return pl.pallas_call(
        body,
        grid=(count,),
        in_specs=[part] * rows
        + [
            pl.BlockSpec((1, length, length), lambda i: (first + i, 0, 0)),
            pl.BlockSpec((HDIM, length), lambda i: (first + i, 0)),
        ],
        out_specs=[pl.BlockSpec((3, tokens, HDIM), lambda i: (0, 0, i))] * rows,
        out_shape=[jax.ShapeDtypeStruct(shape, jnp.bfloat16)] * rows,
        scratch_shapes=[pltpu.VMEM((length, length), jnp.bfloat16)],
        cost_estimate=cost(8 * count * length * length * HDIM, 2 * count * length * length),
        name="backward",
    )(*parts, probs, grad_attn)


def stacked(refs):
    return jnp.concatenate([ref[...] for ref in refs], axis=0)


def project(place, weights, grads):
    chunks, count = len(grads), len(grads[0])
    half, depth = weights[0].shape
    step = grads[0][0].shape[1] // 2

    def body(place_ref, *refs):
        first, second = refs[:2]
        ins, out, total = refs[2:-2], refs[-2], refs[-1]
        at = pl.program_id(0)
        lines = jnp.concatenate([first[...], second[...]], axis=0)
        for chunk in range(chunks):

            @pl.when(at // 2 == chunk)
            def _():
                term = dot(lines, stacked(ins[chunk * count : (chunk + 1) * count]), NT)
                if chunk:
                    total[...] += term
                else:
                    total[...] = jnp.where(at == 0, 0.0, total[...]) + term

        @pl.when(at == chunks * 2 - 1)
        def _():
            for core in range(2):

                @pl.when(place_ref[2] == core)
                def _():
                    out[core * half : (core + 1) * half] = total[:half].astype(out.dtype)
                    out[(1 - core) * half : (2 - core) * half] = total[half:].astype(out.dtype)

    def block_of(chunk, block):
        return pl.BlockSpec(
            (block.shape[0], step), lambda i, place_ref: (0, jnp.clip(i - chunk * 2, 0, 1))
        )

    shape = (2 * half, sum(block.shape[0] for block in grads[0]))
    return pl.pallas_call(
        body,
        grid_spec=pltpu.PrefetchScalarGridSpec(
            num_scalar_prefetch=1,
            grid=(chunks * 2,),
            in_specs=[pl.BlockSpec((half, step), lambda i, place_ref: (0, i))] * 2
            + [block_of(chunk, block) for chunk in range(chunks) for block in grads[chunk]],
            out_specs=whole(shape),
            scratch_shapes=[pltpu.VMEM(shape, jnp.float32)],
        ),
        out_shape=jax.ShapeDtypeStruct(shape, jnp.bfloat16),
        cost_estimate=cost(2 * shape[0] * shape[1] * depth, 2 * depth * (shape[0] + shape[1])),
        name="project",
    )(place, *weights, *(block for chunk in grads for block in chunk))


def weight_terms(place, attended, grads, rows):
    width, length = attended.shape
    step = grads[0].shape[1] // 2
    piece = width // 2 // rows

    def body(place_ref, attended_ref, *refs):
        ins, (keep, give) = refs[:-2], refs[-2:]
        term = dot(attended_ref[...], stacked(ins)).astype(jnp.bfloat16)
        row, core = place_ref[0], place_ref[2]
        for side in range(2):
            for out, mine in ((keep, core == side), (give, core != side)):

                @pl.when(mine)
                def _():
                    for at in range(rows):
                        start = (side * rows + at) * piece
                        out[at ^ row] = term[start : start + piece]

    shape = jax.ShapeDtypeStruct((rows, piece, 2 * step), jnp.bfloat16)
    spec = pl.BlockSpec((rows, piece, step), lambda i, place_ref: (0, 0, i))
    return pl.pallas_call(
        body,
        grid_spec=pltpu.PrefetchScalarGridSpec(
            num_scalar_prefetch=1,
            grid=(2,),
            in_specs=[whole((width, length))]
            + [pl.BlockSpec((block.shape[0], step), lambda i, place_ref: (0, i)) for block in grads],
            out_specs=[spec] * 2,
        ),
        out_shape=[shape] * 2,
        cost_estimate=cost(4 * width * length * step, 2 * (width * length + 2 * length * step)),
        name="weight_terms",
    )(place, attended, *grads)


def assemble(place, pieces):
    chunks, rows = len(pieces), len(pieces[0])
    piece, wide = pieces[0][0].shape

    def body(place_ref, *refs):
        ins, out = refs[:-1], refs[-1]
        for chunk in range(chunks):
            for slot in range(rows):
                start = pl.multiple_of((place_ref[0] ^ slot) * piece, 16)
                out[pl.ds(start, piece), chunk * wide : (chunk + 1) * wide] = ins[
                    chunk * rows + slot
                ][...].astype(out.dtype)

    shape = (rows * piece, chunks * wide)
    return pl.pallas_call(
        body,
        grid_spec=pltpu.PrefetchScalarGridSpec(
            num_scalar_prefetch=1,
            grid=(1,),
            in_specs=[whole((piece, wide))] * (chunks * rows),
            out_specs=whole(shape),
        ),
        out_shape=jax.ShapeDtypeStruct(shape, jnp.float32),
        cost_estimate=cost(0, 6 * shape[0] * shape[1]),
        name="assemble",
    )(place, *(block for chunk in pieces for block in chunk))


def after(value, *done):
    return lax.optimization_barrier((value, done))[0]


def by_heads(fsdp, rows, query_rows, key_rows, value_rows, grad_out, w_out):
    planes = fsdp // 2
    row = lax.axis_index("rows")
    member = lax.axis_index("fsdp")
    plane, core = member // 2, member % 2
    place = jnp.stack([row, plane, core]).astype(jnp.int32)

    def send(array, target):
        pairs = []
        for z in range(planes):
            for c in range(2):
                for r in range(rows):
                    to = target(z, c, r)
                    if to is not None:
                        pairs.append(((z * 2 + c) * rows + r, (to[0] * 2 + to[1]) * rows + to[2]))
        return lax.ppermute(array, ("fsdp", "rows"), pairs)

    def to_row(array, slot):
        return send(array, lambda z, c, r: (z, c, r ^ slot))

    def to_core(array):
        return send(array, lambda z, c, r: (z, 1 - c, r))

    def to_plane(array, ahead):
        return send(array, lambda z, c, r: ((z + ahead) % planes, c, r))

    grad_flat = grad_out[0]
    wide = grad_flat.shape[1] // 2

    def gather(chunk):
        by_x, by_y = to_row(chunk, 1), to_row(chunk, 2)
        cut = chunk.shape[0] // 2
        upper = to_row(by_x[:cut], 2)
        lower = to_row(by_y[cut:], 1)
        return [chunk, by_x, by_y, upper, lower]

    grads = [gather(grad_flat[:, :wide])]

    lines = [w_out] + [
        send(w_out, lambda z, c, r: ((z + ahead) % planes, c, r) if z == r else None)
        for ahead in range(1, planes)
    ]

    packed = pack(place, query_rows, key_rows, value_rows, rows)
    parts = [packed[0]] + [to_row(packed[slot], slot) for slot in range(1, rows)]
    probs, attended = forward(parts)
    grads.append(gather(after(grad_flat[:, wide:], parts)))

    def reduce_cores(attended, chunk):
        keep, give = weight_terms(place, attended, chunk, rows)
        return keep, to_core(give)

    def spread(keep, got):
        both = [
            (keep[slot].astype(jnp.float32) + got[slot].astype(jnp.float32)).astype(jnp.bfloat16)
            for slot in range(rows)
        ]
        return [both[0]] + [to_row(both[slot], slot) for slot in range(1, rows)]

    def reduce_planes(blocks):
        stack = jnp.stack(blocks)

        def block_of(ahead):
            return lax.dynamic_index_in_dim(stack, ((plane + ahead) % planes) ^ row, 0, False)

        return block_of(0), [to_plane(block_of(ahead), ahead) for ahead in range(1, planes)]

    def collect(total, got):
        for part in got:
            total = total.astype(jnp.float32) + part.astype(jnp.float32)
        total = total.astype(jnp.bfloat16)
        return [total] + [to_row(total, slot) for slot in range(1, rows)]

    early = reduce_planes(spread(*reduce_cores(attended, grads[0])))
    late = reduce_cores(after(attended, early[0]), grads[1])
    lines = after(lines, late[0])
    here = lines[0]
    for ahead in range(1, planes):
        here = jnp.where((plane - row) % planes == ahead, lines[ahead], here)
    other = to_core(here)
    grad_attn = project(place, [here, other], grads)
    heads = probs.shape[0]
    blocks = spread(*after(late, grad_attn))
    sent = [backward(parts, probs, grad_attn, 0, 1)]
    late = reduce_planes(after(blocks, sent[0][0]))
    sent.append(backward(parts, after(probs, late[0]), grad_attn, 1, heads - 1))
    back = [
        [message[0]]
        + [to_row(message[slot], slot) for slot in range(1, rows)]
        for message in sent
    ]
    pieces = [collect(*after(early, grad_attn)), collect(*after(late, sent[1][0]))]
    grad_query, grad_key, grad_value = unpack(place, back)
    grad_w_out = assemble(place, pieces)
    return grad_query, grad_key, grad_value, grad_w_out


def by_tokens(query_rows, key_rows, value_rows, grad_out, w_out):
    tokens, width = query_rows.shape[1:]
    heads = width // HDIM
    factor = 1.0 / math.sqrt(HDIM)
    grad_flat = grad_out[0]
    groups = math.gcd(heads, 3)

    def split(array, count):
        return jnp.moveaxis(array.reshape(count, groups, heads // groups, HDIM), 1, 0)

    def join(array, count):
        return jnp.moveaxis(array, 0, 1).reshape(count, width)

    grad_attn = lax.dot_general(
        grad_flat,
        lax.all_gather(w_out, "fsdp", axis=0, tiled=True),
        NT,
        preferred_element_type=jnp.float32,
    ).astype(jnp.bfloat16)
    all_keys = lax.all_gather(key_rows, "rows", axis=1, tiled=True)
    all_values = lax.all_gather(value_rows, "rows", axis=1, tiled=True)
    length = all_keys.shape[1]

    def product(spec, a, b):
        return jnp.einsum(spec, a, b, preferred_element_type=jnp.float32)

    def attend(inputs):
        queries, keys, values, grads = inputs
        probs = jax.nn.softmax(product("qhd,khd->hqk", queries, keys) * factor, axis=-1)
        low = probs.astype(jnp.bfloat16)
        attended = product("hqk,khd->qhd", low, values)
        value_part = product("hqk,qhd->khd", low, grads)
        grad_probs = product("qhd,khd->hqk", grads, values)
        centre = jnp.sum(probs * grad_probs, axis=-1, keepdims=True)
        grad_scores = (probs * (grad_probs - centre)).astype(jnp.bfloat16)
        grad_query = product("hqk,khd->qhd", grad_scores, keys) * factor
        key_part = product("hqk,qhd->khd", grad_scores, queries) * factor
        return (
            attended.astype(jnp.bfloat16),
            grad_query.astype(jnp.bfloat16),
            key_part.astype(jnp.bfloat16),
            value_part.astype(jnp.bfloat16),
        )

    attended, grad_query, key_part, value_part = lax.map(
        attend,
        (
            split(query_rows[0], tokens),
            split(all_keys[0], length),
            split(all_values[0], length),
            split(grad_attn, tokens),
        ),
    )

    def scatter(part):
        part = join(part, length).reshape(1, length, width)
        return lax.psum_scatter(part, "rows", scatter_dimension=1, tiled=True)

    term = lax.dot_general(
        join(attended, tokens),
        grad_flat,
        (((0,), (0,)), ((), ())),
        preferred_element_type=jnp.float32,
    ).astype(jnp.bfloat16)
    share = lax.psum_scatter(term, "fsdp", scatter_dimension=0, tiled=True)
    grad_w_out = lax.psum(share, "rows").astype(jnp.float32)
    return (
        join(grad_query, tokens).reshape(1, tokens, width),
        scatter(key_part),
        scatter(value_part),
        grad_w_out,
    )


def solution(mesh):
    fsdp, rows = mesh.shape["fsdp"], mesh.shape["rows"]

    def local(query_rows, key_rows, value_rows, grad_out, w_out):
        heads = query_rows.shape[2] // HDIM
        if rows == 4 and fsdp == 2 * rows and heads % rows == 0:
            plan = functools.partial(by_heads, fsdp, rows)
        else:
            plan = by_tokens
        return plan(query_rows, key_rows, value_rows, grad_out, w_out)

    tokens = P("fsdp", "rows", None)
    return jax.shard_map(
        local,
        mesh=mesh,
        in_specs=(tokens, tokens, tokens, tokens, P("fsdp", None)),
        out_specs=(tokens, tokens, tokens, P("fsdp", None)),
        check_vma=False,
    )
```

```python
import functools
import math

import jax
import jax.numpy as jnp
from jax import lax
from jax.experimental import pallas as pl
from jax.experimental.pallas import tpu as pltpu
from jax.sharding import PartitionSpec as P


HDIM = 128


NT = (((1,), (1,)), ((), ()))
NN = (((1,), (0,)), ((), ()))


def dot(a, b, dims=NN):
    return lax.dot_general(a, b, dims, preferred_element_type=jnp.float32)


def far(*arrays):
    return [pltpu.with_memory_space_constraint(array, pltpu.HBM) for array in arrays]


def whole(shape):
    return pl.BlockSpec(shape, lambda *_: (0,) * len(shape))


def cost(flops, moved, exps=0):
    return pl.CostEstimate(flops=flops, bytes_accessed=moved, transcendentals=exps)


def pack(place, query, key, value, rows):
    tokens, width = query.shape[1], query.shape[2] // rows

    def body(place_ref, *refs):
        ins, outs, (held, sems) = refs[:3], refs[3:-2], refs[-2:]
        moves = []
        for slot in (*range(1, rows), 0):
            start = pl.multiple_of((place_ref[0] ^ slot) * width, HDIM)
            for at in range(3):
                box = held.at[slot, at]
                moves.append(
                    (
                        pltpu.make_async_copy(
                            ins[at].at[0, :, pl.ds(start, width)], box, sems.at[0, slot, at]
                        ),
                        pltpu.make_async_copy(box, outs[slot].at[at], sems.at[1, slot, at]),
                    )
                )
        run(moves)

    shape = (3, tokens, width)
    return pl.pallas_call(
        body,
        grid_spec=pltpu.PrefetchScalarGridSpec(
            num_scalar_prefetch=1,
            grid=(1,),
            in_specs=[pl.BlockSpec(memory_space=pltpu.HBM)] * 3,
            out_specs=[pl.BlockSpec(memory_space=pltpu.HBM)] * rows,
            scratch_shapes=[
                pltpu.VMEM((rows, *shape), query.dtype),
                pltpu.SemaphoreType.DMA((2, rows, 3)),
            ],
        ),
        out_shape=[jax.ShapeDtypeStruct(shape, query.dtype)] * rows,
        cost_estimate=cost(0, 12 * query.size),
        name="pack",
    )(place, query, key, value)


def run(moves):
    for fetch, _ in moves:
        fetch.start()
    for fetch, store in moves:
        fetch.wait()
        store.start()
    for _, store in moves:
        store.wait()


def unpack(place, parts):
    calls, rows = len(parts), len(parts[0])
    tokens = parts[0][0].shape[1]
    widths = [part[0].shape[2] for part in parts]
    starts = [sum(widths[:at]) for at in range(calls + 1)]
    width = starts[-1]

    def body(place_ref, *refs):
        ins, outs, held, sems = refs[: calls * rows], refs[calls * rows : -2], refs[-2], refs[-1]
        moves = []
        for call in range(calls):
            for slot in range(rows):
                start = (place_ref[0] ^ slot) * width + starts[call]
                start = pl.multiple_of(start, HDIM)
                for at in range(3):
                    box = held.at[slot, at, :, starts[call] : starts[call + 1]]
                    moves.append(
                        (
                            pltpu.make_async_copy(
                                ins[call * rows + slot].at[at], box, sems.at[0, call, slot, at]
                            ),
                            pltpu.make_async_copy(
                                box,
                                outs[at].at[0, :, pl.ds(start, widths[call])],
                                sems.at[1, call, slot, at],
                            ),
                        )
                    )
        run(moves)

    full = jax.ShapeDtypeStruct((1, tokens, width * rows), parts[0][0].dtype)
    return pl.pallas_call(
        body,
        grid_spec=pltpu.PrefetchScalarGridSpec(
            num_scalar_prefetch=1,
            grid=(1,),
            in_specs=[pl.BlockSpec(memory_space=pltpu.HBM)] * (calls * rows),
            out_specs=[pl.BlockSpec(memory_space=pltpu.HBM)] * 3,
            scratch_shapes=[
                pltpu.VMEM((rows, 3, tokens, width), parts[0][0].dtype),
                pltpu.SemaphoreType.DMA((2, calls, rows, 3)),
            ],
        ),
        out_shape=[full] * 3,
        cost_estimate=cost(0, 12 * tokens * width * rows),
        name="unpack",
    )(place, *far(*(block for part in parts for block in part)))


def forward(parts):
    rows = len(parts)
    _, tokens, width = parts[0].shape
    length, heads = rows * tokens, width // HDIM
    scale = math.log2(math.e) / math.sqrt(HDIM)

    def body(*refs):
        ins, (probs_ref, attended_ref) = refs[:rows], refs[rows:]
        keys = jnp.concatenate([ref[1] for ref in ins], axis=0)
        values = jnp.concatenate([ref[2] for ref in ins], axis=0).T
        for slot in range(rows):
            across = slice(slot * tokens, (slot + 1) * tokens)
            scores = dot(keys, ins[slot][0], NT)
            top = jnp.max(scores, axis=0, keepdims=True)
            powers = jnp.exp2((scores - top) * scale)
            total = jnp.sum(powers, axis=0, keepdims=True)
            probs = (powers * (1.0 / total)).astype(jnp.bfloat16)
            probs_ref[0, :, across] = probs
            attended_ref[:, across] = dot(values, probs).astype(jnp.bfloat16)

    part = pl.BlockSpec((3, tokens, HDIM), lambda h: (0, 0, h))
    return pl.pallas_call(
        body,
        grid=(heads,),
        in_specs=[part] * rows,
        out_specs=[
            pl.BlockSpec((1, length, length), lambda h: (h, 0, 0)),
            pl.BlockSpec((HDIM, length), lambda h: (h, 0)),
        ],
        out_shape=[
            jax.ShapeDtypeStruct((heads, length, length), jnp.bfloat16),
            jax.ShapeDtypeStruct((width, length), jnp.bfloat16),
        ],
        cost_estimate=cost(
            8 * heads * length * length * HDIM, 2 * heads * length * length, heads * length * length
        ),
        name="forward",
    )(*far(*parts))


def backward(parts, probs, grad_attn, first, count):
    rows = len(parts)
    tokens = parts[0].shape[1]
    length = rows * tokens
    factor = 1.0 / math.sqrt(HDIM)

    def body(*refs):
        ins, (probs_ref, grad_ref) = refs[:rows], refs[rows : rows + 2]
        outs, scores_ref = refs[rows + 2 : -1], refs[-1]
        queries = jnp.concatenate([ref[0] for ref in ins], axis=0)
        keys = jnp.concatenate([ref[1] for ref in ins], axis=0).T
        values = jnp.concatenate([ref[2] for ref in ins], axis=0)
        for slot in range(rows):
            across = slice(slot * tokens, (slot + 1) * tokens)
            probs = probs_ref[0, :, across].astype(jnp.float32)
            terms = probs * dot(values, grad_ref[:, across])
            centre = jnp.sum(terms, axis=0, keepdims=True)
            scores_ref[:, across] = (terms - probs * centre).astype(jnp.bfloat16)
        scores = scores_ref[...]
        grad_query = (dot(keys, scores) * factor).T
        grad_key = dot(scores, queries) * factor
        grad_value = dot(probs_ref[0], grad_ref[...], NT)
        for slot in range(rows):
            down = slice(slot * tokens, (slot + 1) * tokens)
            outs[slot][0] = grad_query[down].astype(jnp.bfloat16)
            outs[slot][1] = grad_key[down].astype(jnp.bfloat16)
            outs[slot][2] = grad_value[down].astype(jnp.bfloat16)

    part = pl.BlockSpec((3, tokens, HDIM), lambda i: (0, 0, first + i))
    shape = (3, tokens, count * HDIM)
    return pl.pallas_call(
        body,
        grid=(count,),
        in_specs=[part] * rows
        + [
            pl.BlockSpec((1, length, length), lambda i: (first + i, 0, 0)),
            pl.BlockSpec((HDIM, length), lambda i: (first + i, 0)),
        ],
        out_specs=[pl.BlockSpec((3, tokens, HDIM), lambda i: (0, 0, i))] * rows,
        out_shape=[jax.ShapeDtypeStruct(shape, jnp.bfloat16)] * rows,
        scratch_shapes=[pltpu.VMEM((length, length), jnp.bfloat16)],
        cost_estimate=cost(8 * count * length * length * HDIM, 2 * count * length * length),
        name="backward",
    )(*far(*parts, probs, grad_attn))


def stacked(refs):
    return jnp.concatenate([ref[...] for ref in refs], axis=0)


def project(place, weights, grads):
    chunks, count = len(grads), len(grads[0])
    half, depth = weights[0].shape
    step = grads[0][0].shape[1] // 2

    def body(place_ref, *refs):
        first, second = refs[:2]
        ins, out, total = refs[2:-2], refs[-2], refs[-1]
        at = pl.program_id(0)
        lines = jnp.concatenate([first[...], second[...]], axis=0)
        for chunk in range(chunks):

            @pl.when(at // 2 == chunk)
            def _():
                term = dot(lines, stacked(ins[chunk * count : (chunk + 1) * count]), NT)
                if chunk:
                    total[...] += term
                else:
                    total[...] = jnp.where(at == 0, 0.0, total[...]) + term

        @pl.when(at == chunks * 2 - 1)
        def _():
            for core in range(2):

                @pl.when(place_ref[2] == core)
                def _():
                    out[core * half : (core + 1) * half] = total[:half].astype(out.dtype)
                    out[(1 - core) * half : (2 - core) * half] = total[half:].astype(out.dtype)

    def block_of(chunk, block):
        return pl.BlockSpec(
            (block.shape[0], step), lambda i, place_ref: (0, jnp.clip(i - chunk * 2, 0, 1))
        )

    shape = (2 * half, sum(block.shape[0] for block in grads[0]))
    return pl.pallas_call(
        body,
        grid_spec=pltpu.PrefetchScalarGridSpec(
            num_scalar_prefetch=1,
            grid=(chunks * 2,),
            in_specs=[pl.BlockSpec((half, step), lambda i, place_ref: (0, i))] * 2
            + [block_of(chunk, block) for chunk in range(chunks) for block in grads[chunk]],
            out_specs=whole(shape),
            scratch_shapes=[pltpu.VMEM(shape, jnp.float32)],
        ),
        out_shape=jax.ShapeDtypeStruct(shape, jnp.bfloat16),
        cost_estimate=cost(2 * shape[0] * shape[1] * depth, 2 * depth * (shape[0] + shape[1])),
        name="project",
    )(place, *far(*weights, *(block for chunk in grads for block in chunk)))


def weight_terms(place, attended, grads, rows):
    width, length = attended.shape
    step = grads[0].shape[1] // 2
    piece = width // 2 // rows

    def body(place_ref, attended_ref, *refs):
        ins, (keep, give) = refs[:-2], refs[-2:]
        term = dot(attended_ref[...], stacked(ins)).astype(jnp.bfloat16)
        row, core = place_ref[0], place_ref[2]
        for side in range(2):
            for out, mine in ((keep, core == side), (give, core != side)):

                @pl.when(mine)
                def _():
                    for at in range(rows):
                        start = (side * rows + at) * piece
                        out[at ^ row] = term[start : start + piece]

    shape = jax.ShapeDtypeStruct((rows, piece, 2 * step), jnp.bfloat16)
    spec = pl.BlockSpec((rows, piece, step), lambda i, place_ref: (0, 0, i))
    return pl.pallas_call(
        body,
        grid_spec=pltpu.PrefetchScalarGridSpec(
            num_scalar_prefetch=1,
            grid=(2,),
            in_specs=[whole((width, length))]
            + [pl.BlockSpec((block.shape[0], step), lambda i, place_ref: (0, i)) for block in grads],
            out_specs=[spec] * 2,
        ),
        out_shape=[shape] * 2,
        cost_estimate=cost(4 * width * length * step, 2 * (width * length + 2 * length * step)),
        name="weight_terms",
    )(place, *far(attended, *grads))


def assemble(place, pieces):
    chunks, rows = len(pieces), len(pieces[0])
    piece, wide = pieces[0][0].shape

    def body(place_ref, *refs):
        ins, out = refs[:-1], refs[-1]
        for chunk in range(chunks):
            for slot in range(rows):
                start = pl.multiple_of((place_ref[0] ^ slot) * piece, 16)
                out[pl.ds(start, piece), chunk * wide : (chunk + 1) * wide] = ins[
                    chunk * rows + slot
                ][...].astype(out.dtype)

    shape = (rows * piece, chunks * wide)
    return pl.pallas_call(
        body,
        grid_spec=pltpu.PrefetchScalarGridSpec(
            num_scalar_prefetch=1,
            grid=(1,),
            in_specs=[whole((piece, wide))] * (chunks * rows),
            out_specs=whole(shape),
        ),
        out_shape=jax.ShapeDtypeStruct(shape, jnp.float32),
        cost_estimate=cost(0, 6 * shape[0] * shape[1]),
        name="assemble",
    )(place, *far(*(block for chunk in pieces for block in chunk)))


def after(value, *done):
    return lax.optimization_barrier((value, done))[0]


def by_heads(fsdp, rows, query_rows, key_rows, value_rows, grad_out, w_out):
    planes = fsdp // 2
    row = lax.axis_index("rows")
    member = lax.axis_index("fsdp")
    plane, core = member // 2, member % 2
    place = jnp.stack([row, plane, core]).astype(jnp.int32)

    def send(array, target):
        pairs = []
        for z in range(planes):
            for c in range(2):
                for r in range(rows):
                    to = target(z, c, r)
                    if to is not None:
                        pairs.append(((z * 2 + c) * rows + r, (to[0] * 2 + to[1]) * rows + to[2]))
        return lax.ppermute(array, ("fsdp", "rows"), pairs)

    def to_row(array, slot):
        return send(array, lambda z, c, r: (z, c, r ^ slot))

    def to_core(array):
        return send(array, lambda z, c, r: (z, 1 - c, r))

    def to_plane(array, ahead):
        return send(array, lambda z, c, r: ((z + ahead) % planes, c, r))

    grad_flat = grad_out[0]
    wide = grad_flat.shape[1] // 2

    def gather(chunk, *done):
        by_x, by_y = to_row(chunk, 1), to_row(chunk, 2)
        by_x, by_y = after((by_x, by_y), *done)
        cut = chunk.shape[0] // 2
        upper = to_row(by_x[:cut], 2)
        lower = to_row(by_y[cut:], 1)
        return [chunk, by_x, by_y, upper, lower]

    grads = [gather(grad_flat[:, :wide])]

    lines = [w_out] + [
        send(w_out, lambda z, c, r: ((z + ahead) % planes, c, r) if z == r else None)
        for ahead in range(1, planes)
    ]

    packed = pack(place, query_rows, key_rows, value_rows, rows)
    parts = [packed[0]] + [to_row(packed[slot], slot) for slot in range(1, rows)]
    probs, attended = forward(parts)
    grads.append(gather(after(grad_flat[:, wide:], parts), attended))

    def reduce_cores(attended, chunk):
        keep, give = weight_terms(place, attended, chunk, rows)
        return keep, to_core(give)

    def spread(keep, got):
        both = [
            (keep[slot].astype(jnp.float32) + got[slot].astype(jnp.float32)).astype(jnp.bfloat16)
            for slot in range(rows)
        ]
        return [both[0]] + [to_row(both[slot], slot) for slot in range(1, rows)]

    def reduce_planes(blocks):
        stack = jnp.stack(blocks)

        def block_of(ahead):
            return lax.dynamic_index_in_dim(stack, ((plane + ahead) % planes) ^ row, 0, False)

        return block_of(0), [to_plane(block_of(ahead), ahead) for ahead in range(1, planes)]

    def collect(total, got):
        for part in got:
            total = total.astype(jnp.float32) + part.astype(jnp.float32)
        total = total.astype(jnp.bfloat16)
        return [total] + [to_row(total, slot) for slot in range(1, rows)]

    blocks = spread(*reduce_cores(attended, grads[0]))
    late = reduce_cores(attended, grads[1])
    early = reduce_planes(after(blocks, late[0]))
    lines = after(lines, late[0])
    here = lines[0]
    for ahead in range(1, planes):
        here = jnp.where((plane - row) % planes == ahead, lines[ahead], here)
    other = to_core(here)
    grad_attn = project(place, [here, other], grads)
    heads = probs.shape[0]
    blocks = spread(*after(late, early[0]))
    sent = [backward(parts, probs, grad_attn, 0, 1)]
    late = reduce_planes(after(blocks, sent[0][0]))
    sent.append(backward(parts, after(probs, late[0]), grad_attn, 1, heads - 1))
    back = [
        [message[0]]
        + [to_row(message[slot], slot) for slot in range(1, rows)]
        for message in sent
    ]
    pieces = [collect(*after(early, sent[0][0])), collect(*after(late, sent[1][0]))]
    grad_query, grad_key, grad_value = unpack(place, back)
    grad_w_out = assemble(place, pieces)
    return grad_query, grad_key, grad_value, grad_w_out


def by_tokens(query_rows, key_rows, value_rows, grad_out, w_out):
    tokens, width = query_rows.shape[1:]
    heads = width // HDIM
    factor = 1.0 / math.sqrt(HDIM)
    grad_flat = grad_out[0]
    groups = math.gcd(heads, 3)

    def split(array, count):
        return jnp.moveaxis(array.reshape(count, groups, heads // groups, HDIM), 1, 0)

    def join(array, count):
        return jnp.moveaxis(array, 0, 1).reshape(count, width)

    grad_attn = lax.dot_general(
        grad_flat,
        lax.all_gather(w_out, "fsdp", axis=0, tiled=True),
        NT,
        preferred_element_type=jnp.float32,
    ).astype(jnp.bfloat16)
    all_keys = lax.all_gather(key_rows, "rows", axis=1, tiled=True)
    all_values = lax.all_gather(value_rows, "rows", axis=1, tiled=True)
    length = all_keys.shape[1]

    def product(spec, a, b):
        return jnp.einsum(spec, a, b, preferred_element_type=jnp.float32)

    def attend(inputs):
        queries, keys, values, grads = inputs
        probs = jax.nn.softmax(product("qhd,khd->hqk", queries, keys) * factor, axis=-1)
        low = probs.astype(jnp.bfloat16)
        attended = product("hqk,khd->qhd", low, values)
        value_part = product("hqk,qhd->khd", low, grads)
        grad_probs = product("qhd,khd->hqk", grads, values)
        centre = jnp.sum(probs * grad_probs, axis=-1, keepdims=True)
        grad_scores = (probs * (grad_probs - centre)).astype(jnp.bfloat16)
        grad_query = product("hqk,khd->qhd", grad_scores, keys) * factor
        key_part = product("hqk,qhd->khd", grad_scores, queries) * factor
        return (
            attended.astype(jnp.bfloat16),
            grad_query.astype(jnp.bfloat16),
            key_part.astype(jnp.bfloat16),
            value_part.astype(jnp.bfloat16),
        )

    attended, grad_query, key_part, value_part = lax.map(
        attend,
        (
            split(query_rows[0], tokens),
            split(all_keys[0], length),
            split(all_values[0], length),
            split(grad_attn, tokens),
        ),
    )

    def scatter(part):
        part = join(part, length).reshape(1, length, width)
        return lax.psum_scatter(part, "rows", scatter_dimension=1, tiled=True)

    term = lax.dot_general(
        join(attended, tokens),
        grad_flat,
        (((0,), (0,)), ((), ())),
        preferred_element_type=jnp.float32,
    ).astype(jnp.bfloat16)
    share = lax.psum_scatter(term, "fsdp", scatter_dimension=0, tiled=True)
    grad_w_out = lax.psum(share, "rows").astype(jnp.float32)
    return (
        join(grad_query, tokens).reshape(1, tokens, width),
        scatter(key_part),
        scatter(value_part),
        grad_w_out,
    )


def solution(mesh):
    fsdp, rows = mesh.shape["fsdp"], mesh.shape["rows"]

    def local(query_rows, key_rows, value_rows, grad_out, w_out):
        heads = query_rows.shape[2] // HDIM
        if rows == 4 and fsdp == 2 * rows and heads % rows == 0:
            plan = functools.partial(by_heads, fsdp, rows)
        else:
            plan = by_tokens
        return plan(query_rows, key_rows, value_rows, grad_out, w_out)

    tokens = P("fsdp", "rows", None)
    return jax.shard_map(
        local,
        mesh=mesh,
        in_specs=(tokens, tokens, tokens, tokens, P("fsdp", None)),
        out_specs=(tokens, tokens, tokens, P("fsdp", None)),
        check_vma=False,
    )
```

```python
import functools
import math

import jax
import jax.numpy as jnp
from jax import lax
from jax.experimental import pallas as pl
from jax.experimental.pallas import tpu as pltpu
from jax.sharding import PartitionSpec as P


HDIM = 128


NT = (((1,), (1,)), ((), ()))
NN = (((1,), (0,)), ((), ()))


def dot(a, b, dims=NN):
    return lax.dot_general(a, b, dims, preferred_element_type=jnp.float32)


def whole(shape):
    return pl.BlockSpec(shape, lambda *_: (0,) * len(shape))


def cost(flops, moved, exps=0):
    return pl.CostEstimate(flops=flops, bytes_accessed=moved, transcendentals=exps)


def pack(place, query, key, value, rows):
    tokens, width = query.shape[1], query.shape[2] // rows

    def body(place_ref, *refs):
        ins, outs, (held, sems) = refs[:3], refs[3:-2], refs[-2:]
        moves = []
        for slot in (*range(1, rows), 0):
            start = pl.multiple_of((place_ref[0] ^ slot) * width, HDIM)
            for at in range(3):
                box = held.at[slot, at]
                moves.append(
                    (
                        pltpu.make_async_copy(
                            ins[at].at[0, :, pl.ds(start, width)], box, sems.at[0, slot, at]
                        ),
                        pltpu.make_async_copy(box, outs[slot].at[at], sems.at[1, slot, at]),
                    )
                )
        run(moves)

    shape = (3, tokens, width)
    return pl.pallas_call(
        body,
        grid_spec=pltpu.PrefetchScalarGridSpec(
            num_scalar_prefetch=1,
            grid=(1,),
            in_specs=[pl.BlockSpec(memory_space=pltpu.HBM)] * 3,
            out_specs=[pl.BlockSpec(memory_space=pltpu.HBM)] * rows,
            scratch_shapes=[
                pltpu.VMEM((rows, *shape), query.dtype),
                pltpu.SemaphoreType.DMA((2, rows, 3)),
            ],
        ),
        out_shape=[jax.ShapeDtypeStruct(shape, query.dtype)] * rows,
        cost_estimate=cost(0, 12 * query.size),
        name="pack",
    )(place, query, key, value)


def run(moves):
    for fetch, _ in moves:
        fetch.start()
    for fetch, store in moves:
        fetch.wait()
        store.start()
    for _, store in moves:
        store.wait()


def finish(place, parts, pieces):
    calls, rows, chunks = len(parts), len(parts[0]), len(pieces)
    tokens = parts[0][0].shape[1]
    widths = [part[0].shape[2] for part in parts]
    starts = [sum(widths[:at]) for at in range(calls + 1)]
    width = starts[-1]
    piece, wide = pieces[0][0].shape

    def body(place_ref, *refs):
        ins, terms = refs[: calls * rows], refs[calls * rows : (calls + chunks) * rows]
        outs, total = refs[(calls + chunks) * rows :][:3], refs[(calls + chunks) * rows + 3]
        held, low, high, sems, term_sems = refs[-5:]
        moves, sums = [], []
        for call in range(calls):
            for slot in range(rows):
                start = (place_ref[0] ^ slot) * width + starts[call]
                start = pl.multiple_of(start, HDIM)
                for at in range(3):
                    box = held.at[slot, at, :, starts[call] : starts[call + 1]]
                    fetch = pltpu.make_async_copy(
                        ins[call * rows + slot].at[at], box, sems.at[0, call, slot, at]
                    )
                    store = pltpu.make_async_copy(
                        box,
                        outs[at].at[0, :, pl.ds(start, widths[call])],
                        sems.at[1, call, slot, at],
                    )
                    moves.append((fetch, store))
        for chunk in range(chunks):
            for slot in range(rows):
                start = pl.multiple_of((place_ref[0] ^ slot) * piece, 16)
                fetch = pltpu.make_async_copy(
                    terms[chunk * rows + slot], low.at[chunk, slot], term_sems.at[0, chunk, slot]
                )
                store = pltpu.make_async_copy(
                    high.at[chunk, slot],
                    total.at[pl.ds(start, piece), chunk * wide : (chunk + 1) * wide],
                    term_sems.at[1, chunk, slot],
                )
                sums.append((chunk, slot, fetch, store))
        for _, _, fetch, _ in sums:
            fetch.start()
        for fetch, _ in moves:
            fetch.start()
        for chunk, slot, fetch, store in sums:
            fetch.wait()
            high[chunk, slot] = low[chunk, slot].astype(jnp.float32)
            store.start()
        for fetch, store in moves:
            fetch.wait()
            store.start()
        for _, _, _, store in sums:
            store.wait()
        for _, store in moves:
            store.wait()

    full = jax.ShapeDtypeStruct((1, tokens, width * rows), parts[0][0].dtype)
    return pl.pallas_call(
        body,
        grid_spec=pltpu.PrefetchScalarGridSpec(
            num_scalar_prefetch=1,
            grid=(1,),
            in_specs=[pl.BlockSpec(memory_space=pltpu.HBM)] * ((calls + chunks) * rows),
            out_specs=[pl.BlockSpec(memory_space=pltpu.HBM)] * 4,
            scratch_shapes=[
                pltpu.VMEM((rows, 3, tokens, width), parts[0][0].dtype),
                pltpu.VMEM((chunks, rows, piece, wide), pieces[0][0].dtype),
                pltpu.VMEM((chunks, rows, piece, wide), jnp.float32),
                pltpu.SemaphoreType.DMA((2, calls, rows, 3)),
                pltpu.SemaphoreType.DMA((2, chunks, rows)),
            ],
        ),
        out_shape=[full] * 3 + [jax.ShapeDtypeStruct((rows * piece, chunks * wide), jnp.float32)],
        cost_estimate=cost(0, 12 * tokens * width * rows + 6 * rows * piece * chunks * wide),
        name="finish",
    )(place, *(block for part in (*parts, *pieces) for block in part))


def forward(parts):
    rows = len(parts)
    _, tokens, width = parts[0].shape
    length, heads = rows * tokens, width // HDIM
    scale = math.log2(math.e) / math.sqrt(HDIM)

    def body(*refs):
        ins, (probs_ref, attended_ref) = refs[:rows], refs[rows:]
        keys = jnp.concatenate([ref[1] for ref in ins], axis=0)
        values = jnp.concatenate([ref[2] for ref in ins], axis=0).T
        for slot in range(rows):
            across = slice(slot * tokens, (slot + 1) * tokens)
            scores = dot(keys, ins[slot][0], NT)
            top = jnp.max(scores, axis=0, keepdims=True)
            powers = jnp.exp2((scores - top) * scale)
            total = jnp.sum(powers, axis=0, keepdims=True)
            probs = (powers * (1.0 / total)).astype(jnp.bfloat16)
            probs_ref[0, :, across] = probs
            attended_ref[:, across] = dot(values, probs).astype(jnp.bfloat16)

    part = pl.BlockSpec((3, tokens, HDIM), lambda h: (0, 0, h))
    return pl.pallas_call(
        body,
        grid=(heads,),
        in_specs=[part] * rows,
        out_specs=[
            pl.BlockSpec((1, length, length), lambda h: (h, 0, 0)),
            pl.BlockSpec((HDIM, length), lambda h: (h, 0)),
        ],
        out_shape=[
            jax.ShapeDtypeStruct((heads, length, length), jnp.bfloat16),
            jax.ShapeDtypeStruct((width, length), jnp.bfloat16),
        ],
        cost_estimate=cost(
            8 * heads * length * length * HDIM, 2 * heads * length * length, heads * length * length
        ),
        name="forward",
    )(*parts)


def backward(parts, probs, grad_attn, first, count):
    rows = len(parts)
    tokens = parts[0].shape[1]
    length = rows * tokens
    factor = 1.0 / math.sqrt(HDIM)

    def body(*refs):
        ins, (probs_ref, grad_ref) = refs[:rows], refs[rows : rows + 2]
        outs, scores_ref = refs[rows + 2 : -1], refs[-1]
        queries = jnp.concatenate([ref[0] for ref in ins], axis=0)
        keys = jnp.concatenate([ref[1] for ref in ins], axis=0).T
        values = jnp.concatenate([ref[2] for ref in ins], axis=0)
        for slot in range(rows):
            across = slice(slot * tokens, (slot + 1) * tokens)
            probs = probs_ref[0, :, across].astype(jnp.float32)
            terms = probs * dot(values, grad_ref[:, across])
            centre = jnp.sum(terms, axis=0, keepdims=True)
            scores_ref[:, across] = (terms - probs * centre).astype(jnp.bfloat16)
        scores = scores_ref[...]
        grad_query = (dot(keys, scores) * factor).T
        grad_key = dot(scores, queries) * factor
        grad_value = dot(probs_ref[0], grad_ref[...], NT)
        for slot in range(rows):
            down = slice(slot * tokens, (slot + 1) * tokens)
            outs[slot][0] = grad_query[down].astype(jnp.bfloat16)
            outs[slot][1] = grad_key[down].astype(jnp.bfloat16)
            outs[slot][2] = grad_value[down].astype(jnp.bfloat16)

    part = pl.BlockSpec((3, tokens, HDIM), lambda i: (0, 0, first + i))
    shape = (3, tokens, count * HDIM)
    return pl.pallas_call(
        body,
        grid=(count,),
        in_specs=[part] * rows
        + [
            pl.BlockSpec((1, length, length), lambda i: (first + i, 0, 0)),
            pl.BlockSpec((HDIM, length), lambda i: (first + i, 0)),
        ],
        out_specs=[pl.BlockSpec((3, tokens, HDIM), lambda i: (0, 0, i))] * rows,
        out_shape=[jax.ShapeDtypeStruct(shape, jnp.bfloat16)] * rows,
        scratch_shapes=[pltpu.VMEM((length, length), jnp.bfloat16)],
        cost_estimate=cost(8 * count * length * length * HDIM, 2 * count * length * length),
        name="backward",
    )(*parts, probs, grad_attn)


def stacked(refs):
    return jnp.concatenate([ref[...] for ref in refs], axis=0)


def project(place, weights, grads):
    chunks, count = len(grads), len(grads[0])
    half, depth = weights[0].shape
    half = half * len(weights) // 2
    step = grads[0][0].shape[1] // 2

    def body(place_ref, *refs):
        ins, out, total = refs[len(weights) : -2], refs[-2], refs[-1]
        at = pl.program_id(0)
        lines = stacked(refs[: len(weights)])
        for chunk in range(chunks):

            @pl.when(at // 2 == chunk)
            def _():
                term = dot(lines, stacked(ins[chunk * count : (chunk + 1) * count]), NT)
                if chunk:
                    total[...] += term
                else:
                    total[...] = jnp.where(at == 0, 0.0, total[...]) + term

        @pl.when(at == chunks * 2 - 1)
        def _():
            for core in range(2):

                @pl.when(place_ref[2] == core)
                def _():
                    out[core * half : (core + 1) * half] = total[:half].astype(out.dtype)
                    out[(1 - core) * half : (2 - core) * half] = total[half:].astype(out.dtype)

    def block_of(chunk, block):
        return pl.BlockSpec(
            (block.shape[0], step), lambda i, place_ref: (0, jnp.clip(i - chunk * 2, 0, 1))
        )

    shape = (2 * half, sum(block.shape[0] for block in grads[0]))
    return pl.pallas_call(
        body,
        grid_spec=pltpu.PrefetchScalarGridSpec(
            num_scalar_prefetch=1,
            grid=(chunks * 2,),
            in_specs=[
                pl.BlockSpec((part.shape[0], step), lambda i, place_ref: (0, i)) for part in weights
            ]
            + [block_of(chunk, block) for chunk in range(chunks) for block in grads[chunk]],
            out_specs=whole(shape),
            scratch_shapes=[pltpu.VMEM(shape, jnp.float32)],
        ),
        out_shape=jax.ShapeDtypeStruct(shape, jnp.bfloat16),
        cost_estimate=cost(2 * shape[0] * shape[1] * depth, 2 * depth * (shape[0] + shape[1])),
        name="project",
    )(place, *weights, *(block for chunk in grads for block in chunk))


def weight_terms(place, attended, grads, rows):
    width, length = attended.shape
    step = grads[0].shape[1] // 2
    piece = width // 2 // rows

    def body(place_ref, attended_ref, *refs):
        ins, (keep, give) = refs[:-2], refs[-2:]
        term = dot(attended_ref[...], stacked(ins)).astype(jnp.bfloat16)
        row, core = place_ref[0], place_ref[2]
        for side in range(2):
            for out, mine in ((keep, core == side), (give, core != side)):

                @pl.when(mine)
                def _():
                    for at in range(rows):
                        start = (side * rows + at) * piece
                        out[at ^ row] = term[start : start + piece]

    shape = jax.ShapeDtypeStruct((rows, piece, 2 * step), jnp.bfloat16)
    spec = pl.BlockSpec((rows, piece, step), lambda i, place_ref: (0, 0, i))
    return pl.pallas_call(
        body,
        grid_spec=pltpu.PrefetchScalarGridSpec(
            num_scalar_prefetch=1,
            grid=(2,),
            in_specs=[whole((width, length))]
            + [pl.BlockSpec((block.shape[0], step), lambda i, place_ref: (0, i)) for block in grads],
            out_specs=[spec] * 2,
        ),
        out_shape=[shape] * 2,
        cost_estimate=cost(4 * width * length * step, 2 * (width * length + 2 * length * step)),
        name="weight_terms",
    )(place, attended, *grads)


def after(value, *done):
    return lax.optimization_barrier((value, done))[0]


def onward(planes, hop, z, c, r):
    to = z + 1 if z > r else z - 1
    return (to, c, r) if abs(z - r) == hop and 0 <= to < planes else None


def by_heads(fsdp, rows, query_rows, key_rows, value_rows, grad_out, w_out):
    planes = fsdp // 2
    row = lax.axis_index("rows")
    member = lax.axis_index("fsdp")
    plane, core = member // 2, member % 2
    place = jnp.stack([row, plane, core]).astype(jnp.int32)

    def send(array, target):
        pairs = []
        for z in range(planes):
            for c in range(2):
                for r in range(rows):
                    to = target(z, c, r)
                    if to is not None:
                        pairs.append(((z * 2 + c) * rows + r, (to[0] * 2 + to[1]) * rows + to[2]))
        return lax.ppermute(array, ("fsdp", "rows"), pairs)

    def to_row(array, slot):
        return send(array, lambda z, c, r: (z, c, r ^ slot))

    def to_core(array):
        return send(array, lambda z, c, r: (z, 1 - c, r))

    def to_plane(array, ahead):
        return send(array, lambda z, c, r: ((z + ahead) % planes, c, r))

    grad_flat = grad_out[0]
    wide = grad_flat.shape[1] // 2

    def gather(chunk, *done):
        by_x, by_y = to_row(chunk, 1), to_row(chunk, 2)
        by_x, by_y = after((by_x, by_y), *done)
        cut = chunk.shape[0] // 2
        upper, lower = by_x[:cut], by_y[cut:]
        upper = to_row(upper, 2)
        lower = to_row(lower, 1)
        return [chunk, by_x, by_y, upper, lower]

    grads = [gather(grad_flat[:, :wide])]

    away = jnp.abs(plane - row)
    cut = w_out.shape[0] // 2

    def leave(lines):
        above = send(lines, lambda z, c, r: (z + 1, c, r) if z == r and z + 1 < planes else None)
        below = send(lines, lambda z, c, r: (z - 1, c, r) if z == r and z > 0 else None)
        return jnp.where(plane > row, above, below)

    def go_on(hop, lines):
        return send(lines, functools.partial(onward, planes, hop))

    first = [w_out[:cut]]
    first.append(leave(first[0]))
    first.append(go_on(1, first[1]))
    second = [w_out[cut:]]
    second.append(leave(after(second[0], first[1])))
    first.append(go_on(2, first[2]))
    second.append(go_on(1, second[1]))

    packed = pack(place, query_rows, key_rows, value_rows, rows)
    parts = [packed[0]] + [to_row(packed[slot], slot) for slot in range(1, rows)]
    probs, attended = forward(parts)
    second.append(go_on(2, after(second[2], attended)))

    def mine(stages):
        here = stages[0]
        for hop in range(1, planes):
            here = jnp.where(away == hop, stages[hop], here)
        return here

    weights = [mine(first), mine(second)]
    weights += [to_core(part) for part in weights]
    grads.append(gather(after(grad_flat[:, wide:], parts), attended))

    def reduce_cores(attended, chunk):
        keep, give = weight_terms(place, attended, chunk, rows)
        return keep, to_core(give)

    def spread(keep, got):
        both = [
            (keep[slot].astype(jnp.float32) + got[slot].astype(jnp.float32)).astype(jnp.bfloat16)
            for slot in range(rows)
        ]
        return [both[0]] + [to_row(both[slot], slot) for slot in range(1, rows)]

    def reduce_planes(blocks):
        stack = jnp.stack(blocks)

        def block_of(ahead):
            return lax.dynamic_index_in_dim(stack, ((plane + ahead) % planes) ^ row, 0, False)

        return block_of(0), [to_plane(block_of(ahead), ahead) for ahead in range(1, planes)]

    def collect(total, got):
        for part in got:
            total = total.astype(jnp.float32) + part.astype(jnp.float32)
        total = total.astype(jnp.bfloat16)
        return [total] + [to_row(total, slot) for slot in range(1, rows)]

    blocks = spread(*reduce_cores(attended, grads[0]))
    late = reduce_cores(attended, grads[1])
    early = reduce_planes(after(blocks, late[0]))
    grad_attn = project(place, weights, grads)
    heads = probs.shape[0]
    blocks = spread(*after(late, early[0]))
    sent = [backward(parts, probs, grad_attn, 0, 1)]
    late = reduce_planes(after(blocks, sent[0][0]))
    sent.append(backward(parts, after(probs, late[0]), grad_attn, 1, heads - 1))
    back = [
        [message[0]]
        + [to_row(message[slot], slot) for slot in range(1, rows)]
        for message in sent
    ]
    pieces = [collect(*after(early, sent[0][0])), collect(*after(late, sent[1][0]))]
    return tuple(finish(place, back, pieces))


def by_tokens(query_rows, key_rows, value_rows, grad_out, w_out):
    tokens, width = query_rows.shape[1:]
    heads = width // HDIM
    factor = 1.0 / math.sqrt(HDIM)
    grad_flat = grad_out[0]
    groups = math.gcd(heads, 3)

    def split(array, count):
        return jnp.moveaxis(array.reshape(count, groups, heads // groups, HDIM), 1, 0)

    def join(array, count):
        return jnp.moveaxis(array, 0, 1).reshape(count, width)

    grad_attn = lax.dot_general(
        grad_flat,
        lax.all_gather(w_out, "fsdp", axis=0, tiled=True),
        NT,
        preferred_element_type=jnp.float32,
    ).astype(jnp.bfloat16)
    all_keys = lax.all_gather(key_rows, "rows", axis=1, tiled=True)
    all_values = lax.all_gather(value_rows, "rows", axis=1, tiled=True)
    length = all_keys.shape[1]

    def product(spec, a, b):
        return jnp.einsum(spec, a, b, preferred_element_type=jnp.float32)

    def attend(inputs):
        queries, keys, values, grads = inputs
        probs = jax.nn.softmax(product("qhd,khd->hqk", queries, keys) * factor, axis=-1)
        low = probs.astype(jnp.bfloat16)
        attended = product("hqk,khd->qhd", low, values)
        value_part = product("hqk,qhd->khd", low, grads)
        grad_probs = product("qhd,khd->hqk", grads, values)
        centre = jnp.sum(probs * grad_probs, axis=-1, keepdims=True)
        grad_scores = (probs * (grad_probs - centre)).astype(jnp.bfloat16)
        grad_query = product("hqk,khd->qhd", grad_scores, keys) * factor
        key_part = product("hqk,qhd->khd", grad_scores, queries) * factor
        return (
            attended.astype(jnp.bfloat16),
            grad_query.astype(jnp.bfloat16),
            key_part.astype(jnp.bfloat16),
            value_part.astype(jnp.bfloat16),
        )

    attended, grad_query, key_part, value_part = lax.map(
        attend,
        (
            split(query_rows[0], tokens),
            split(all_keys[0], length),
            split(all_values[0], length),
            split(grad_attn, tokens),
        ),
    )

    def scatter(part):
        part = join(part, length).reshape(1, length, width)
        return lax.psum_scatter(part, "rows", scatter_dimension=1, tiled=True)

    term = lax.dot_general(
        join(attended, tokens),
        grad_flat,
        (((0,), (0,)), ((), ())),
        preferred_element_type=jnp.float32,
    ).astype(jnp.bfloat16)
    share = lax.psum_scatter(term, "fsdp", scatter_dimension=0, tiled=True)
    grad_w_out = lax.psum(share, "rows").astype(jnp.float32)
    return (
        join(grad_query, tokens).reshape(1, tokens, width),
        scatter(key_part),
        scatter(value_part),
        grad_w_out,
    )


def solution(mesh):
    fsdp, rows = mesh.shape["fsdp"], mesh.shape["rows"]

    def local(query_rows, key_rows, value_rows, grad_out, w_out):
        heads = query_rows.shape[2] // HDIM
        if rows == 4 and fsdp == 2 * rows and heads % rows == 0:
            plan = functools.partial(by_heads, fsdp, rows)
        else:
            plan = by_tokens
        return plan(query_rows, key_rows, value_rows, grad_out, w_out)

    tokens = P("fsdp", "rows", None)
    return jax.shard_map(
        local,
        mesh=mesh,
        in_specs=(tokens, tokens, tokens, tokens, P("fsdp", None)),
        out_specs=(tokens, tokens, tokens, P("fsdp", None)),
        check_vma=False,
    )
```

```python
import functools
import math

import jax
import jax.numpy as jnp
from jax import lax
from jax.experimental import pallas as pl
from jax.experimental.pallas import tpu as pltpu
from jax.sharding import PartitionSpec as P


HDIM = 128


NT = (((1,), (1,)), ((), ()))
NN = (((1,), (0,)), ((), ()))


def dot(a, b, dims=NN):
    return lax.dot_general(a, b, dims, preferred_element_type=jnp.float32)


def whole(shape):
    return pl.BlockSpec(shape, lambda *_: (0,) * len(shape))


def cost(flops, moved, exps=0):
    return pl.CostEstimate(flops=flops, bytes_accessed=moved, transcendentals=exps)


def pack(place, query, key, value, rows):
    tokens, width = query.shape[1], query.shape[2] // rows

    def body(place_ref, *refs):
        ins, outs, (held, sems) = refs[:3], refs[3:-2], refs[-2:]
        moves = []
        for slot in (*range(1, rows), 0):
            start = pl.multiple_of((place_ref[0] ^ slot) * width, HDIM)
            for at in range(3):
                box = held.at[slot, at]
                moves.append(
                    (
                        pltpu.make_async_copy(
                            ins[at].at[0, :, pl.ds(start, width)], box, sems.at[0, slot, at]
                        ),
                        pltpu.make_async_copy(box, outs[slot].at[at], sems.at[1, slot, at]),
                    )
                )
        run(moves)

    shape = (3, tokens, width)
    return pl.pallas_call(
        body,
        grid_spec=pltpu.PrefetchScalarGridSpec(
            num_scalar_prefetch=1,
            grid=(1,),
            in_specs=[pl.BlockSpec(memory_space=pltpu.HBM)] * 3,
            out_specs=[pl.BlockSpec(memory_space=pltpu.HBM)] * rows,
            scratch_shapes=[
                pltpu.VMEM((rows, *shape), query.dtype),
                pltpu.SemaphoreType.DMA((2, rows, 3)),
            ],
        ),
        out_shape=[jax.ShapeDtypeStruct(shape, query.dtype)] * rows,
        cost_estimate=cost(0, 12 * query.size),
        name="pack",
    )(place, query, key, value)


def run(moves):
    for fetch, _ in moves:
        fetch.start()
    for fetch, store in moves:
        fetch.wait()
        store.start()
    for _, store in moves:
        store.wait()


def finish(place, parts, pieces):
    calls, rows, chunks = len(parts), len(parts[0]), len(pieces)
    tokens = parts[0][0].shape[1]
    widths = [part[0].shape[2] for part in parts]
    starts = [sum(widths[:at]) for at in range(calls + 1)]
    width = starts[-1]
    piece, wide = pieces[0][0].shape

    def body(place_ref, *refs):
        ins, terms = refs[: calls * rows], refs[calls * rows : (calls + chunks) * rows]
        outs, total = refs[(calls + chunks) * rows :][:3], refs[(calls + chunks) * rows + 3]
        held, low, high, sems, term_sems = refs[-5:]
        moves, sums = [], []
        for call in range(calls):
            for slot in range(rows):
                start = (place_ref[0] ^ slot) * width + starts[call]
                start = pl.multiple_of(start, HDIM)
                for at in range(3):
                    box = held.at[slot, at, :, starts[call] : starts[call + 1]]
                    fetch = pltpu.make_async_copy(
                        ins[call * rows + slot].at[at], box, sems.at[0, call, slot, at]
                    )
                    store = pltpu.make_async_copy(
                        box,
                        outs[at].at[0, :, pl.ds(start, widths[call])],
                        sems.at[1, call, slot, at],
                    )
                    moves.append((fetch, store))
        for chunk in range(chunks):
            for slot in range(rows):
                start = pl.multiple_of((place_ref[0] ^ slot) * piece, 16)
                fetch = pltpu.make_async_copy(
                    terms[chunk * rows + slot], low.at[chunk, slot], term_sems.at[0, chunk, slot]
                )
                store = pltpu.make_async_copy(
                    high.at[chunk, slot],
                    total.at[pl.ds(start, piece), chunk * wide : (chunk + 1) * wide],
                    term_sems.at[1, chunk, slot],
                )
                sums.append((chunk, slot, fetch, store))
        for _, _, fetch, _ in sums:
            fetch.start()
        for fetch, _ in moves:
            fetch.start()
        for chunk, slot, fetch, store in sums:
            fetch.wait()
            high[chunk, slot] = low[chunk, slot].astype(jnp.float32)
            store.start()
        for fetch, store in moves:
            fetch.wait()
            store.start()
        for _, _, _, store in sums:
            store.wait()
        for _, store in moves:
            store.wait()

    full = jax.ShapeDtypeStruct((1, tokens, width * rows), parts[0][0].dtype)
    return pl.pallas_call(
        body,
        grid_spec=pltpu.PrefetchScalarGridSpec(
            num_scalar_prefetch=1,
            grid=(1,),
            in_specs=[pl.BlockSpec(memory_space=pltpu.HBM)] * ((calls + chunks) * rows),
            out_specs=[pl.BlockSpec(memory_space=pltpu.HBM)] * 4,
            scratch_shapes=[
                pltpu.VMEM((rows, 3, tokens, width), parts[0][0].dtype),
                pltpu.VMEM((chunks, rows, piece, wide), pieces[0][0].dtype),
                pltpu.VMEM((chunks, rows, piece, wide), jnp.float32),
                pltpu.SemaphoreType.DMA((2, calls, rows, 3)),
                pltpu.SemaphoreType.DMA((2, chunks, rows)),
            ],
        ),
        out_shape=[full] * 3 + [jax.ShapeDtypeStruct((rows * piece, chunks * wide), jnp.float32)],
        cost_estimate=cost(0, 12 * tokens * width * rows + 6 * rows * piece * chunks * wide),
        name="finish",
    )(place, *(block for part in (*parts, *pieces) for block in part))


def forward(parts):
    rows = len(parts)
    _, tokens, width = parts[0].shape
    length, heads = rows * tokens, width // HDIM
    scale = math.log2(math.e) / math.sqrt(HDIM)

    def body(*refs):
        ins, (probs_ref, attended_ref) = refs[:rows], refs[rows:]
        keys = jnp.concatenate([ref[1] for ref in ins], axis=0)
        values = jnp.concatenate([ref[2] for ref in ins], axis=0).T
        for slot in range(rows):
            across = slice(slot * tokens, (slot + 1) * tokens)
            scores = dot(keys, ins[slot][0], NT)
            top = jnp.max(scores, axis=0, keepdims=True)
            powers = jnp.exp2((scores - top) * scale)
            total = jnp.sum(powers, axis=0, keepdims=True)
            probs = (powers * (1.0 / total)).astype(jnp.bfloat16)
            probs_ref[0, :, across] = probs
            attended_ref[:, across] = dot(values, probs).astype(jnp.bfloat16)

    part = pl.BlockSpec((3, tokens, HDIM), lambda h: (0, 0, h))
    return pl.pallas_call(
        body,
        grid=(heads,),
        in_specs=[part] * rows,
        out_specs=[
            pl.BlockSpec((1, length, length), lambda h: (h, 0, 0)),
            pl.BlockSpec((HDIM, length), lambda h: (h, 0)),
        ],
        out_shape=[
            jax.ShapeDtypeStruct((heads, length, length), jnp.bfloat16),
            jax.ShapeDtypeStruct((width, length), jnp.bfloat16),
        ],
        cost_estimate=cost(
            8 * heads * length * length * HDIM, 2 * heads * length * length, heads * length * length
        ),
        name="forward",
    )(*parts)


def backward(parts, probs, grad_attn, first, count):
    rows = len(parts)
    tokens = parts[0].shape[1]
    length = rows * tokens
    factor = 1.0 / math.sqrt(HDIM)

    def body(*refs):
        ins, (probs_ref, grad_ref) = refs[:rows], refs[rows : rows + 2]
        outs, scores_ref = refs[rows + 2 : -1], refs[-1]
        queries = jnp.concatenate([ref[0] for ref in ins], axis=0)
        keys = jnp.concatenate([ref[1] for ref in ins], axis=0).T
        values = jnp.concatenate([ref[2] for ref in ins], axis=0)
        for slot in range(rows):
            across = slice(slot * tokens, (slot + 1) * tokens)
            probs = probs_ref[0, :, across].astype(jnp.float32)
            terms = probs * dot(values, grad_ref[:, across])
            centre = jnp.sum(terms, axis=0, keepdims=True)
            scores_ref[:, across] = (terms - probs * centre).astype(jnp.bfloat16)
        scores = scores_ref[...]
        grad_query = (dot(keys, scores) * factor).T
        grad_key = dot(scores, queries) * factor
        grad_value = dot(probs_ref[0], grad_ref[...], NT)
        for slot in range(rows):
            down = slice(slot * tokens, (slot + 1) * tokens)
            outs[slot][0] = grad_query[down].astype(jnp.bfloat16)
            outs[slot][1] = grad_key[down].astype(jnp.bfloat16)
            outs[slot][2] = grad_value[down].astype(jnp.bfloat16)

    part = pl.BlockSpec((3, tokens, HDIM), lambda i: (0, 0, first + i))
    shape = (3, tokens, count * HDIM)
    return pl.pallas_call(
        body,
        grid=(count,),
        in_specs=[part] * rows
        + [
            pl.BlockSpec((1, length, length), lambda i: (first + i, 0, 0)),
            pl.BlockSpec((HDIM, length), lambda i: (first + i, 0)),
        ],
        out_specs=[pl.BlockSpec((3, tokens, HDIM), lambda i: (0, 0, i))] * rows,
        out_shape=[jax.ShapeDtypeStruct(shape, jnp.bfloat16)] * rows,
        scratch_shapes=[pltpu.VMEM((length, length), jnp.bfloat16)],
        cost_estimate=cost(8 * count * length * length * HDIM, 2 * count * length * length),
        name="backward",
    )(*parts, probs, grad_attn)


def stacked(refs):
    return jnp.concatenate([ref[...] for ref in refs], axis=0)


def project(place, weights, grads, chunk, before=None):
    half = sum(part.shape[0] for part in weights) // 2
    step = grads[0].shape[1] // 2
    parts, count = len(weights), len(grads)
    shape = (2 * half, sum(block.shape[0] for block in grads))

    def body(place_ref, *refs):
        ins = refs[parts : parts + count]
        out, total = refs[-2:]
        at = pl.program_id(0)
        start = pl.multiple_of((2 * chunk + at) * step, HDIM)
        lines = jnp.concatenate([ref[:, pl.ds(start, step)] for ref in refs[:parts]], axis=0)
        term = dot(lines, stacked(ins), NT)

        @pl.when(at == 0)
        def _():
            total[...] = term

        @pl.when(at == 1)
        def _():
            if before is None:
                out[...] = total[...] + term
                return
            whole_sum = (refs[parts + count][...] + total[...] + term).astype(out.dtype)
            for core in range(2):

                @pl.when(place_ref[2] == core)
                def _():
                    out[core * half : (core + 1) * half] = whole_sum[:half]
                    out[(1 - core) * half : (2 - core) * half] = whole_sum[half:]

    more = [] if before is None else [before]
    return pl.pallas_call(
        body,
        grid_spec=pltpu.PrefetchScalarGridSpec(
            num_scalar_prefetch=1,
            grid=(2,),
            in_specs=[pl.BlockSpec(memory_space=pltpu.VMEM)] * parts
            + [pl.BlockSpec((block.shape[0], step), lambda i, place_ref: (0, i)) for block in grads]
            + [whole(shape) for _ in more],
            out_specs=whole(shape),
            scratch_shapes=[pltpu.VMEM(shape, jnp.float32)],
        ),
        out_shape=jax.ShapeDtypeStruct(shape, jnp.bfloat16 if more else jnp.float32),
        cost_estimate=cost(4 * shape[0] * shape[1] * step, 4 * step * (shape[0] + shape[1])),
        name="project",
    )(place, *weights, *grads, *more)


def weight_terms(place, attended, grads, rows):
    width, length = attended.shape
    step = grads[0].shape[1] // 2
    piece = width // 2 // rows

    def body(place_ref, attended_ref, *refs):
        ins, (keep, give) = refs[:-2], refs[-2:]
        term = dot(attended_ref[...], stacked(ins)).astype(jnp.bfloat16)
        row, core = place_ref[0], place_ref[2]
        for side in range(2):
            for out, mine in ((keep, core == side), (give, core != side)):

                @pl.when(mine)
                def _():
                    for at in range(rows):
                        start = (side * rows + at) * piece
                        out[at ^ row] = term[start : start + piece]

    shape = jax.ShapeDtypeStruct((rows, piece, 2 * step), jnp.bfloat16)
    spec = pl.BlockSpec((rows, piece, step), lambda i, place_ref: (0, 0, i))
    return pl.pallas_call(
        body,
        grid_spec=pltpu.PrefetchScalarGridSpec(
            num_scalar_prefetch=1,
            grid=(2,),
            in_specs=[whole((width, length))]
            + [pl.BlockSpec((block.shape[0], step), lambda i, place_ref: (0, i)) for block in grads],
            out_specs=[spec] * 2,
        ),
        out_shape=[shape] * 2,
        cost_estimate=cost(4 * width * length * step, 2 * (width * length + 2 * length * step)),
        name="weight_terms",
    )(place, attended, *grads)


def after(value, *done):
    return lax.optimization_barrier((value, done))[0]


def onward(planes, hop, z, c, r):
    to = z + 1 if z > r else z - 1
    return (to, c, r) if abs(z - r) == hop and 0 <= to < planes else None


def by_heads(fsdp, rows, query_rows, key_rows, value_rows, grad_out, w_out):
    planes = fsdp // 2
    row = lax.axis_index("rows")
    member = lax.axis_index("fsdp")
    plane, core = member // 2, member % 2
    place = jnp.stack([row, plane, core]).astype(jnp.int32)

    def send(array, target):
        pairs = []
        for z in range(planes):
            for c in range(2):
                for r in range(rows):
                    to = target(z, c, r)
                    if to is not None:
                        pairs.append(((z * 2 + c) * rows + r, (to[0] * 2 + to[1]) * rows + to[2]))
        return lax.ppermute(array, ("fsdp", "rows"), pairs)

    def to_row(array, slot):
        return send(array, lambda z, c, r: (z, c, r ^ slot))

    def to_core(array):
        return send(array, lambda z, c, r: (z, 1 - c, r))

    def to_plane(array, turn):
        return send(array, lambda z, c, r: (z ^ turn, c, r))

    grad_flat = grad_out[0]
    wide = grad_flat.shape[1] // 2

    def gather(chunk, *done):
        by_x, by_y = to_row(chunk, 1), to_row(chunk, 2)
        by_x, by_y = after((by_x, by_y), *done)
        cut = chunk.shape[0] // 2
        upper, lower = by_x[:cut], by_y[cut:]
        by_both = [to_row(upper, 2), to_row(lower, 1)]
        return [chunk, by_x, by_y, *by_both], (upper, lower)

    grads = [gather(grad_flat[:, :wide])[0]]

    away = jnp.abs(plane - row)
    cut = w_out.shape[0] // 2

    def leave(lines):
        above = send(lines, lambda z, c, r: (z + 1, c, r) if z == r and z + 1 < planes else None)
        below = send(lines, lambda z, c, r: (z - 1, c, r) if z == r and z > 0 else None)
        return jnp.where(plane > row, above, below)

    def go_on(hop, lines):
        return send(lines, functools.partial(onward, planes, hop))

    first = [w_out[:cut]]
    first.append(leave(first[0]))
    first.append(go_on(1, first[1]))
    second = [w_out[cut:]]
    second.append(leave(after(second[0], first[1])))
    first.append(go_on(2, first[2]))
    second.append(go_on(1, second[1]))

    packed = pack(place, query_rows, key_rows, value_rows, rows)
    parts = [packed[0]] + [to_row(packed[slot], slot) for slot in range(1, rows)]
    probs, attended = forward(parts)
    second.append(go_on(2, after(second[2], attended)))

    def mine(stages):
        here = stages[0]
        for hop in range(1, planes):
            here = jnp.where(away == hop, stages[hop], here)
        return here

    block, handed = gather(after(grad_flat[:, wide:], parts), attended)
    grads.append(block)
    first[-1], second[-1] = after((first[-1], second[-1]), handed)
    weights = [mine(first), mine(second)]
    weights += [to_core(part) for part in weights]

    def reduce_cores(attended, chunk):
        keep, give = weight_terms(place, attended, chunk, rows)
        return keep, to_core(give)

    def spread(keep, got):
        both = [
            (keep[slot].astype(jnp.float32) + got[slot].astype(jnp.float32)).astype(jnp.bfloat16)
            for slot in range(rows)
        ]
        return [both[0]] + [to_row(both[slot], slot) for slot in range(1, rows)]

    def reduce_planes(blocks):
        picked = [
            lax.select_n((plane ^ turn) ^ row, *blocks) for turn in range(planes)
        ]
        return picked[0], [to_plane(picked[turn], turn) for turn in range(1, planes)]

    def collect(total, got):
        for part in got:
            total = total.astype(jnp.float32) + part.astype(jnp.float32)
        total = total.astype(jnp.bfloat16)
        return [total] + [to_row(total, slot) for slot in range(1, rows)]

    blocks = spread(*reduce_cores(attended, grads[0]))
    late = reduce_cores(attended, grads[1])
    early = reduce_planes(after(blocks, late[0]))
    grad_attn = project(place, weights, grads[0], 0)
    grad_attn = project(place, weights, grads[1], 1, grad_attn)
    sent = backward(parts, probs, grad_attn, 0, probs.shape[0])
    back = [sent[0]] + [to_row(sent[slot], slot) for slot in range(1, rows)]
    late = reduce_planes(after(spread(*after(late, early[0])), sent[0]))
    pieces = [collect(*after(early, sent[0])), collect(*late)]
    return tuple(finish(place, [back], pieces))


def by_tokens(query_rows, key_rows, value_rows, grad_out, w_out):
    tokens, width = query_rows.shape[1:]
    heads = width // HDIM
    factor = 1.0 / math.sqrt(HDIM)
    grad_flat = grad_out[0]
    groups = math.gcd(heads, 3)

    def split(array, count):
        return jnp.moveaxis(array.reshape(count, groups, heads // groups, HDIM), 1, 0)

    def join(array, count):
        return jnp.moveaxis(array, 0, 1).reshape(count, width)

    grad_attn = lax.dot_general(
        grad_flat,
        lax.all_gather(w_out, "fsdp", axis=0, tiled=True),
        NT,
        preferred_element_type=jnp.float32,
    ).astype(jnp.bfloat16)
    all_keys = lax.all_gather(key_rows, "rows", axis=1, tiled=True)
    all_values = lax.all_gather(value_rows, "rows", axis=1, tiled=True)
    length = all_keys.shape[1]

    def product(spec, a, b):
        return jnp.einsum(spec, a, b, preferred_element_type=jnp.float32)

    def attend(inputs):
        queries, keys, values, grads = inputs
        probs = jax.nn.softmax(product("qhd,khd->hqk", queries, keys) * factor, axis=-1)
        low = probs.astype(jnp.bfloat16)
        attended = product("hqk,khd->qhd", low, values)
        value_part = product("hqk,qhd->khd", low, grads)
        grad_probs = product("qhd,khd->hqk", grads, values)
        centre = jnp.sum(probs * grad_probs, axis=-1, keepdims=True)
        grad_scores = (probs * (grad_probs - centre)).astype(jnp.bfloat16)
        grad_query = product("hqk,khd->qhd", grad_scores, keys) * factor
        key_part = product("hqk,qhd->khd", grad_scores, queries) * factor
        return (
            attended.astype(jnp.bfloat16),
            grad_query.astype(jnp.bfloat16),
            key_part.astype(jnp.bfloat16),
            value_part.astype(jnp.bfloat16),
        )

    attended, grad_query, key_part, value_part = lax.map(
        attend,
        (
            split(query_rows[0], tokens),
            split(all_keys[0], length),
            split(all_values[0], length),
            split(grad_attn, tokens),
        ),
    )

    def scatter(part):
        part = join(part, length).reshape(1, length, width)
        return lax.psum_scatter(part, "rows", scatter_dimension=1, tiled=True)

    term = lax.dot_general(
        join(attended, tokens),
        grad_flat,
        (((0,), (0,)), ((), ())),
        preferred_element_type=jnp.float32,
    ).astype(jnp.bfloat16)
    share = lax.psum_scatter(term, "fsdp", scatter_dimension=0, tiled=True)
    grad_w_out = lax.psum(share, "rows").astype(jnp.float32)
    return (
        join(grad_query, tokens).reshape(1, tokens, width),
        scatter(key_part),
        scatter(value_part),
        grad_w_out,
    )


def solution(mesh):
    fsdp, rows = mesh.shape["fsdp"], mesh.shape["rows"]

    def local(query_rows, key_rows, value_rows, grad_out, w_out):
        heads = query_rows.shape[2] // HDIM
        if rows == 4 and fsdp == 2 * rows and heads % rows == 0:
            plan = functools.partial(by_heads, fsdp, rows)
        else:
            plan = by_tokens
        return plan(query_rows, key_rows, value_rows, grad_out, w_out)

    tokens = P("fsdp", "rows", None)
    return jax.shard_map(
        local,
        mesh=mesh,
        in_specs=(tokens, tokens, tokens, tokens, P("fsdp", None)),
        out_specs=(tokens, tokens, tokens, P("fsdp", None)),
        check_vma=False,
    )
```

```python
import functools
import math

import jax
import jax.numpy as jnp
from jax import lax
from jax.experimental import pallas as pl
from jax.experimental.pallas import tpu as pltpu
from jax.sharding import PartitionSpec as P


HDIM = 128


NT = (((1,), (1,)), ((), ()))
NN = (((1,), (0,)), ((), ()))


def dot(a, b, dims=NN):
    return lax.dot_general(a, b, dims, preferred_element_type=jnp.float32)


def whole(shape):
    return pl.BlockSpec(shape, lambda *_: (0,) * len(shape))


def cost(flops, moved, exps=0):
    return pl.CostEstimate(flops=flops, bytes_accessed=moved, transcendentals=exps)


def pack(place, query, key, value, rows):
    tokens, width = query.shape[1], query.shape[2] // rows

    def body(place_ref, *refs):
        ins, outs, (held, sems) = refs[:3], refs[3:-2], refs[-2:]
        moves = []
        for slot in (*range(1, rows), 0):
            start = pl.multiple_of((place_ref[0] ^ slot) * width, HDIM)
            for at in range(3):
                box = held.at[slot, at]
                moves.append(
                    (
                        pltpu.make_async_copy(
                            ins[at].at[0, :, pl.ds(start, width)], box, sems.at[0, slot, at]
                        ),
                        pltpu.make_async_copy(box, outs[slot].at[at], sems.at[1, slot, at]),
                    )
                )
        run(moves)

    shape = (3, tokens, width)
    return pl.pallas_call(
        body,
        grid_spec=pltpu.PrefetchScalarGridSpec(
            num_scalar_prefetch=1,
            grid=(1,),
            in_specs=[pl.BlockSpec(memory_space=pltpu.HBM)] * 3,
            out_specs=[pl.BlockSpec(memory_space=pltpu.HBM)] * rows,
            scratch_shapes=[
                pltpu.VMEM((rows, *shape), query.dtype),
                pltpu.SemaphoreType.DMA((2, rows, 3)),
            ],
        ),
        out_shape=[jax.ShapeDtypeStruct(shape, query.dtype)] * rows,
        cost_estimate=cost(0, 12 * query.size),
        name="pack",
    )(place, query, key, value)


def run(moves):
    for fetch, _ in moves:
        fetch.start()
    for fetch, store in moves:
        fetch.wait()
        store.start()
    for _, store in moves:
        store.wait()


def finish(place, parts, pieces):
    calls, rows, chunks = len(parts), len(parts[0]), len(pieces)
    tokens = parts[0][0].shape[1]
    widths = [part[0].shape[2] for part in parts]
    starts = [sum(widths[:at]) for at in range(calls + 1)]
    width = starts[-1]
    piece, wide = pieces[0][0].shape

    def body(place_ref, *refs):
        ins, terms = refs[: calls * rows], refs[calls * rows : (calls + chunks) * rows]
        outs, total = refs[(calls + chunks) * rows :][:3], refs[(calls + chunks) * rows + 3]
        held, low, high, sems, term_sems = refs[-5:]
        moves, sums = [], []
        for call in range(calls):
            for slot in range(rows):
                start = (place_ref[0] ^ slot) * width + starts[call]
                start = pl.multiple_of(start, HDIM)
                for at in range(3):
                    box = held.at[slot, at, :, starts[call] : starts[call + 1]]
                    fetch = pltpu.make_async_copy(
                        ins[call * rows + slot].at[at], box, sems.at[0, call, slot, at]
                    )
                    store = pltpu.make_async_copy(
                        box,
                        outs[at].at[0, :, pl.ds(start, widths[call])],
                        sems.at[1, call, slot, at],
                    )
                    moves.append((fetch, store))
        for chunk in range(chunks):
            for slot in range(rows):
                owner = place_ref[0] ^ slot if chunk else (place_ref[1] - slot) & (rows - 1)
                start = pl.multiple_of(owner * piece, 16)
                fetch = pltpu.make_async_copy(
                    terms[chunk * rows + slot], low.at[chunk, slot], term_sems.at[0, chunk, slot]
                )
                store = pltpu.make_async_copy(
                    high.at[chunk, slot],
                    total.at[pl.ds(start, piece), chunk * wide : (chunk + 1) * wide],
                    term_sems.at[1, chunk, slot],
                )
                sums.append((chunk, slot, fetch, store))
        for _, _, fetch, _ in sums:
            fetch.start()
        for fetch, _ in moves:
            fetch.start()
        for chunk, slot, fetch, store in sums:
            fetch.wait()
            high[chunk, slot] = low[chunk, slot].astype(jnp.float32)
            store.start()
        for fetch, store in moves:
            fetch.wait()
            store.start()
        for _, _, _, store in sums:
            store.wait()
        for _, store in moves:
            store.wait()

    full = jax.ShapeDtypeStruct((1, tokens, width * rows), parts[0][0].dtype)
    return pl.pallas_call(
        body,
        grid_spec=pltpu.PrefetchScalarGridSpec(
            num_scalar_prefetch=1,
            grid=(1,),
            in_specs=[pl.BlockSpec(memory_space=pltpu.HBM)] * ((calls + chunks) * rows),
            out_specs=[pl.BlockSpec(memory_space=pltpu.HBM)] * 4,
            scratch_shapes=[
                pltpu.VMEM((rows, 3, tokens, width), parts[0][0].dtype),
                pltpu.VMEM((chunks, rows, piece, wide), pieces[0][0].dtype),
                pltpu.VMEM((chunks, rows, piece, wide), jnp.float32),
                pltpu.SemaphoreType.DMA((2, calls, rows, 3)),
                pltpu.SemaphoreType.DMA((2, chunks, rows)),
            ],
        ),
        out_shape=[full] * 3 + [jax.ShapeDtypeStruct((rows * piece, chunks * wide), jnp.float32)],
        cost_estimate=cost(0, 12 * tokens * width * rows + 6 * rows * piece * chunks * wide),
        name="finish",
    )(place, *(block for part in (*parts, *pieces) for block in part))


def forward(parts):
    rows = len(parts)
    _, tokens, width = parts[0].shape
    length, heads = rows * tokens, width // HDIM
    scale = math.log2(math.e) / math.sqrt(HDIM)

    def body(*refs):
        ins, (probs_ref, attended_ref) = refs[:rows], refs[rows:]
        keys = jnp.concatenate([ref[1] for ref in ins], axis=0)
        values = jnp.concatenate([ref[2] for ref in ins], axis=0).T
        for slot in range(rows):
            across = slice(slot * tokens, (slot + 1) * tokens)
            scores = dot(keys, ins[slot][0], NT)
            top = jnp.max(scores, axis=0, keepdims=True)
            powers = jnp.exp2((scores - top) * scale)
            total = jnp.sum(powers, axis=0, keepdims=True)
            probs = (powers * (1.0 / total)).astype(jnp.bfloat16)
            probs_ref[0, :, across] = probs
            attended_ref[:, across] = dot(values, probs).astype(jnp.bfloat16)

    part = pl.BlockSpec((3, tokens, HDIM), lambda h: (0, 0, h))
    return pl.pallas_call(
        body,
        grid=(heads,),
        in_specs=[part] * rows,
        out_specs=[
            pl.BlockSpec((1, length, length), lambda h: (h, 0, 0)),
            pl.BlockSpec((HDIM, length), lambda h: (h, 0)),
        ],
        out_shape=[
            jax.ShapeDtypeStruct((heads, length, length), jnp.bfloat16),
            jax.ShapeDtypeStruct((width, length), jnp.bfloat16),
        ],
        cost_estimate=cost(
            8 * heads * length * length * HDIM, 2 * heads * length * length, heads * length * length
        ),
        name="forward",
    )(*parts)


def backward(parts, probs, grad_attn, first, count):
    rows = len(parts)
    tokens = parts[0].shape[1]
    length = rows * tokens
    factor = 1.0 / math.sqrt(HDIM)

    def body(*refs):
        ins, (probs_ref, grad_ref) = refs[:rows], refs[rows : rows + 2]
        outs, scores_ref = refs[rows + 2 : -1], refs[-1]
        queries = jnp.concatenate([ref[0] for ref in ins], axis=0)
        keys = jnp.concatenate([ref[1] for ref in ins], axis=0).T
        values = jnp.concatenate([ref[2] for ref in ins], axis=0)
        for slot in range(rows):
            across = slice(slot * tokens, (slot + 1) * tokens)
            probs = probs_ref[0, :, across].astype(jnp.float32)
            terms = probs * dot(values, grad_ref[:, across])
            centre = jnp.sum(terms, axis=0, keepdims=True)
            scores_ref[:, across] = (terms - probs * centre).astype(jnp.bfloat16)
        scores = scores_ref[...]
        grad_query = (dot(keys, scores) * factor).T
        grad_key = dot(scores, queries) * factor
        grad_value = dot(probs_ref[0], grad_ref[...], NT)
        for slot in range(rows):
            down = slice(slot * tokens, (slot + 1) * tokens)
            outs[slot][0] = grad_query[down].astype(jnp.bfloat16)
            outs[slot][1] = grad_key[down].astype(jnp.bfloat16)
            outs[slot][2] = grad_value[down].astype(jnp.bfloat16)

    part = pl.BlockSpec((3, tokens, HDIM), lambda i: (0, 0, first + i))
    shape = (3, tokens, count * HDIM)
    return pl.pallas_call(
        body,
        grid=(count,),
        in_specs=[part] * rows
        + [
            pl.BlockSpec((1, length, length), lambda i: (first + i, 0, 0)),
            pl.BlockSpec((HDIM, length), lambda i: (first + i, 0)),
        ],
        out_specs=[pl.BlockSpec((3, tokens, HDIM), lambda i: (0, 0, i))] * rows,
        out_shape=[jax.ShapeDtypeStruct(shape, jnp.bfloat16)] * rows,
        scratch_shapes=[pltpu.VMEM((length, length), jnp.bfloat16)],
        cost_estimate=cost(8 * count * length * length * HDIM, 2 * count * length * length),
        name="backward",
    )(*parts, probs, grad_attn)


def stacked(refs):
    return jnp.concatenate([ref[...] for ref in refs], axis=0)


def project(place, weights, grads):
    chunks, count = len(grads), len(grads[0])
    half, depth = weights[0].shape
    half = half * len(weights) // 2
    step = grads[0][0].shape[1] // 2

    def body(place_ref, *refs):
        ins, out, total = refs[len(weights) : -2], refs[-2], refs[-1]
        at = pl.program_id(0)
        lines = stacked(refs[: len(weights)])
        for chunk in range(chunks):

            @pl.when(at // 2 == chunk)
            def _():
                term = dot(lines, stacked(ins[chunk * count : (chunk + 1) * count]), NT)
                if chunk:
                    total[...] += term
                else:
                    total[...] = jnp.where(at == 0, 0.0, total[...]) + term

        @pl.when(at == chunks * 2 - 1)
        def _():
            for core in range(2):

                @pl.when(place_ref[2] == core)
                def _():
                    out[core * half : (core + 1) * half] = total[:half].astype(out.dtype)
                    out[(1 - core) * half : (2 - core) * half] = total[half:].astype(out.dtype)

    def block_of(chunk, block):
        return pl.BlockSpec(
            (block.shape[0], step), lambda i, place_ref: (0, jnp.clip(i - chunk * 2, 0, 1))
        )

    shape = (2 * half, sum(block.shape[0] for block in grads[0]))
    return pl.pallas_call(
        body,
        grid_spec=pltpu.PrefetchScalarGridSpec(
            num_scalar_prefetch=1,
            grid=(chunks * 2,),
            in_specs=[
                pl.BlockSpec((part.shape[0], step), lambda i, place_ref: (0, i)) for part in weights
            ]
            + [block_of(chunk, block) for chunk in range(chunks) for block in grads[chunk]],
            out_specs=whole(shape),
            scratch_shapes=[pltpu.VMEM(shape, jnp.float32)],
        ),
        out_shape=jax.ShapeDtypeStruct(shape, jnp.bfloat16),
        cost_estimate=cost(2 * shape[0] * shape[1] * depth, 2 * depth * (shape[0] + shape[1])),
        name="project",
    )(place, *weights, *(block for chunk in grads for block in chunk))


def weight_terms(place, attended, grads, parts, by_plane):
    width, length = attended.shape
    step = grads[0].shape[1] // 2
    piece = width // 2 // parts

    def body(place_ref, attended_ref, *refs):
        ins, (keep, give) = refs[:-2], refs[-2:]
        term = dot(attended_ref[...], stacked(ins)).astype(jnp.bfloat16)
        row, plane, core = place_ref[0], place_ref[1], place_ref[2]
        for side in range(2):
            for out, mine in ((keep, core == side), (give, core != side)):

                @pl.when(mine)
                def _():
                    for at in range(parts):
                        start = (side * parts + at) * piece
                        slot = (at - plane) & (parts - 1) if by_plane else at ^ row
                        out[slot] = term[start : start + piece]

    shape = jax.ShapeDtypeStruct((parts, piece, 2 * step), jnp.bfloat16)
    spec = pl.BlockSpec((parts, piece, step), lambda i, place_ref: (0, 0, i))
    return pl.pallas_call(
        body,
        grid_spec=pltpu.PrefetchScalarGridSpec(
            num_scalar_prefetch=1,
            grid=(2,),
            in_specs=[whole((width, length))]
            + [pl.BlockSpec((block.shape[0], step), lambda i, place_ref: (0, i)) for block in grads],
            out_specs=[spec] * 2,
        ),
        out_shape=[shape] * 2,
        cost_estimate=cost(4 * width * length * step, 2 * (width * length + 2 * length * step)),
        name="weight_terms",
    )(place, attended, *grads)


def after(value, *done):
    return lax.optimization_barrier((value, done))[0]


def onward(planes, hop, z, c, r):
    to = z + 1 if z > r else z - 1
    return (to, c, r) if abs(z - r) == hop and 0 <= to < planes else None


def by_heads(fsdp, rows, query_rows, key_rows, value_rows, grad_out, w_out):
    planes = fsdp // 2
    row = lax.axis_index("rows")
    member = lax.axis_index("fsdp")
    plane, core = member // 2, member % 2
    place = jnp.stack([row, plane, core]).astype(jnp.int32)

    def send(array, target):
        pairs = []
        for z in range(planes):
            for c in range(2):
                for r in range(rows):
                    to = target(z, c, r)
                    if to is not None:
                        pairs.append(((z * 2 + c) * rows + r, (to[0] * 2 + to[1]) * rows + to[2]))
        return lax.ppermute(array, ("fsdp", "rows"), pairs)

    def to_row(array, slot):
        return send(array, lambda z, c, r: (z, c, r ^ slot))

    def to_core(array):
        return send(array, lambda z, c, r: (z, 1 - c, r))

    def to_plane(array, ahead):
        return send(array, lambda z, c, r: ((z + ahead) % planes, c, r))

    grad_flat = grad_out[0]
    wide = grad_flat.shape[1] // 2

    def gather(chunk, *done):
        by_x, by_y = to_row(chunk, 1), to_row(chunk, 2)
        by_x, by_y = after((by_x, by_y), *done)
        cut = chunk.shape[0] // 2
        upper, lower = by_x[:cut], by_y[cut:]
        by_both = [to_row(upper, 2), to_row(lower, 1)]
        return [chunk, by_x, by_y, *by_both], (upper, lower)

    grads = [gather(grad_flat[:, :wide])[0]]

    away = jnp.abs(plane - row)
    cut = w_out.shape[0] // 2

    def leave(lines):
        above = send(lines, lambda z, c, r: (z + 1, c, r) if z == r and z + 1 < planes else None)
        below = send(lines, lambda z, c, r: (z - 1, c, r) if z == r and z > 0 else None)
        return jnp.where(plane > row, above, below)

    def go_on(hop, lines):
        return send(lines, functools.partial(onward, planes, hop))

    first = [w_out[:cut]]
    first.append(leave(first[0]))
    first.append(go_on(1, first[1]))
    second = [w_out[cut:]]
    second.append(leave(after(second[0], first[1])))
    first.append(go_on(2, first[2]))
    second.append(go_on(1, second[1]))

    packed = pack(place, query_rows, key_rows, value_rows, rows)
    parts = [packed[0]] + [to_row(packed[slot], slot) for slot in range(1, rows)]
    probs, attended = forward(parts)
    second.append(go_on(2, after(second[2], attended)))

    def mine(stages):
        here = stages[0]
        for hop in range(1, planes):
            here = jnp.where(away == hop, stages[hop], here)
        return here

    weights = [mine(first), mine(second)]
    weights += [to_core(part) for part in weights]
    block, handed = gather(after(grad_flat[:, wide:], parts), attended)
    grads.append(block)
    first[-1], second[-1] = after((first[-1], second[-1]), handed)

    def reduce_cores(at, attended, chunk):
        keep, give = weight_terms(place, attended, chunk, rows, not at)
        return keep, to_core(give)

    def add_cores(keep, got):
        return [
            (keep[slot].astype(jnp.float32) + got[slot].astype(jnp.float32)).astype(jnp.bfloat16)
            for slot in range(rows)
        ]

    def to_rows(blocks):
        return [blocks[0]] + [to_row(blocks[slot], slot) for slot in range(1, rows)]

    def to_planes(blocks):
        return [blocks[0]] + [to_plane(blocks[ahead], ahead) for ahead in range(1, planes)]

    def by_plane(blocks):
        return [
            lax.select_n(((plane + ahead) % planes) ^ row, *blocks) for ahead in range(planes)
        ]

    def added(blocks):
        total = blocks[0].astype(jnp.float32)
        for block in blocks[1:]:
            total = total + block.astype(jnp.float32)
        return total.astype(jnp.bfloat16)

    early = to_planes(add_cores(*reduce_cores(0, attended, grads[0])))
    late = to_rows(add_cores(*reduce_cores(1, attended, grads[1])))
    grad_attn = project(place, weights, grads)
    early = to_rows([added(after(early, grad_attn))] * rows)
    sent = backward(parts, probs, grad_attn, 0, probs.shape[0])
    back = to_rows(sent)
    late = to_planes(by_plane(after(late, sent[0])))
    early = to_planes(by_plane(after(early, sent[0])))
    late = to_rows([added(late)] * rows)
    return tuple(finish(place, [back], [early, late]))


def by_tokens(query_rows, key_rows, value_rows, grad_out, w_out):
    tokens, width = query_rows.shape[1:]
    heads = width // HDIM
    factor = 1.0 / math.sqrt(HDIM)
    grad_flat = grad_out[0]
    groups = math.gcd(heads, 3)

    def split(array, count):
        return jnp.moveaxis(array.reshape(count, groups, heads // groups, HDIM), 1, 0)

    def join(array, count):
        return jnp.moveaxis(array, 0, 1).reshape(count, width)

    grad_attn = lax.dot_general(
        grad_flat,
        lax.all_gather(w_out, "fsdp", axis=0, tiled=True),
        NT,
        preferred_element_type=jnp.float32,
    ).astype(jnp.bfloat16)
    all_keys = lax.all_gather(key_rows, "rows", axis=1, tiled=True)
    all_values = lax.all_gather(value_rows, "rows", axis=1, tiled=True)
    length = all_keys.shape[1]

    def product(spec, a, b):
        return jnp.einsum(spec, a, b, preferred_element_type=jnp.float32)

    def attend(inputs):
        queries, keys, values, grads = inputs
        probs = jax.nn.softmax(product("qhd,khd->hqk", queries, keys) * factor, axis=-1)
        low = probs.astype(jnp.bfloat16)
        attended = product("hqk,khd->qhd", low, values)
        value_part = product("hqk,qhd->khd", low, grads)
        grad_probs = product("qhd,khd->hqk", grads, values)
        centre = jnp.sum(probs * grad_probs, axis=-1, keepdims=True)
        grad_scores = (probs * (grad_probs - centre)).astype(jnp.bfloat16)
        grad_query = product("hqk,khd->qhd", grad_scores, keys) * factor
        key_part = product("hqk,qhd->khd", grad_scores, queries) * factor
        return (
            attended.astype(jnp.bfloat16),
            grad_query.astype(jnp.bfloat16),
            key_part.astype(jnp.bfloat16),
            value_part.astype(jnp.bfloat16),
        )

    attended, grad_query, key_part, value_part = lax.map(
        attend,
        (
            split(query_rows[0], tokens),
            split(all_keys[0], length),
            split(all_values[0], length),
            split(grad_attn, tokens),
        ),
    )

    def scatter(part):
        part = join(part, length).reshape(1, length, width)
        return lax.psum_scatter(part, "rows", scatter_dimension=1, tiled=True)

    term = lax.dot_general(
        join(attended, tokens),
        grad_flat,
        (((0,), (0,)), ((), ())),
        preferred_element_type=jnp.float32,
    ).astype(jnp.bfloat16)
    share = lax.psum_scatter(term, "fsdp", scatter_dimension=0, tiled=True)
    grad_w_out = lax.psum(share, "rows").astype(jnp.float32)
    return (
        join(grad_query, tokens).reshape(1, tokens, width),
        scatter(key_part),
        scatter(value_part),
        grad_w_out,
    )


def solution(mesh):
    fsdp, rows = mesh.shape["fsdp"], mesh.shape["rows"]

    def local(query_rows, key_rows, value_rows, grad_out, w_out):
        heads = query_rows.shape[2] // HDIM
        if rows == 4 and fsdp == 2 * rows and heads % rows == 0:
            plan = functools.partial(by_heads, fsdp, rows)
        else:
            plan = by_tokens
        return plan(query_rows, key_rows, value_rows, grad_out, w_out)

    tokens = P("fsdp", "rows", None)
    return jax.shard_map(
        local,
        mesh=mesh,
        in_specs=(tokens, tokens, tokens, tokens, P("fsdp", None)),
        out_specs=(tokens, tokens, tokens, P("fsdp", None)),
        check_vma=False,
    )
```

```python
import functools
import math

import jax
import jax.numpy as jnp
from jax import lax
from jax.experimental import pallas as pl
from jax.experimental.pallas import tpu as pltpu
from jax.sharding import PartitionSpec as P


HDIM = 128


NT = (((1,), (1,)), ((), ()))
NN = (((1,), (0,)), ((), ()))


def dot(a, b, dims=NN):
    return lax.dot_general(a, b, dims, preferred_element_type=jnp.float32)


def whole(shape):
    return pl.BlockSpec(shape, lambda *_: (0,) * len(shape))


def cost(flops, moved, exps=0):
    return pl.CostEstimate(flops=flops, bytes_accessed=moved, transcendentals=exps)


def pack(place, query, key, value, rows):
    tokens, width = query.shape[1], query.shape[2] // rows

    def body(place_ref, *refs):
        ins, outs, (held, sems) = refs[:3], refs[3:-2], refs[-2:]
        moves = []
        for slot in (*range(1, rows), 0):
            start = pl.multiple_of((place_ref[0] ^ slot) * width, HDIM)
            for at in range(3):
                box = held.at[slot, at]
                moves.append(
                    (
                        pltpu.make_async_copy(
                            ins[at].at[0, :, pl.ds(start, width)], box, sems.at[0, slot, at]
                        ),
                        pltpu.make_async_copy(box, outs[slot].at[at], sems.at[1, slot, at]),
                    )
                )
        run(moves)

    shape = (3, tokens, width)
    return pl.pallas_call(
        body,
        grid_spec=pltpu.PrefetchScalarGridSpec(
            num_scalar_prefetch=1,
            grid=(1,),
            in_specs=[pl.BlockSpec(memory_space=pltpu.HBM)] * 3,
            out_specs=[pl.BlockSpec(memory_space=pltpu.HBM)] * rows,
            scratch_shapes=[
                pltpu.VMEM((rows, *shape), query.dtype),
                pltpu.SemaphoreType.DMA((2, rows, 3)),
            ],
        ),
        out_shape=[jax.ShapeDtypeStruct(shape, query.dtype)] * rows,
        cost_estimate=cost(0, 12 * query.size),
        name="pack",
    )(place, query, key, value)


def run(moves):
    for fetch, _ in moves:
        fetch.start()
    for fetch, store in moves:
        fetch.wait()
        store.start()
    for _, store in moves:
        store.wait()


def finish(place, parts, pieces):
    calls, rows, chunks = len(parts), len(parts[0]), len(pieces)
    tokens = parts[0][0].shape[1]
    widths = [part[0].shape[2] for part in parts]
    starts = [sum(widths[:at]) for at in range(calls + 1)]
    width = starts[-1]
    piece, wide = pieces[0][0].shape

    def body(place_ref, *refs):
        ins, terms = refs[: calls * rows], refs[calls * rows : (calls + chunks) * rows]
        outs, total = refs[(calls + chunks) * rows :][:3], refs[(calls + chunks) * rows + 3]
        held, low, high, sems, term_sems = refs[-5:]
        moves, sums = [], []
        for call in range(calls):
            for slot in range(rows):
                start = (place_ref[0] ^ slot) * width + starts[call]
                start = pl.multiple_of(start, HDIM)
                for at in range(3):
                    box = held.at[slot, at, :, starts[call] : starts[call + 1]]
                    fetch = pltpu.make_async_copy(
                        ins[call * rows + slot].at[at], box, sems.at[0, call, slot, at]
                    )
                    store = pltpu.make_async_copy(
                        box,
                        outs[at].at[0, :, pl.ds(start, widths[call])],
                        sems.at[1, call, slot, at],
                    )
                    moves.append((fetch, store))
        for chunk in range(chunks):
            for slot in range(rows):
                owner = place_ref[0] ^ slot if chunk else (place_ref[1] - slot) & (rows - 1)
                start = pl.multiple_of(owner * piece, 16)
                fetch = pltpu.make_async_copy(
                    terms[chunk * rows + slot], low.at[chunk, slot], term_sems.at[0, chunk, slot]
                )
                store = pltpu.make_async_copy(
                    high.at[chunk, slot],
                    total.at[pl.ds(start, piece), chunk * wide : (chunk + 1) * wide],
                    term_sems.at[1, chunk, slot],
                )
                sums.append((chunk, slot, fetch, store))
        for _, _, fetch, _ in sums:
            fetch.start()
        for fetch, _ in moves:
            fetch.start()
        for chunk, slot, fetch, store in sums:
            fetch.wait()
            high[chunk, slot] = low[chunk, slot].astype(jnp.float32)
            store.start()
        for fetch, store in moves:
            fetch.wait()
            store.start()
        for _, _, _, store in sums:
            store.wait()
        for _, store in moves:
            store.wait()

    full = jax.ShapeDtypeStruct((1, tokens, width * rows), parts[0][0].dtype)
    return pl.pallas_call(
        body,
        grid_spec=pltpu.PrefetchScalarGridSpec(
            num_scalar_prefetch=1,
            grid=(1,),
            in_specs=[pl.BlockSpec(memory_space=pltpu.HBM)] * ((calls + chunks) * rows),
            out_specs=[pl.BlockSpec(memory_space=pltpu.HBM)] * 4,
            scratch_shapes=[
                pltpu.VMEM((rows, 3, tokens, width), parts[0][0].dtype),
                pltpu.VMEM((chunks, rows, piece, wide), pieces[0][0].dtype),
                pltpu.VMEM((chunks, rows, piece, wide), jnp.float32),
                pltpu.SemaphoreType.DMA((2, calls, rows, 3)),
                pltpu.SemaphoreType.DMA((2, chunks, rows)),
            ],
        ),
        out_shape=[full] * 3 + [jax.ShapeDtypeStruct((rows * piece, chunks * wide), jnp.float32)],
        cost_estimate=cost(0, 12 * tokens * width * rows + 6 * rows * piece * chunks * wide),
        name="finish",
    )(place, *(block for part in (*parts, *pieces) for block in part))


def forward(parts):
    rows = len(parts)
    _, tokens, width = parts[0].shape
    length, heads = rows * tokens, width // HDIM
    scale = math.log2(math.e) / math.sqrt(HDIM)

    def body(*refs):
        ins, (probs_ref, attended_ref) = refs[:rows], refs[rows:]
        keys = jnp.concatenate([ref[1] for ref in ins], axis=0)
        values = jnp.concatenate([ref[2] for ref in ins], axis=0).T
        for slot in range(rows):
            across = slice(slot * tokens, (slot + 1) * tokens)
            scores = dot(keys, ins[slot][0], NT)
            top = jnp.max(scores, axis=0, keepdims=True)
            powers = jnp.exp2((scores - top) * scale)
            total = jnp.sum(powers, axis=0, keepdims=True)
            probs = (powers * (1.0 / total)).astype(jnp.bfloat16)
            probs_ref[0, :, across] = probs
            attended_ref[:, across] = dot(values, probs).astype(jnp.bfloat16)

    part = pl.BlockSpec((3, tokens, HDIM), lambda h: (0, 0, h))
    return pl.pallas_call(
        body,
        grid=(heads,),
        in_specs=[part] * rows,
        out_specs=[
            pl.BlockSpec((1, length, length), lambda h: (h, 0, 0)),
            pl.BlockSpec((HDIM, length), lambda h: (h, 0)),
        ],
        out_shape=[
            jax.ShapeDtypeStruct((heads, length, length), jnp.bfloat16),
            jax.ShapeDtypeStruct((width, length), jnp.bfloat16),
        ],
        cost_estimate=cost(
            8 * heads * length * length * HDIM, 2 * heads * length * length, heads * length * length
        ),
        name="forward",
    )(*parts)


def backward(parts, probs, grad_attn, first, count):
    rows = len(parts)
    tokens = parts[0].shape[1]
    length = rows * tokens
    factor = 1.0 / math.sqrt(HDIM)

    def body(*refs):
        ins, (probs_ref, grad_ref) = refs[:rows], refs[rows : rows + 2]
        outs, scores_ref = refs[rows + 2 : -1], refs[-1]
        queries = jnp.concatenate([ref[0] for ref in ins], axis=0)
        keys = jnp.concatenate([ref[1] for ref in ins], axis=0).T
        values = jnp.concatenate([ref[2] for ref in ins], axis=0)
        for slot in range(rows):
            across = slice(slot * tokens, (slot + 1) * tokens)
            probs = probs_ref[0, :, across].astype(jnp.float32)
            terms = probs * dot(values, grad_ref[:, across])
            centre = jnp.sum(terms, axis=0, keepdims=True)
            scores_ref[:, across] = (terms - probs * centre).astype(jnp.bfloat16)
        scores = scores_ref[...]
        grad_query = (dot(keys, scores) * factor).T
        grad_key = dot(scores, queries) * factor
        grad_value = dot(probs_ref[0], grad_ref[...], NT)
        for slot in range(rows):
            down = slice(slot * tokens, (slot + 1) * tokens)
            outs[slot][0] = grad_query[down].astype(jnp.bfloat16)
            outs[slot][1] = grad_key[down].astype(jnp.bfloat16)
            outs[slot][2] = grad_value[down].astype(jnp.bfloat16)

    part = pl.BlockSpec((3, tokens, HDIM), lambda i: (0, 0, first + i))
    shape = (3, tokens, count * HDIM)
    return pl.pallas_call(
        body,
        grid=(count,),
        in_specs=[part] * rows
        + [
            pl.BlockSpec((1, length, length), lambda i: (first + i, 0, 0)),
            pl.BlockSpec((HDIM, length), lambda i: (first + i, 0)),
        ],
        out_specs=[pl.BlockSpec((3, tokens, HDIM), lambda i: (0, 0, i))] * rows,
        out_shape=[jax.ShapeDtypeStruct(shape, jnp.bfloat16)] * rows,
        scratch_shapes=[pltpu.VMEM((length, length), jnp.bfloat16)],
        cost_estimate=cost(8 * count * length * length * HDIM, 2 * count * length * length),
        name="backward",
    )(*parts, probs, grad_attn)


def stacked(refs):
    return jnp.concatenate([ref[...] for ref in refs], axis=0)


def project(place, weights, grads):
    chunks, count = len(grads), len(grads[0])
    half, depth = weights[0].shape
    half = half * len(weights) // 2
    step = grads[0][0].shape[1] // 2

    def body(place_ref, *refs):
        ins, out, total = refs[len(weights) : -2], refs[-2], refs[-1]
        at = pl.program_id(0)
        lines = stacked(refs[: len(weights)])
        for chunk in range(chunks):

            @pl.when(at // 2 == chunk)
            def _():
                term = dot(lines, stacked(ins[chunk * count : (chunk + 1) * count]), NT)
                if chunk:
                    total[...] += term
                else:
                    total[...] = jnp.where(at == 0, 0.0, total[...]) + term

        @pl.when(at == chunks * 2 - 1)
        def _():
            for core in range(2):

                @pl.when(place_ref[2] == core)
                def _():
                    out[core * half : (core + 1) * half] = total[:half].astype(out.dtype)
                    out[(1 - core) * half : (2 - core) * half] = total[half:].astype(out.dtype)

    def block_of(chunk, block):
        return pl.BlockSpec(
            (block.shape[0], step), lambda i, place_ref: (0, jnp.clip(i - chunk * 2, 0, 1))
        )

    shape = (2 * half, sum(block.shape[0] for block in grads[0]))
    return pl.pallas_call(
        body,
        grid_spec=pltpu.PrefetchScalarGridSpec(
            num_scalar_prefetch=1,
            grid=(chunks * 2,),
            in_specs=[
                pl.BlockSpec((part.shape[0], step), lambda i, place_ref: (0, i)) for part in weights
            ]
            + [block_of(chunk, block) for chunk in range(chunks) for block in grads[chunk]],
            out_specs=whole(shape),
            scratch_shapes=[pltpu.VMEM(shape, jnp.float32)],
        ),
        out_shape=jax.ShapeDtypeStruct(shape, jnp.bfloat16),
        cost_estimate=cost(2 * shape[0] * shape[1] * depth, 2 * depth * (shape[0] + shape[1])),
        name="project",
    )(place, *weights, *(block for chunk in grads for block in chunk))


def weight_terms(place, attended, grads, parts, by_plane):
    width, length = attended.shape
    step = grads[0].shape[1] // 2
    piece = width // 2 // parts

    def body(place_ref, attended_ref, *refs):
        ins, (keep, give) = refs[:-2], refs[-2:]
        term = dot(attended_ref[...], stacked(ins)).astype(jnp.bfloat16)
        row, plane, core = place_ref[0], place_ref[1], place_ref[2]
        for side in range(2):
            for out, mine in ((keep, core == side), (give, core != side)):

                @pl.when(mine)
                def _():
                    for at in range(parts):
                        start = (side * parts + at) * piece
                        slot = (at - plane) & (parts - 1) if by_plane else at ^ row
                        out[slot] = term[start : start + piece]

    shape = jax.ShapeDtypeStruct((parts, piece, 2 * step), jnp.bfloat16)
    spec = pl.BlockSpec((parts, piece, step), lambda i, place_ref: (0, 0, i))
    return pl.pallas_call(
        body,
        grid_spec=pltpu.PrefetchScalarGridSpec(
            num_scalar_prefetch=1,
            grid=(2,),
            in_specs=[whole((width, length))]
            + [pl.BlockSpec((block.shape[0], step), lambda i, place_ref: (0, i)) for block in grads],
            out_specs=[spec] * 2,
        ),
        out_shape=[shape] * 2,
        cost_estimate=cost(4 * width * length * step, 2 * (width * length + 2 * length * step)),
        name="weight_terms",
    )(place, attended, *grads)


def after(value, *done):
    return lax.optimization_barrier((value, done))[0]


def onward(planes, hop, z, c, r):
    to = z + 1 if z > r else z - 1
    return (to, c, r) if abs(z - r) == hop and 0 <= to < planes else None


def by_heads(fsdp, rows, query_rows, key_rows, value_rows, grad_out, w_out):
    planes = fsdp // 2
    row = lax.axis_index("rows")
    member = lax.axis_index("fsdp")
    plane, core = member // 2, member % 2
    place = jnp.stack([row, plane, core]).astype(jnp.int32)

    def send(array, target):
        pairs = []
        for z in range(planes):
            for c in range(2):
                for r in range(rows):
                    to = target(z, c, r)
                    if to is not None:
                        pairs.append(((z * 2 + c) * rows + r, (to[0] * 2 + to[1]) * rows + to[2]))
        return lax.ppermute(array, ("fsdp", "rows"), pairs)

    def to_row(array, slot):
        return send(array, lambda z, c, r: (z, c, r ^ slot))

    def to_core(array):
        return send(array, lambda z, c, r: (z, 1 - c, r))

    def to_plane(array, ahead):
        return send(array, lambda z, c, r: ((z + ahead) % planes, c, r))

    grad_flat = grad_out[0]
    wide = grad_flat.shape[1] // 2

    def gather(chunk, *done):
        by_x, by_y = to_row(chunk, 1), to_row(chunk, 2)
        by_x, by_y = after((by_x, by_y), *done)
        cut = chunk.shape[0] // 2
        upper, lower = by_x[:cut], by_y[cut:]
        by_both = [to_row(upper, 2), to_row(lower, 1)]
        return [chunk, by_x, by_y, *by_both]

    grads = [gather(grad_flat[:, :wide])]

    away = jnp.abs(plane - row)
    cut = w_out.shape[0] // 2

    def leave(lines):
        above = send(lines, lambda z, c, r: (z + 1, c, r) if z == r and z + 1 < planes else None)
        below = send(lines, lambda z, c, r: (z - 1, c, r) if z == r and z > 0 else None)
        return jnp.where(plane > row, above, below)

    def go_on(hop, lines):
        return send(lines, functools.partial(onward, planes, hop))

    first = [w_out[:cut]]
    first.append(leave(first[0]))
    first.append(go_on(1, first[1]))
    second = [w_out[cut:]]
    second.append(leave(after(second[0], first[1])))
    first.append(go_on(2, first[2]))
    second.append(go_on(1, second[1]))

    packed = pack(place, query_rows, key_rows, value_rows, rows)
    parts = [packed[0]] + [to_row(packed[slot], slot) for slot in range(1, rows)]
    probs, attended = forward(parts)
    second.append(go_on(2, after(second[2], attended)))

    def mine(stages):
        here = stages[0]
        for hop in range(1, planes):
            here = jnp.where(away == hop, stages[hop], here)
        return here

    grads.append(gather(after(grad_flat[:, wide:], parts), attended))

    def reduce_cores(at, attended, chunk):
        keep, give = weight_terms(place, attended, chunk, rows, not at)
        return keep, to_core(give)

    def add_cores(keep, got):
        return [
            (keep[slot].astype(jnp.float32) + got[slot].astype(jnp.float32)).astype(jnp.bfloat16)
            for slot in range(rows)
        ]

    def to_rows(blocks):
        return [blocks[0]] + [to_row(blocks[slot], slot) for slot in range(1, rows)]

    def to_planes(blocks):
        return [blocks[0]] + [to_plane(blocks[ahead], ahead) for ahead in range(1, planes)]

    def by_plane(blocks):
        return [
            lax.select_n(((plane + ahead) % planes) ^ row, *blocks) for ahead in range(planes)
        ]

    def added(blocks):
        total = blocks[0].astype(jnp.float32)
        for block in blocks[1:]:
            total = total + block.astype(jnp.float32)
        return total.astype(jnp.bfloat16)

    early = to_planes(add_cores(*reduce_cores(0, attended, grads[0])))
    late = to_rows(add_cores(*reduce_cores(1, attended, grads[1])))
    first[-1], second[-1] = after((first[-1], second[-1]), late[0])
    weights = [mine(first), mine(second)]
    weights += [to_core(part) for part in weights]
    grad_attn = project(place, weights, grads)
    early = to_rows([added(after(early, grad_attn))] * rows)
    sent = backward(parts, probs, grad_attn, 0, probs.shape[0])
    back = to_rows(sent)
    late = to_planes(by_plane(after(late, sent[0])))
    early = to_planes(by_plane(after(early, sent[0])))
    late = to_rows([added(late)] * rows)
    return tuple(finish(place, [back], [early, late]))


def by_tokens(query_rows, key_rows, value_rows, grad_out, w_out):
    tokens, width = query_rows.shape[1:]
    heads = width // HDIM
    factor = 1.0 / math.sqrt(HDIM)
    grad_flat = grad_out[0]
    groups = math.gcd(heads, 3)

    def split(array, count):
        return jnp.moveaxis(array.reshape(count, groups, heads // groups, HDIM), 1, 0)

    def join(array, count):
        return jnp.moveaxis(array, 0, 1).reshape(count, width)

    grad_attn = lax.dot_general(
        grad_flat,
        lax.all_gather(w_out, "fsdp", axis=0, tiled=True),
        NT,
        preferred_element_type=jnp.float32,
    ).astype(jnp.bfloat16)
    all_keys = lax.all_gather(key_rows, "rows", axis=1, tiled=True)
    all_values = lax.all_gather(value_rows, "rows", axis=1, tiled=True)
    length = all_keys.shape[1]

    def product(spec, a, b):
        return jnp.einsum(spec, a, b, preferred_element_type=jnp.float32)

    def attend(inputs):
        queries, keys, values, grads = inputs
        probs = jax.nn.softmax(product("qhd,khd->hqk", queries, keys) * factor, axis=-1)
        low = probs.astype(jnp.bfloat16)
        attended = product("hqk,khd->qhd", low, values)
        value_part = product("hqk,qhd->khd", low, grads)
        grad_probs = product("qhd,khd->hqk", grads, values)
        centre = jnp.sum(probs * grad_probs, axis=-1, keepdims=True)
        grad_scores = (probs * (grad_probs - centre)).astype(jnp.bfloat16)
        grad_query = product("hqk,khd->qhd", grad_scores, keys) * factor
        key_part = product("hqk,qhd->khd", grad_scores, queries) * factor
        return (
            attended.astype(jnp.bfloat16),
            grad_query.astype(jnp.bfloat16),
            key_part.astype(jnp.bfloat16),
            value_part.astype(jnp.bfloat16),
        )

    attended, grad_query, key_part, value_part = lax.map(
        attend,
        (
            split(query_rows[0], tokens),
            split(all_keys[0], length),
            split(all_values[0], length),
            split(grad_attn, tokens),
        ),
    )

    def scatter(part):
        part = join(part, length).reshape(1, length, width)
        return lax.psum_scatter(part, "rows", scatter_dimension=1, tiled=True)

    term = lax.dot_general(
        join(attended, tokens),
        grad_flat,
        (((0,), (0,)), ((), ())),
        preferred_element_type=jnp.float32,
    ).astype(jnp.bfloat16)
    share = lax.psum_scatter(term, "fsdp", scatter_dimension=0, tiled=True)
    grad_w_out = lax.psum(share, "rows").astype(jnp.float32)
    return (
        join(grad_query, tokens).reshape(1, tokens, width),
        scatter(key_part),
        scatter(value_part),
        grad_w_out,
    )


def solution(mesh):
    fsdp, rows = mesh.shape["fsdp"], mesh.shape["rows"]

    def local(query_rows, key_rows, value_rows, grad_out, w_out):
        heads = query_rows.shape[2] // HDIM
        if rows == 4 and fsdp == 2 * rows and heads % rows == 0:
            plan = functools.partial(by_heads, fsdp, rows)
        else:
            plan = by_tokens
        return plan(query_rows, key_rows, value_rows, grad_out, w_out)

    tokens = P("fsdp", "rows", None)
    return jax.shard_map(
        local,
        mesh=mesh,
        in_specs=(tokens, tokens, tokens, tokens, P("fsdp", None)),
        out_specs=(tokens, tokens, tokens, P("fsdp", None)),
        check_vma=False,
    )
```

```python
import functools
import math

import jax
import jax.numpy as jnp
from jax import lax
from jax.experimental import pallas as pl
from jax.experimental.pallas import tpu as pltpu
from jax.sharding import PartitionSpec as P


HDIM = 128


NT = (((1,), (1,)), ((), ()))
NN = (((1,), (0,)), ((), ()))


def dot(a, b, dims=NN):
    return lax.dot_general(a, b, dims, preferred_element_type=jnp.float32)


def whole(shape):
    return pl.BlockSpec(shape, lambda *_: (0,) * len(shape))


def cost(flops, moved, exps=0):
    return pl.CostEstimate(flops=flops, bytes_accessed=moved, transcendentals=exps)


def pack(place, query, key, value, rows):
    tokens, width = query.shape[1], query.shape[2] // rows

    def body(place_ref, *refs):
        ins, outs, (held, sems) = refs[:3], refs[3:-2], refs[-2:]
        moves = []
        for slot in (*range(1, rows), 0):
            start = pl.multiple_of((place_ref[0] ^ slot) * width, HDIM)
            for at in range(3):
                box = held.at[slot, at]
                moves.append(
                    (
                        pltpu.make_async_copy(
                            ins[at].at[0, :, pl.ds(start, width)], box, sems.at[0, slot, at]
                        ),
                        pltpu.make_async_copy(box, outs[slot].at[at], sems.at[1, slot, at]),
                    )
                )
        run(moves)

    shape = (3, tokens, width)
    return pl.pallas_call(
        body,
        grid_spec=pltpu.PrefetchScalarGridSpec(
            num_scalar_prefetch=1,
            grid=(1,),
            in_specs=[pl.BlockSpec(memory_space=pltpu.HBM)] * 3,
            out_specs=[pl.BlockSpec(memory_space=pltpu.HBM)] * rows,
            scratch_shapes=[
                pltpu.VMEM((rows, *shape), query.dtype),
                pltpu.SemaphoreType.DMA((2, rows, 3)),
            ],
        ),
        out_shape=[jax.ShapeDtypeStruct(shape, query.dtype)] * rows,
        cost_estimate=cost(0, 12 * query.size),
        name="pack",
    )(place, query, key, value)


def run(moves, rest=None):
    for fetch, _ in moves:
        fetch.start()
    for fetch, store in moves:
        fetch.wait()
        store.start()
    for store in rest() if rest else ():
        store.wait()
    for _, store in moves:
        store.wait()


def write_terms(place, pieces, total, low, high, sems, chunk):
    rows, piece, wide = low.shape
    steps = []
    for slot in range(rows):
        owner = place[0] ^ slot if chunk else (place[1] - slot) & (rows - 1)
        start = pl.multiple_of(owner * piece, 16)
        fetch = pltpu.make_async_copy(pieces[slot], low.at[slot], sems.at[0, slot])
        store = pltpu.make_async_copy(
            high.at[slot],
            total.at[pl.ds(start, piece), chunk * wide : (chunk + 1) * wide],
            sems.at[1, slot],
        )
        steps.append((fetch, store))
    for fetch, _ in steps:
        fetch.start()

    def rest():
        for slot, (fetch, store) in enumerate(steps):
            fetch.wait()
            high[slot] = low[slot].astype(jnp.float32)
            store.start()
        return [store for _, store in steps]

    return rest


def finish(place, parts, pieces, chunks):
    rows = len(parts)
    _, tokens, width = parts[0].shape
    piece, wide = pieces[0].shape

    def body(place_ref, *refs):
        ins, terms, outs, total = refs[:rows], refs[rows : 2 * rows], refs[2 * rows :][:3], refs[-6]
        held, low, high, sems, term_sems = refs[-5:]
        moves = []
        for slot in range(rows):
            start = pl.multiple_of((place_ref[0] ^ slot) * width, HDIM)
            for at in range(3):
                box = held.at[slot, at]
                moves.append(
                    (
                        pltpu.make_async_copy(ins[slot].at[at], box, sems.at[0, slot, at]),
                        pltpu.make_async_copy(
                            box, outs[at].at[0, :, pl.ds(start, width)], sems.at[1, slot, at]
                        ),
                    )
                )
        rest = write_terms(place_ref, terms, total, low, high, term_sems, 0)
        run(moves, rest)

    full = jax.ShapeDtypeStruct((1, tokens, width * rows), parts[0].dtype)
    return pl.pallas_call(
        body,
        grid_spec=pltpu.PrefetchScalarGridSpec(
            num_scalar_prefetch=1,
            grid=(1,),
            in_specs=[pl.BlockSpec(memory_space=pltpu.HBM)] * (2 * rows),
            out_specs=[pl.BlockSpec(memory_space=pltpu.HBM)] * 4,
            scratch_shapes=[
                pltpu.VMEM((rows, 3, tokens, width), parts[0].dtype),
                pltpu.VMEM((rows, piece, wide), pieces[0].dtype),
                pltpu.VMEM((rows, piece, wide), jnp.float32),
                pltpu.SemaphoreType.DMA((2, rows, 3)),
                pltpu.SemaphoreType.DMA((2, rows)),
            ],
        ),
        out_shape=[full] * 3 + [jax.ShapeDtypeStruct((rows * piece, chunks * wide), jnp.float32)],
        cost_estimate=cost(0, 12 * tokens * width * rows + 6 * rows * piece * wide),
        name="finish",
    )(place, *parts, *pieces)


def finish_terms(place, total, pieces, chunk):
    rows = len(pieces)
    piece, wide = pieces[0].shape

    def body(place_ref, _, *refs):
        terms, (out, low, high, sems) = refs[:rows], refs[rows:]
        for store in write_terms(place_ref, terms, out, low, high, sems, chunk)():
            store.wait()

    return pl.pallas_call(
        body,
        grid_spec=pltpu.PrefetchScalarGridSpec(
            num_scalar_prefetch=1,
            grid=(1,),
            in_specs=[pl.BlockSpec(memory_space=pltpu.HBM)] * (1 + rows),
            out_specs=pl.BlockSpec(memory_space=pltpu.HBM),
            scratch_shapes=[
                pltpu.VMEM((rows, piece, wide), pieces[0].dtype),
                pltpu.VMEM((rows, piece, wide), jnp.float32),
                pltpu.SemaphoreType.DMA((2, rows)),
            ],
        ),
        out_shape=jax.ShapeDtypeStruct(total.shape, total.dtype),
        input_output_aliases={1: 0},
        cost_estimate=cost(0, 6 * rows * piece * wide),
        name="finish_terms",
    )(place, total, *pieces)


def forward(parts):
    rows = len(parts)
    _, tokens, width = parts[0].shape
    length, heads = rows * tokens, width // HDIM
    scale = math.log2(math.e) / math.sqrt(HDIM)

    def body(*refs):
        ins, (probs_ref, attended_ref) = refs[:rows], refs[rows:]
        keys = jnp.concatenate([ref[1] for ref in ins], axis=0)
        values = jnp.concatenate([ref[2] for ref in ins], axis=0).T
        for slot in range(rows):
            across = slice(slot * tokens, (slot + 1) * tokens)
            scores = dot(keys, ins[slot][0], NT)
            top = jnp.max(scores, axis=0, keepdims=True)
            powers = jnp.exp2((scores - top) * scale)
            total = jnp.sum(powers, axis=0, keepdims=True)
            probs = (powers * (1.0 / total)).astype(jnp.bfloat16)
            probs_ref[0, :, across] = probs
            attended_ref[:, across] = dot(values, probs).astype(jnp.bfloat16)

    part = pl.BlockSpec((3, tokens, HDIM), lambda h: (0, 0, h))
    return pl.pallas_call(
        body,
        grid=(heads,),
        in_specs=[part] * rows,
        out_specs=[
            pl.BlockSpec((1, length, length), lambda h: (h, 0, 0)),
            pl.BlockSpec((HDIM, length), lambda h: (h, 0)),
        ],
        out_shape=[
            jax.ShapeDtypeStruct((heads, length, length), jnp.bfloat16),
            jax.ShapeDtypeStruct((width, length), jnp.bfloat16),
        ],
        cost_estimate=cost(
            8 * heads * length * length * HDIM, 2 * heads * length * length, heads * length * length
        ),
        name="forward",
    )(*parts)


def backward(parts, probs, grad_attn, first, count):
    rows = len(parts)
    tokens = parts[0].shape[1]
    length = rows * tokens
    factor = 1.0 / math.sqrt(HDIM)

    def body(*refs):
        ins, (probs_ref, grad_ref) = refs[:rows], refs[rows : rows + 2]
        outs, scores_ref = refs[rows + 2 : -1], refs[-1]
        queries = jnp.concatenate([ref[0] for ref in ins], axis=0)
        keys = jnp.concatenate([ref[1] for ref in ins], axis=0).T
        values = jnp.concatenate([ref[2] for ref in ins], axis=0)
        for slot in range(rows):
            across = slice(slot * tokens, (slot + 1) * tokens)
            probs = probs_ref[0, :, across].astype(jnp.float32)
            terms = probs * dot(values, grad_ref[:, across])
            centre = jnp.sum(terms, axis=0, keepdims=True)
            scores_ref[:, across] = (terms - probs * centre).astype(jnp.bfloat16)
        scores = scores_ref[...]
        grad_query = (dot(keys, scores) * factor).T
        grad_key = dot(scores, queries) * factor
        grad_value = dot(probs_ref[0], grad_ref[...], NT)
        for slot in range(rows):
            down = slice(slot * tokens, (slot + 1) * tokens)
            outs[slot][0] = grad_query[down].astype(jnp.bfloat16)
            outs[slot][1] = grad_key[down].astype(jnp.bfloat16)
            outs[slot][2] = grad_value[down].astype(jnp.bfloat16)

    part = pl.BlockSpec((3, tokens, HDIM), lambda i: (0, 0, first + i))
    shape = (3, tokens, count * HDIM)
    return pl.pallas_call(
        body,
        grid=(count,),
        in_specs=[part] * rows
        + [
            pl.BlockSpec((1, length, length), lambda i: (first + i, 0, 0)),
            pl.BlockSpec((HDIM, length), lambda i: (first + i, 0)),
        ],
        out_specs=[pl.BlockSpec((3, tokens, HDIM), lambda i: (0, 0, i))] * rows,
        out_shape=[jax.ShapeDtypeStruct(shape, jnp.bfloat16)] * rows,
        scratch_shapes=[pltpu.VMEM((length, length), jnp.bfloat16)],
        cost_estimate=cost(8 * count * length * length * HDIM, 2 * count * length * length),
        name="backward",
    )(*parts, probs, grad_attn)


def stacked(refs):
    return jnp.concatenate([ref[...] for ref in refs], axis=0)


def project(place, weights, grads):
    chunks, count = len(grads), len(grads[0])
    half, depth = weights[0].shape
    half = half * len(weights) // 2
    step = grads[0][0].shape[1] // 2

    def body(place_ref, *refs):
        ins, out, total = refs[len(weights) : -2], refs[-2], refs[-1]
        at = pl.program_id(0)
        lines = stacked(refs[: len(weights)])
        for chunk in range(chunks):

            @pl.when(at // 2 == chunk)
            def _():
                term = dot(lines, stacked(ins[chunk * count : (chunk + 1) * count]), NT)
                if chunk:
                    total[...] += term
                else:
                    total[...] = jnp.where(at == 0, 0.0, total[...]) + term

        @pl.when(at == chunks * 2 - 1)
        def _():
            for core in range(2):

                @pl.when(place_ref[2] == core)
                def _():
                    out[core * half : (core + 1) * half] = total[:half].astype(out.dtype)
                    out[(1 - core) * half : (2 - core) * half] = total[half:].astype(out.dtype)

    def block_of(chunk, block):
        return pl.BlockSpec(
            (block.shape[0], step), lambda i, place_ref: (0, jnp.clip(i - chunk * 2, 0, 1))
        )

    shape = (2 * half, sum(block.shape[0] for block in grads[0]))
    return pl.pallas_call(
        body,
        grid_spec=pltpu.PrefetchScalarGridSpec(
            num_scalar_prefetch=1,
            grid=(chunks * 2,),
            in_specs=[
                pl.BlockSpec((part.shape[0], step), lambda i, place_ref: (0, i)) for part in weights
            ]
            + [block_of(chunk, block) for chunk in range(chunks) for block in grads[chunk]],
            out_specs=whole(shape),
            scratch_shapes=[pltpu.VMEM(shape, jnp.float32)],
        ),
        out_shape=jax.ShapeDtypeStruct(shape, jnp.bfloat16),
        cost_estimate=cost(2 * shape[0] * shape[1] * depth, 2 * depth * (shape[0] + shape[1])),
        name="project",
    )(place, *weights, *(block for chunk in grads for block in chunk))


def weight_terms(place, attended, grads, parts, by_plane):
    width, length = attended.shape
    step = grads[0].shape[1] // 2
    piece = width // 2 // parts

    def body(place_ref, attended_ref, *refs):
        ins, (keep, give) = refs[:-2], refs[-2:]
        term = dot(attended_ref[...], stacked(ins)).astype(jnp.bfloat16)
        row, plane, core = place_ref[0], place_ref[1], place_ref[2]
        for side in range(2):
            for out, mine in ((keep, core == side), (give, core != side)):

                @pl.when(mine)
                def _():
                    for at in range(parts):
                        start = (side * parts + at) * piece
                        slot = (at - plane) & (parts - 1) if by_plane else at ^ row
                        out[slot] = term[start : start + piece]

    shape = jax.ShapeDtypeStruct((parts, piece, 2 * step), jnp.bfloat16)
    spec = pl.BlockSpec((parts, piece, step), lambda i, place_ref: (0, 0, i))
    return pl.pallas_call(
        body,
        grid_spec=pltpu.PrefetchScalarGridSpec(
            num_scalar_prefetch=1,
            grid=(2,),
            in_specs=[whole((width, length))]
            + [pl.BlockSpec((block.shape[0], step), lambda i, place_ref: (0, i)) for block in grads],
            out_specs=[spec] * 2,
        ),
        out_shape=[shape] * 2,
        cost_estimate=cost(4 * width * length * step, 2 * (width * length + 2 * length * step)),
        name="weight_terms",
    )(place, attended, *grads)


def after(value, *done):
    return lax.optimization_barrier((value, done))[0]


def onward(planes, hop, z, c, r):
    to = z + 1 if z > r else z - 1
    return (to, c, r) if abs(z - r) == hop and 0 <= to < planes else None


def by_heads(fsdp, rows, query_rows, key_rows, value_rows, grad_out, w_out):
    planes = fsdp // 2
    row = lax.axis_index("rows")
    member = lax.axis_index("fsdp")
    plane, core = member // 2, member % 2
    place = jnp.stack([row, plane, core]).astype(jnp.int32)

    def send(array, target):
        pairs = []
        for z in range(planes):
            for c in range(2):
                for r in range(rows):
                    to = target(z, c, r)
                    if to is not None:
                        pairs.append(((z * 2 + c) * rows + r, (to[0] * 2 + to[1]) * rows + to[2]))
        return lax.ppermute(array, ("fsdp", "rows"), pairs)

    def to_row(array, slot):
        return send(array, lambda z, c, r: (z, c, r ^ slot))

    def to_core(array):
        return send(array, lambda z, c, r: (z, 1 - c, r))

    def to_plane(array, ahead):
        return send(array, lambda z, c, r: ((z + ahead) % planes, c, r))

    grad_flat = grad_out[0]
    wide = grad_flat.shape[1] // 2

    def gather(chunk, *done):
        by_x, by_y = to_row(chunk, 1), to_row(chunk, 2)
        by_x, by_y = after((by_x, by_y), *done)
        cut = chunk.shape[0] // 2
        upper, lower = by_x[:cut], by_y[cut:]
        by_both = [to_row(upper, 2), to_row(lower, 1)]
        return [chunk, by_x, by_y, *by_both]

    grads = [gather(grad_flat[:, :wide])]

    away = jnp.abs(plane - row)
    cut = w_out.shape[0] // 2

    def leave(lines):
        above = send(lines, lambda z, c, r: (z + 1, c, r) if z == r and z + 1 < planes else None)
        below = send(lines, lambda z, c, r: (z - 1, c, r) if z == r and z > 0 else None)
        return jnp.where(plane > row, above, below)

    def go_on(hop, lines):
        return send(lines, functools.partial(onward, planes, hop))

    first = [w_out[:cut]]
    first.append(leave(first[0]))
    first.append(go_on(1, first[1]))
    second = [w_out[cut:]]
    second.append(leave(after(second[0], first[1])))
    first.append(go_on(2, first[2]))
    second.append(go_on(1, second[1]))

    packed = pack(place, query_rows, key_rows, value_rows, rows)
    parts = [packed[0]] + [to_row(packed[slot], slot) for slot in range(1, rows)]
    probs, attended = forward(parts)
    second.append(go_on(2, after(second[2], attended)))

    def mine(stages):
        here = stages[0]
        for hop in range(1, planes):
            here = jnp.where(away == hop, stages[hop], here)
        return here

    grads.append(gather(after(grad_flat[:, wide:], parts), attended))


    def reduce_cores(at, attended, chunk):
        keep, give = weight_terms(place, attended, chunk, rows, not at)
        return keep, to_core(give)

    def add_cores(keep, got):
        return [
            (keep[slot].astype(jnp.float32) + got[slot].astype(jnp.float32)).astype(jnp.bfloat16)
            for slot in range(rows)
        ]

    def to_rows(blocks):
        return [blocks[0]] + [to_row(blocks[slot], slot) for slot in range(1, rows)]

    def to_planes(blocks):
        return [blocks[0]] + [to_plane(blocks[ahead], ahead) for ahead in range(1, planes)]

    def by_plane(blocks):
        return [
            lax.select_n(((plane + ahead) % planes) ^ row, *blocks) for ahead in range(planes)
        ]

    def added(blocks):
        total = blocks[0].astype(jnp.float32)
        for block in blocks[1:]:
            total = total + block.astype(jnp.float32)
        return total.astype(jnp.bfloat16)

    early = to_planes(add_cores(*reduce_cores(0, attended, grads[0])))
    first[-1], second[-1] = after((first[-1], second[-1]), early[0])
    weights = [mine(first), mine(second)]
    weights += [to_core(part) for part in weights]
    late = reduce_cores(1, after(attended, weights), grads[1])
    grad_attn = project(place, weights, grads)
    late = to_rows(add_cores(*after(late, grad_attn)))
    early = to_rows([added(after(early, grad_attn))] * rows)
    sent = backward(parts, probs, grad_attn, 0, probs.shape[0])
    back = to_rows(sent)
    late = to_planes(by_plane(after(late, sent[0])))
    early = to_planes(by_plane(after(early, sent[0])))
    late = to_rows([added(late)] * rows)
    *outs, total = finish(place, back, early, len(grads))
    return (*outs, finish_terms(place, total, after(late, outs[0]), 1))


def by_tokens(query_rows, key_rows, value_rows, grad_out, w_out):
    tokens, width = query_rows.shape[1:]
    heads = width // HDIM
    factor = 1.0 / math.sqrt(HDIM)
    grad_flat = grad_out[0]
    groups = math.gcd(heads, 3)

    def split(array, count):
        return jnp.moveaxis(array.reshape(count, groups, heads // groups, HDIM), 1, 0)

    def join(array, count):
        return jnp.moveaxis(array, 0, 1).reshape(count, width)

    grad_attn = lax.dot_general(
        grad_flat,
        lax.all_gather(w_out, "fsdp", axis=0, tiled=True),
        NT,
        preferred_element_type=jnp.float32,
    ).astype(jnp.bfloat16)
    all_keys = lax.all_gather(key_rows, "rows", axis=1, tiled=True)
    all_values = lax.all_gather(value_rows, "rows", axis=1, tiled=True)
    length = all_keys.shape[1]

    def product(spec, a, b):
        return jnp.einsum(spec, a, b, preferred_element_type=jnp.float32)

    def attend(inputs):
        queries, keys, values, grads = inputs
        probs = jax.nn.softmax(product("qhd,khd->hqk", queries, keys) * factor, axis=-1)
        low = probs.astype(jnp.bfloat16)
        attended = product("hqk,khd->qhd", low, values)
        value_part = product("hqk,qhd->khd", low, grads)
        grad_probs = product("qhd,khd->hqk", grads, values)
        centre = jnp.sum(probs * grad_probs, axis=-1, keepdims=True)
        grad_scores = (probs * (grad_probs - centre)).astype(jnp.bfloat16)
        grad_query = product("hqk,khd->qhd", grad_scores, keys) * factor
        key_part = product("hqk,qhd->khd", grad_scores, queries) * factor
        return (
            attended.astype(jnp.bfloat16),
            grad_query.astype(jnp.bfloat16),
            key_part.astype(jnp.bfloat16),
            value_part.astype(jnp.bfloat16),
        )

    attended, grad_query, key_part, value_part = lax.map(
        attend,
        (
            split(query_rows[0], tokens),
            split(all_keys[0], length),
            split(all_values[0], length),
            split(grad_attn, tokens),
        ),
    )

    def scatter(part):
        part = join(part, length).reshape(1, length, width)
        return lax.psum_scatter(part, "rows", scatter_dimension=1, tiled=True)

    term = lax.dot_general(
        join(attended, tokens),
        grad_flat,
        (((0,), (0,)), ((), ())),
        preferred_element_type=jnp.float32,
    ).astype(jnp.bfloat16)
    share = lax.psum_scatter(term, "fsdp", scatter_dimension=0, tiled=True)
    grad_w_out = lax.psum(share, "rows").astype(jnp.float32)
    return (
        join(grad_query, tokens).reshape(1, tokens, width),
        scatter(key_part),
        scatter(value_part),
        grad_w_out,
    )


def solution(mesh):
    fsdp, rows = mesh.shape["fsdp"], mesh.shape["rows"]

    def local(query_rows, key_rows, value_rows, grad_out, w_out):
        heads = query_rows.shape[2] // HDIM
        if rows == 4 and fsdp == 2 * rows and heads % rows == 0:
            plan = functools.partial(by_heads, fsdp, rows)
        else:
            plan = by_tokens
        return plan(query_rows, key_rows, value_rows, grad_out, w_out)

    tokens = P("fsdp", "rows", None)
    return jax.shard_map(
        local,
        mesh=mesh,
        in_specs=(tokens, tokens, tokens, tokens, P("fsdp", None)),
        out_specs=(tokens, tokens, tokens, P("fsdp", None)),
        check_vma=False,
    )
```

```python
import functools
import math

import jax
import jax.numpy as jnp
from jax import lax
from jax.experimental import pallas as pl
from jax.experimental.pallas import tpu as pltpu
from jax.sharding import PartitionSpec as P


HDIM = 128


NT = (((1,), (1,)), ((), ()))
NN = (((1,), (0,)), ((), ()))


def dot(a, b, dims=NN):
    return lax.dot_general(a, b, dims, preferred_element_type=jnp.float32)


def whole(shape):
    return pl.BlockSpec(shape, lambda *_: (0,) * len(shape))


def cost(flops, moved, exps=0):
    return pl.CostEstimate(flops=flops, bytes_accessed=moved, transcendentals=exps)


def pack(place, query, key, value, rows):
    tokens, width = query.shape[1], query.shape[2] // rows

    def body(place_ref, *refs):
        ins, outs, (held, sems) = refs[:3], refs[3:-2], refs[-2:]
        moves = []
        for slot in (*range(1, rows), 0):
            start = pl.multiple_of((place_ref[0] ^ slot) * width, HDIM)
            for at in range(3):
                box = held.at[slot, at]
                moves.append(
                    (
                        pltpu.make_async_copy(
                            ins[at].at[0, :, pl.ds(start, width)], box, sems.at[0, slot, at]
                        ),
                        pltpu.make_async_copy(box, outs[slot].at[at], sems.at[1, slot, at]),
                    )
                )
        run(moves)

    shape = (3, tokens, width)
    return pl.pallas_call(
        body,
        grid_spec=pltpu.PrefetchScalarGridSpec(
            num_scalar_prefetch=1,
            grid=(1,),
            in_specs=[pl.BlockSpec(memory_space=pltpu.HBM)] * 3,
            out_specs=[pl.BlockSpec(memory_space=pltpu.HBM)] * rows,
            scratch_shapes=[
                pltpu.VMEM((rows, *shape), query.dtype),
                pltpu.SemaphoreType.DMA((2, rows, 3)),
            ],
        ),
        out_shape=[jax.ShapeDtypeStruct(shape, query.dtype)] * rows,
        cost_estimate=cost(0, 12 * query.size),
        name="pack",
    )(place, query, key, value)


def run(moves, rest=None):
    for fetch, _ in moves:
        fetch.start()
    for fetch, store in moves:
        fetch.wait()
        store.start()
    for store in rest() if rest else ():
        store.wait()
    for _, store in moves:
        store.wait()


def write_terms(place, pieces, total, low, high, sems, chunk):
    rows, piece, wide = low.shape
    steps = []
    for slot in range(rows):
        owner = place[0] ^ slot if chunk else (place[1] - slot) & (rows - 1)
        start = pl.multiple_of(owner * piece, 16)
        fetch = pltpu.make_async_copy(pieces[slot], low.at[slot], sems.at[0, slot])
        store = pltpu.make_async_copy(
            high.at[slot],
            total.at[pl.ds(start, piece), chunk * wide : (chunk + 1) * wide],
            sems.at[1, slot],
        )
        steps.append((fetch, store))
    for fetch, _ in steps:
        fetch.start()

    def rest():
        for slot, (fetch, store) in enumerate(steps):
            fetch.wait()
            high[slot] = low[slot].astype(jnp.float32)
            store.start()
        return [store for _, store in steps]

    return rest


def finish(place, parts, pieces, chunks):
    rows = len(parts)
    _, tokens, width = parts[0].shape
    piece, wide = pieces[0].shape

    def body(place_ref, *refs):
        ins, terms, outs, total = refs[:rows], refs[rows : 2 * rows], refs[2 * rows :][:3], refs[-6]
        held, low, high, sems, term_sems = refs[-5:]
        moves = []
        for slot in range(rows):
            start = pl.multiple_of((place_ref[0] ^ slot) * width, HDIM)
            for at in range(3):
                box = held.at[slot, at]
                moves.append(
                    (
                        pltpu.make_async_copy(ins[slot].at[at], box, sems.at[0, slot, at]),
                        pltpu.make_async_copy(
                            box, outs[at].at[0, :, pl.ds(start, width)], sems.at[1, slot, at]
                        ),
                    )
                )
        rest = write_terms(place_ref, terms, total, low, high, term_sems, 0)
        run(moves, rest)

    full = jax.ShapeDtypeStruct((1, tokens, width * rows), parts[0].dtype)
    return pl.pallas_call(
        body,
        grid_spec=pltpu.PrefetchScalarGridSpec(
            num_scalar_prefetch=1,
            grid=(1,),
            in_specs=[pl.BlockSpec(memory_space=pltpu.HBM)] * (2 * rows),
            out_specs=[pl.BlockSpec(memory_space=pltpu.HBM)] * 4,
            scratch_shapes=[
                pltpu.VMEM((rows, 3, tokens, width), parts[0].dtype),
                pltpu.VMEM((rows, piece, wide), pieces[0].dtype),
                pltpu.VMEM((rows, piece, wide), jnp.float32),
                pltpu.SemaphoreType.DMA((2, rows, 3)),
                pltpu.SemaphoreType.DMA((2, rows)),
            ],
        ),
        out_shape=[full] * 3 + [jax.ShapeDtypeStruct((rows * piece, chunks * wide), jnp.float32)],
        cost_estimate=cost(0, 12 * tokens * width * rows + 6 * rows * piece * wide),
        name="finish",
    )(place, *parts, *pieces)


def finish_terms(place, total, pieces, chunk):
    rows = len(pieces)
    piece, wide = pieces[0].shape

    def body(place_ref, _, *refs):
        terms, (out, low, high, sems) = refs[:rows], refs[rows:]
        for store in write_terms(place_ref, terms, out, low, high, sems, chunk)():
            store.wait()

    return pl.pallas_call(
        body,
        grid_spec=pltpu.PrefetchScalarGridSpec(
            num_scalar_prefetch=1,
            grid=(1,),
            in_specs=[pl.BlockSpec(memory_space=pltpu.HBM)] * (1 + rows),
            out_specs=pl.BlockSpec(memory_space=pltpu.HBM),
            scratch_shapes=[
                pltpu.VMEM((rows, piece, wide), pieces[0].dtype),
                pltpu.VMEM((rows, piece, wide), jnp.float32),
                pltpu.SemaphoreType.DMA((2, rows)),
            ],
        ),
        out_shape=jax.ShapeDtypeStruct(total.shape, total.dtype),
        input_output_aliases={1: 0},
        cost_estimate=cost(0, 6 * rows * piece * wide),
        name="finish_terms",
    )(place, total, *pieces)


def forward(parts):
    rows = len(parts)
    _, tokens, width = parts[0].shape
    length, heads = rows * tokens, width // HDIM
    scale = math.log2(math.e) / math.sqrt(HDIM)

    def body(*refs):
        ins, (probs_ref, attended_ref) = refs[:rows], refs[rows:]
        keys = jnp.concatenate([ref[1] for ref in ins], axis=0)
        values = jnp.concatenate([ref[2] for ref in ins], axis=0).T
        for slot in range(rows):
            across = slice(slot * tokens, (slot + 1) * tokens)
            scores = dot(keys, ins[slot][0], NT)
            top = jnp.max(scores, axis=0, keepdims=True)
            powers = jnp.exp2((scores - top) * scale)
            total = jnp.sum(powers, axis=0, keepdims=True)
            probs = (powers * (1.0 / total)).astype(jnp.bfloat16)
            probs_ref[0, :, across] = probs
            attended_ref[:, across] = dot(values, probs).astype(jnp.bfloat16)

    part = pl.BlockSpec((3, tokens, HDIM), lambda h: (0, 0, h))
    return pl.pallas_call(
        body,
        grid=(heads,),
        in_specs=[part] * rows,
        out_specs=[
            pl.BlockSpec((1, length, length), lambda h: (h, 0, 0)),
            pl.BlockSpec((HDIM, length), lambda h: (h, 0)),
        ],
        out_shape=[
            jax.ShapeDtypeStruct((heads, length, length), jnp.bfloat16),
            jax.ShapeDtypeStruct((width, length), jnp.bfloat16),
        ],
        cost_estimate=cost(
            8 * heads * length * length * HDIM, 2 * heads * length * length, heads * length * length
        ),
        name="forward",
    )(*parts)


def backward(parts, probs, grad_attn, first, count):
    rows = len(parts)
    tokens = parts[0].shape[1]
    length = rows * tokens
    factor = 1.0 / math.sqrt(HDIM)

    def body(*refs):
        ins, (probs_ref, grad_ref) = refs[:rows], refs[rows : rows + 2]
        outs, scores_ref = refs[rows + 2 : -1], refs[-1]
        queries = jnp.concatenate([ref[0] for ref in ins], axis=0)
        keys = jnp.concatenate([ref[1] for ref in ins], axis=0).T
        values = jnp.concatenate([ref[2] for ref in ins], axis=0)
        for slot in range(rows):
            across = slice(slot * tokens, (slot + 1) * tokens)
            probs = probs_ref[0, :, across].astype(jnp.float32)
            terms = probs * dot(values, grad_ref[:, across])
            centre = jnp.sum(terms, axis=0, keepdims=True)
            scores_ref[:, across] = (terms - probs * centre).astype(jnp.bfloat16)
        scores = scores_ref[...]
        grad_query = (dot(keys, scores) * factor).T
        grad_key = dot(scores, queries) * factor
        grad_value = dot(probs_ref[0], grad_ref[...], NT)
        for slot in range(rows):
            down = slice(slot * tokens, (slot + 1) * tokens)
            outs[slot][0] = grad_query[down].astype(jnp.bfloat16)
            outs[slot][1] = grad_key[down].astype(jnp.bfloat16)
            outs[slot][2] = grad_value[down].astype(jnp.bfloat16)

    part = pl.BlockSpec((3, tokens, HDIM), lambda i: (0, 0, first + i))
    shape = (3, tokens, count * HDIM)
    return pl.pallas_call(
        body,
        grid=(count,),
        in_specs=[part] * rows
        + [
            pl.BlockSpec((1, length, length), lambda i: (first + i, 0, 0)),
            pl.BlockSpec((HDIM, length), lambda i: (first + i, 0)),
        ],
        out_specs=[pl.BlockSpec((3, tokens, HDIM), lambda i: (0, 0, i))] * rows,
        out_shape=[jax.ShapeDtypeStruct(shape, jnp.bfloat16)] * rows,
        scratch_shapes=[pltpu.VMEM((length, length), jnp.bfloat16)],
        cost_estimate=cost(8 * count * length * length * HDIM, 2 * count * length * length),
        name="backward",
    )(*parts, probs, grad_attn)


def stacked(refs):
    return jnp.concatenate([ref[...] for ref in refs], axis=0)


def project(place, weights, grads):
    chunks = len(grads)
    ends = [sum(len(chunk) for chunk in grads[: at + 1]) for at in range(chunks)]
    half, depth = weights[0].shape
    half = half * len(weights) // 2
    step = grads[0][0].shape[1] // 2

    def body(place_ref, *refs):
        ins, out, total = refs[len(weights) : -2], refs[-2], refs[-1]
        at = pl.program_id(0)
        lines = stacked(refs[: len(weights)])
        for chunk in range(chunks):

            @pl.when(at // 2 == chunk)
            def _():
                term = dot(lines, stacked(ins[ends[chunk] - len(grads[chunk]) : ends[chunk]]), NT)
                if chunk:
                    total[...] += term
                else:
                    total[...] = jnp.where(at == 0, 0.0, total[...]) + term

        @pl.when(at == chunks * 2 - 1)
        def _():
            for core in range(2):

                @pl.when(place_ref[2] == core)
                def _():
                    out[core * half : (core + 1) * half] = total[:half].astype(out.dtype)
                    out[(1 - core) * half : (2 - core) * half] = total[half:].astype(out.dtype)

    def block_of(chunk, block):
        return pl.BlockSpec(
            (block.shape[0], step), lambda i, place_ref: (0, jnp.clip(i - chunk * 2, 0, 1))
        )

    shape = (2 * half, sum(block.shape[0] for block in grads[0]))
    return pl.pallas_call(
        body,
        grid_spec=pltpu.PrefetchScalarGridSpec(
            num_scalar_prefetch=1,
            grid=(chunks * 2,),
            in_specs=[
                pl.BlockSpec((part.shape[0], step), lambda i, place_ref: (0, i)) for part in weights
            ]
            + [block_of(chunk, block) for chunk in range(chunks) for block in grads[chunk]],
            out_specs=whole(shape),
            scratch_shapes=[pltpu.VMEM(shape, jnp.float32)],
        ),
        out_shape=jax.ShapeDtypeStruct(shape, jnp.bfloat16),
        cost_estimate=cost(2 * shape[0] * shape[1] * depth, 2 * depth * (shape[0] + shape[1])),
        name="project",
    )(place, *weights, *(block for chunk in grads for block in chunk))


def weight_terms(place, attended, grads, parts, by_plane):
    width, length = attended.shape
    step = grads[0].shape[1] // 2
    piece = width // 2 // parts

    def body(place_ref, attended_ref, *refs):
        ins, (keep, give) = refs[:-2], refs[-2:]
        term = dot(attended_ref[...], stacked(ins)).astype(jnp.bfloat16)
        row, plane, core = place_ref[0], place_ref[1], place_ref[2]
        for side in range(2):
            for out, mine in ((keep, core == side), (give, core != side)):

                @pl.when(mine)
                def _():
                    for at in range(parts):
                        start = (side * parts + at) * piece
                        slot = (at - plane) & (parts - 1) if by_plane else at ^ row
                        out[slot] = term[start : start + piece]

    shape = jax.ShapeDtypeStruct((parts, piece, 2 * step), jnp.bfloat16)
    spec = pl.BlockSpec((parts, piece, step), lambda i, place_ref: (0, 0, i))
    return pl.pallas_call(
        body,
        grid_spec=pltpu.PrefetchScalarGridSpec(
            num_scalar_prefetch=1,
            grid=(2,),
            in_specs=[whole((width, length))]
            + [pl.BlockSpec((block.shape[0], step), lambda i, place_ref: (0, i)) for block in grads],
            out_specs=[spec] * 2,
        ),
        out_shape=[shape] * 2,
        cost_estimate=cost(4 * width * length * step, 2 * (width * length + 2 * length * step)),
        name="weight_terms",
    )(place, attended, *grads)


def after(value, *done):
    return lax.optimization_barrier((value, done))[0]


def onward(planes, hop, z, c, r):
    to = z + 1 if z > r else z - 1
    return (to, c, r) if abs(z - r) == hop and 0 <= to < planes else None


def by_heads(fsdp, rows, query_rows, key_rows, value_rows, grad_out, w_out):
    planes = fsdp // 2
    row = lax.axis_index("rows")
    member = lax.axis_index("fsdp")
    plane, core = member // 2, member % 2
    place = jnp.stack([row, plane, core]).astype(jnp.int32)

    def send(array, target):
        pairs = []
        for z in range(planes):
            for c in range(2):
                for r in range(rows):
                    to = target(z, c, r)
                    if to is not None:
                        pairs.append(((z * 2 + c) * rows + r, (to[0] * 2 + to[1]) * rows + to[2]))
        return lax.ppermute(array, ("fsdp", "rows"), pairs)

    def to_row(array, slot):
        return send(array, lambda z, c, r: (z, c, r ^ slot))

    def to_core(array):
        return send(array, lambda z, c, r: (z, 1 - c, r))

    def to_plane(array, ahead):
        return send(array, lambda z, c, r: ((z + ahead) % planes, c, r))

    grad_flat = grad_out[0]
    wide = grad_flat.shape[1] // 2

    half_way = grad_flat.shape[0] // 2
    left, upper, lower = (
        grad_flat[:, :wide],
        grad_flat[:half_way, wide:],
        grad_flat[half_way:, wide:],
    )

    def hand_on(by_x, by_y):
        return [to_row(by_x, 2), to_row(by_y, 1)]

    by_x, by_y = to_row(left, 1), to_row(left, 2)
    handed = by_x[:half_way], by_y[half_way:]
    grads = [[left, by_x, by_y, *hand_on(*handed)]]

    away = jnp.abs(plane - row)
    cut = w_out.shape[0] // 2

    def leave(lines):
        above = send(lines, lambda z, c, r: (z + 1, c, r) if z == r and z + 1 < planes else None)
        below = send(lines, lambda z, c, r: (z - 1, c, r) if z == r and z > 0 else None)
        return jnp.where(plane > row, above, below)

    def go_on(hop, lines):
        return send(lines, functools.partial(onward, planes, hop))

    first = [w_out[:cut]]
    first.append(leave(first[0]))
    first.append(go_on(1, first[1]))
    second = [w_out[cut:]]
    second.append(leave(after(second[0], first[1])))
    first.append(go_on(2, first[2]))
    second.append(go_on(1, second[1]))

    packed = pack(place, query_rows, key_rows, value_rows, rows)
    parts = [packed[0]] + [to_row(packed[slot], slot) for slot in range(1, rows)]
    probs, attended = forward(parts)
    second.append(go_on(2, after(second[2], attended)))

    def mine(stages):
        here = stages[0]
        for hop in range(1, planes):
            here = jnp.where(away == hop, stages[hop], here)
        return here

    own = after((upper, lower), parts)
    by_x = [to_row(part, 1) for part in own]
    by_y = [to_row(part, 2) for part in own]
    by_x, by_y = after((by_x, by_y), attended)
    grads.append([*own, *by_x, *by_y, *hand_on(by_x[0], by_y[1])])


    def reduce_cores(at, attended, chunk):
        keep, give = weight_terms(place, attended, chunk, rows, not at)
        return keep, to_core(give)

    def add_cores(keep, got):
        return [
            (keep[slot].astype(jnp.float32) + got[slot].astype(jnp.float32)).astype(jnp.bfloat16)
            for slot in range(rows)
        ]

    def to_rows(blocks):
        return [blocks[0]] + [to_row(blocks[slot], slot) for slot in range(1, rows)]

    def to_planes(blocks):
        return [blocks[0]] + [to_plane(blocks[ahead], ahead) for ahead in range(1, planes)]

    def by_plane(blocks):
        return [
            lax.select_n(((plane + ahead) % planes) ^ row, *blocks) for ahead in range(planes)
        ]

    def added(blocks):
        total = blocks[0].astype(jnp.float32)
        for block in blocks[1:]:
            total = total + block.astype(jnp.float32)
        return total.astype(jnp.bfloat16)

    early = to_planes(add_cores(*reduce_cores(0, attended, grads[0])))
    first[-1], second[-1] = after((first[-1], second[-1]), early[0])
    weights = [mine(first), mine(second)]
    weights += [to_core(part) for part in weights]
    late = reduce_cores(1, attended, grads[1])
    grad_attn = project(place, weights, grads)
    late = to_rows(add_cores(*after(late, grad_attn)))
    early = to_rows([added(after(early, grad_attn))] * rows)
    sent = backward(parts, probs, grad_attn, 0, probs.shape[0])
    back = to_rows(sent)
    late = to_planes(by_plane(after(late, sent[0])))
    early = to_planes(by_plane(after(early, sent[0])))
    late = to_rows([added(late)] * rows)
    *outs, total = finish(place, back, early, len(grads))
    return (*outs, finish_terms(place, total, after(late, outs[0]), 1))


def by_tokens(query_rows, key_rows, value_rows, grad_out, w_out):
    tokens, width = query_rows.shape[1:]
    heads = width // HDIM
    factor = 1.0 / math.sqrt(HDIM)
    grad_flat = grad_out[0]
    groups = math.gcd(heads, 3)

    def split(array, count):
        return jnp.moveaxis(array.reshape(count, groups, heads // groups, HDIM), 1, 0)

    def join(array, count):
        return jnp.moveaxis(array, 0, 1).reshape(count, width)

    grad_attn = lax.dot_general(
        grad_flat,
        lax.all_gather(w_out, "fsdp", axis=0, tiled=True),
        NT,
        preferred_element_type=jnp.float32,
    ).astype(jnp.bfloat16)
    all_keys = lax.all_gather(key_rows, "rows", axis=1, tiled=True)
    all_values = lax.all_gather(value_rows, "rows", axis=1, tiled=True)
    length = all_keys.shape[1]

    def product(spec, a, b):
        return jnp.einsum(spec, a, b, preferred_element_type=jnp.float32)

    def attend(inputs):
        queries, keys, values, grads = inputs
        probs = jax.nn.softmax(product("qhd,khd->hqk", queries, keys) * factor, axis=-1)
        low = probs.astype(jnp.bfloat16)
        attended = product("hqk,khd->qhd", low, values)
        value_part = product("hqk,qhd->khd", low, grads)
        grad_probs = product("qhd,khd->hqk", grads, values)
        centre = jnp.sum(probs * grad_probs, axis=-1, keepdims=True)
        grad_scores = (probs * (grad_probs - centre)).astype(jnp.bfloat16)
        grad_query = product("hqk,khd->qhd", grad_scores, keys) * factor
        key_part = product("hqk,qhd->khd", grad_scores, queries) * factor
        return (
            attended.astype(jnp.bfloat16),
            grad_query.astype(jnp.bfloat16),
            key_part.astype(jnp.bfloat16),
            value_part.astype(jnp.bfloat16),
        )

    attended, grad_query, key_part, value_part = lax.map(
        attend,
        (
            split(query_rows[0], tokens),
            split(all_keys[0], length),
            split(all_values[0], length),
            split(grad_attn, tokens),
        ),
    )

    def scatter(part):
        part = join(part, length).reshape(1, length, width)
        return lax.psum_scatter(part, "rows", scatter_dimension=1, tiled=True)

    term = lax.dot_general(
        join(attended, tokens),
        grad_flat,
        (((0,), (0,)), ((), ())),
        preferred_element_type=jnp.float32,
    ).astype(jnp.bfloat16)
    share = lax.psum_scatter(term, "fsdp", scatter_dimension=0, tiled=True)
    grad_w_out = lax.psum(share, "rows").astype(jnp.float32)
    return (
        join(grad_query, tokens).reshape(1, tokens, width),
        scatter(key_part),
        scatter(value_part),
        grad_w_out,
    )


def solution(mesh):
    fsdp, rows = mesh.shape["fsdp"], mesh.shape["rows"]

    def local(query_rows, key_rows, value_rows, grad_out, w_out):
        heads = query_rows.shape[2] // HDIM
        if rows == 4 and fsdp == 2 * rows and heads % rows == 0:
            plan = functools.partial(by_heads, fsdp, rows)
        else:
            plan = by_tokens
        return plan(query_rows, key_rows, value_rows, grad_out, w_out)

    tokens = P("fsdp", "rows", None)
    return jax.shard_map(
        local,
        mesh=mesh,
        in_specs=(tokens, tokens, tokens, tokens, P("fsdp", None)),
        out_specs=(tokens, tokens, tokens, P("fsdp", None)),
        check_vma=False,
    )
```
